32 devices in a mesh: row: 4 (over y, core), col: 2 (over x), depth: 4 (over z).
Axes of the slice: x: 2, y: 2, z: 4, core: 2. Of those that a mesh axis runs over, the one named last changes fastest.
Arguments:
- density: float32 [512, 5, 128, 128], P(('row', 'depth'), None, 'col'), may hold values from -0.6 to 0.6
- pattern: int32 [512, 5], P(('row', 'depth')), may hold values 0 or 1
Outputs:
- purified: float32 [512, 5, 128, 128], P(('row', 'depth'), None, 'col')
The draws below stay inside these ranges and needn't reach their ends.
All inputs are finite; a program needn't handle non-finite values. No bound on the sum of `pattern` on one device may be relied on, other than what follows from the above.
Results may differ from the reference program's by a relative error of at most 0.0001.
Values sent between devices are 32-bit elements; how exact they have to be, the bound alone decides.
A program may use at most 64 MiB of HBM per device.

```python
import jax
import jax.numpy as jnp
from jax import lax

BLOCK = 128
HALF = 2
BLOCKS = 512
WIDE = 5


def with_ends(drawn, key, low, high):
    place = [jax.random.randint(jax.random.fold_in(key, axis), (), 0, length) for axis, length in enumerate(drawn.shape)]
    main_axis = drawn.shape.index(max(drawn.shape))
    neighbour = place[:main_axis] + [(place[main_axis] + 1) % drawn.shape[main_axis]] + place[main_axis + 1:]
    return drawn.at[tuple(place)].set(low).at[tuple(neighbour)].set(high)


def shard_levels(own_key, extent, pieces, smallest, top_value):
    def one(dim, shards_of):
        heights = jax.random.uniform(jax.random.fold_in(jax.random.fold_in(own_key, 6), dim), (shards_of,), jnp.float32, smallest / len(pieces), top_value / len(pieces))
        return jnp.repeat(jnp.exp(heights), extent[dim] // shards_of).reshape((-1,) + (1,) * (len(extent) - dim - 1))

    gain = one(*pieces[0])
    for cut in pieces[1:]:
        gain = gain * one(*cut)
    return gain


def bell_draw(key, dims, deviation, reach, shards=(), dtype=jnp.bfloat16):
    entries = jax.random.normal(key, dims, jnp.float32) * deviation
    if len(shards) > 0:
        entries = shard_levels(key, dims, shards, -0.22, 0.18) * entries
    return jnp.clip(entries, min=-reach, max=reach).astype(dtype)


def setup_inputs(seed: int = 0) -> dict:
    key_list = jax.random.split(jax.random.key(seed), 3)
    density = bell_draw(key_list[0], (BLOCKS, WIDE, BLOCK, BLOCK), 0.1, 0.6, ((0, 16), (2, 2)), jnp.float32)
    pattern = with_ends((jax.random.randint(key_list[1], (BLOCKS, WIDE), 0, 4) < 3).astype(jnp.int32), jax.random.fold_in(key_list[1], 1), 0, 1)
    return dict(density=density, pattern=pattern)


def banded_product(left_tiles, other_tiles, pattern):
    summed = jnp.zeros(left_tiles.shape, jnp.float32)
    for source in range(WIDE):
        first_slot = max(0, source - HALF)
        last_slot = min(WIDE, source + HALF + 1)
        shifted = jnp.roll(other_tiles, -(source - HALF), axis=0)
        partner = shifted[:, first_slot - source + HALF:last_slot - source + HALF]
        contrib = jnp.einsum("iab,itbc->itac", left_tiles[:, source], partner, precision=lax.Precision.HIGHEST)
        summed = summed.at[:, first_slot:last_slot].add(contrib)
    return summed * pattern[:, :, None, None].astype(jnp.float32)


def reference(density, pattern):
    masked = density * pattern[:, :, None, None].astype(jnp.float32)
    square = banded_product(masked, masked, pattern)
    cube = banded_product(square, masked, pattern)
    return 3.0 * square - 2.0 * cube
```

```python
import functools

import jax
import jax.numpy as jnp
from jax import lax
from jax.experimental import pallas as pl
from jax.experimental.pallas import tpu as pltpu
from jax.sharding import PartitionSpec as P

MESH = pl.DeviceIdType.MESH
WIDE = 5
SLOTS = 6
RING = ("row", "depth")


def split(value):
    high = value.astype(jnp.bfloat16)
    low = (value - high.astype(jnp.float32)).astype(jnp.bfloat16)
    return high, low


def dot(a, b):
    return jnp.dot(a, b, preferred_element_type=jnp.float32)


def products(block, h, me, masks, high, low, out):
    two = 2 * block

    def product(j, a, b, sources=(0, 1, 2), start=None):
        both = jnp.concatenate([a, b], axis=0)
        m = a.shape[0]
        parts = []
        for n in range(3):
            total = None if start is None else start[:, n * two:(n + 1) * two]
            for k in sources:
                at = n - k + 1
                if at < 0 or at > 2:
                    continue
                lanes = slice(at * two, (at + 1) * two)
                ks = slice(k * two, (k + 1) * two)
                stacked = dot(both[:, ks], high[j + k - 1, :, lanes])
                term = stacked[:m] + stacked[m:] + dot(a[:, ks], low[j + k - 1, :, lanes])
                total = term if total is None else total + term
            parts.append(total)
        return jnp.concatenate(parts, axis=1)

    def own_rows(ref, j):
        return jnp.concatenate(
            [ref[j, pl.ds(pl.multiple_of(p * block + me * h, h), h), :] for p in range(2)], axis=0)

    def compute(j, to, sources=(0, 1, 2), start=None):
        factor = jnp.concatenate(
            [jnp.broadcast_to(masks[j, p:p + 1, :], (h, SLOTS * block)) for p in range(2)], axis=0)
        square = product(j, own_rows(high, j), own_rows(low, j), sources, start) * factor
        cube = product(j, *split(square)) * factor
        value = 3.0 * square - 2.0 * cube
        for p in range(2):
            for s in range(WIDE):
                out[to, p, s] = value[p * h:(p + 1) * h, (p + s) * block:(p + s + 1) * block]

    return product, own_rows, compute


BEFORE = ((0, 1), (0, 2), (1, 2))
AFTER = ((2,), (1,), (0,))
LATE = 3


def finish(first_late, masks, high, low, early, begun, out, late, early_sem, late_sem):
    h, block = early.shape[3], early.shape[4]
    me = lax.axis_index("col")
    before = first_late - 1
    after = early.shape[0] - before
    firsts = [pltpu.make_async_copy(early.at[pl.ds(0, before)], out.at[pl.ds(0, before)], early_sem.at[0])]
    if after:
        firsts.append(pltpu.make_async_copy(
            early.at[pl.ds(before, after)], out.at[pl.ds(before + LATE, after)], early_sem.at[1]))
    for first in firsts:
        first.start()
    _, _, compute = products(block, h, me, masks, high, low, late)

    def result(i):
        return pltpu.make_async_copy(late.at[i], out.at[before + i], late_sem.at[i])

    for i in range(LATE):
        compute(first_late + i, i, AFTER[i], begun[i])
        result(i).start()

    for first in firsts:
        first.wait()

    @pl.loop(0, LATE)
    def _(i):
        result(i).wait()


def dense_kernel(cols, ring, dens, pattern, masks, high, low, early, begun, raw, flags,
           local_sem, flag_sem, send_sem, recv_sem, edge_send, edge_recv,
           relay_send, relay_recv, flag_send, flag_recv, up, down, corner):
    pairs = dens.shape[0]
    h = dens.shape[3]
    block = dens.shape[4]
    last = pairs + 1
    me = lax.axis_index("col")
    depth = lax.axis_size("depth")
    place = lax.axis_index("row") * depth + lax.axis_index("depth")

    def on_ring(shift):
        at = lax.rem(place + shift + ring, ring)
        return {"row": at // depth, "depth": lax.rem(at, depth)}

    prev, following = on_ring(-1), on_ring(1)

    def peer(step):
        return {"col": lax.rem(me + step, cols)}

    def source(step):
        return lax.rem(me + cols - step, cols)

    def own(j):
        return pltpu.make_async_copy(dens.at[j - 1], raw.at[me, j], local_sem.at[j - 1])

    def across(step, j):
        return pltpu.make_async_remote_copy(
            dens.at[j - 1], raw.at[me, j], send_sem.at[step - 1, j - 1],
            recv_sem.at[step - 1, j - 1], device_id=peer(step), device_id_type=MESH)

    ends = ((pairs, 0, following), (1, last, prev))

    def edge(side):
        j, slot, device = ends[side]
        return pltpu.make_async_remote_copy(
            dens.at[j - 1], raw.at[me, slot], edge_send.at[side], edge_recv.at[side],
            device_id=device, device_id_type=MESH)

    def relay(side, step):
        j, slot, device = ends[side]
        return pltpu.make_async_remote_copy(
            raw.at[source(step), j], raw.at[source(step), slot], relay_send.at[side, step - 1],
            relay_recv.at[side, step - 1], device_id=device, device_id_type=MESH)

    def flag_edge(side):
        return pltpu.make_async_remote_copy(
            pattern, flags.at[2 * side], flag_send.at[side], flag_recv.at[side],
            device_id=ends[side][2], device_id_type=MESH)

    steps = range(1, cols)

    z, r = lax.axis_index("depth"), lax.axis_index("row")
    row_count = lax.axis_size("row")

    def greet(semaphore, device):
        pl.semaphore_signal(semaphore, inc=1, device_id=device, device_id_type=MESH)

    def along(step):
        return {"depth": z + step}

    def beside(step):
        return {"row": lax.rem(r + step + row_count, row_count)}

    barrier = pltpu.get_barrier_semaphore()
    for s in steps:
        greet(barrier, peer(s))

    @pl.when(z > 0)
    def _():
        greet(barrier, along(-1))

    @pl.when(z < depth - 1)
    def _():
        greet(barrier, along(1))

    @pl.when(z == 0)
    def _():
        greet(barrier, beside(-1))
        greet(barrier, beside(1))

    own_flags = pltpu.make_async_copy(pattern, flags.at[1], flag_sem)
    own_flags.start()
    near = jnp.where(z == 0, 2, 1) + jnp.where(z < depth - 1, 1, 0)
    pl.semaphore_wait(barrier, cols - 1 + near)

    for j in (1, pairs):
        for s in steps:
            across(s, j).start()

    @pl.loop(2, pairs)
    def _(j):
        for s in steps:
            across(s, j).start()

    @pl.when(z > 0)
    def _():
        pl.semaphore_wait(up, 1)

    @pl.when(z < depth - 1)
    def _():
        greet(up, along(1))

    @pl.when(z < depth - 2)
    def _():
        pl.semaphore_wait(down, 1)

    @pl.when((z > 0) & (z <= depth - 2))
    def _():
        greet(down, along(-1))

    @pl.when(z == 0)
    def _():
        greet(corner, beside(1))
        pl.semaphore_wait(corner, 1)

    for side in (0, 1):
        flag_edge(side).start()
        edge(side).start()

    @pl.loop(1, pairs + 1)
    def _(j):
        own(j).start()

    def expand(which, i, j):
        lane = lax.broadcasted_iota(jnp.int32, flags.shape[1:], 1)
        for p in range(2):
            picked = jnp.where(lane == i + p, flags[which], 0).astype(jnp.float32)
            spread = jnp.broadcast_to(jnp.sum(picked, axis=1, keepdims=True), (WIDE, block))
            for s in range(WIDE):
                masks[j, p:p + 1, (p + s) * block:(p + s + 1) * block] = spread[s:s + 1]
            empty = slice(0, block) if p else slice(WIDE * block, SLOTS * block)
            masks[j, p:p + 1, empty] = jnp.zeros((1, block), jnp.float32)

    def convert(j):
        for p in range(2):
            for s in range(WIDE):
                slot = p + s
                factor = masks[j, p:p + 1, slot * block:(slot + 1) * block]
                for c in range(cols):
                    a, b = split(raw[c, j, p, s] * factor)
                    rows = slice(p * block + c * h, p * block + (c + 1) * h)
                    lanes = slice(slot * block, (slot + 1) * block)
                    high[j, rows, lanes] = a
                    low[j, rows, lanes] = b
            empty = slice(0, block) if p else slice(WIDE * block, SLOTS * block)
            nothing = jnp.zeros((block, block), jnp.bfloat16)
            high[j, p * block:(p + 1) * block, empty] = nothing
            low[j, p * block:(p + 1) * block, empty] = nothing

    product, own_rows, compute = products(block, h, me, masks, high, low, early)

    own_flags.wait()

    @pl.loop(1, pairs + 1)
    def _(j):
        expand(1, 2 * (j - 1), j)

    for side in (0, 1):
        flag_edge(side).wait_recv()
    expand(0, 2 * (pairs - 1), 0)
    expand(2, 0, last)

    @pl.loop(1, pairs + 1)
    def _(j):
        own(j).wait()

    for j, side in ((1, 1), (pairs, 0)):
        for s in steps:
            across(s, j).wait_recv()
            relay(side, s).start()
        convert(j)
    for side in (0, 1):
        edge(side).wait_recv()
        for s in steps:
            relay(side, s).wait_recv()
        convert(ends[side][1])

    @pl.loop(2, pairs - 1)
    def _(j):
        for s in steps:
            across(s, j).wait_recv()
        convert(j)
        compute(j - 1, j - 2)

    def local_rows(j):
        rows = []
        for p in range(2):
            blocks = [raw[me, j, p, s] for s in range(WIDE)]
            empty = [jnp.zeros((h, block), jnp.float32)]
            row = jnp.concatenate(empty + blocks if p else blocks + empty, axis=1)
            rows.append(row * masks[j, p:p + 1, :])
        return split(jnp.concatenate(rows, axis=0))

    for i in range(LATE):
        j = pairs - LATE + 1 + i
        a, b = local_rows(j) if i == 1 else (own_rows(high, j), own_rows(low, j))
        begun[i] = product(j, a, b, BEFORE[i])

    for side in (0, 1):
        flag_edge(side).wait_send()
        edge(side).wait_send()
        for s in steps:
            relay(side, s).wait_send()
    for s in steps:
        across(s, pairs - 1).wait_recv()
    convert(pairs - 1)

    @pl.loop(1, pairs + 1)
    def _(j):
        for s in steps:
            across(s, j).wait_send()


GUEST = 2


def sparse_kernel(ring, dens, pattern, masks, high, low, early, begun, over,
                  mine, theirs, hosted, guests, flags, bits, queue, hole, place_of,
                  local_sem, guest_sem, flag_sem, bits_sem, send_sem, recv_sem, edge_send, edge_recv,
                  relay_send, relay_recv, flag_send, flag_recv, up, down, corner):
    pairs, pair_slots, h, block = dens.shape
    last = pairs + 1
    first_guest = pairs - GUEST
    tail = first_guest - 1
    room = guests.shape[0]
    hosts = hosted.shape[0]
    me = lax.axis_index("col")
    depth = lax.axis_size("depth")
    place = lax.axis_index("row") * depth + lax.axis_index("depth")

    def on_ring(shift):
        at = lax.rem(place + shift + ring, ring)
        return {"row": at // depth, "depth": lax.rem(at, depth)}

    prev, following = on_ring(-1), on_ring(1)
    peer = {"col": 1 - me}

    def own(j):
        return pltpu.make_async_copy(dens.at[j - 1], mine.at[j], local_sem.at[j - 1])

    def own_guest(i):
        return pltpu.make_async_copy(
            dens.at[first_guest - 1 + i], guests.at[pl.ds(i * pair_slots, pair_slots)], guest_sem.at[i])

    def crossing(source, target, n):
        return pltpu.make_async_remote_copy(
            source, target, send_sem.at[n], recv_sem.at[n], device_id=peer, device_id_type=MESH)

    def at_host(j):
        return pl.ds((j - 1) * pair_slots, pair_slots)

    def across(j):
        return crossing(mine.at[j], hosted.at[at_host(j)], j)

    across_first = crossing(dens.at[0], theirs.at[1], 1)
    across_last = crossing(mine.at[pairs], hosted.at[pl.ds(0, pair_slots)], 0)
    half_host = pl.ds((tail - 1) * pair_slots, WIDE)
    across_half = crossing(mine.at[tail, pl.ds(0, WIDE)], hosted.at[half_host], tail)
    across_end = crossing(
        dens.at[tail - 1, pl.ds(WIDE, WIDE)], theirs.at[3, pl.ds(WIDE, WIDE)], tail + 1)

    ends = ((pairs, 0, following), (1, last, prev))
    halo = (0, 2)

    def edge(side):
        j, slot, device = ends[side]
        return pltpu.make_async_remote_copy(
            dens.at[j - 1], mine.at[slot], edge_send.at[side], edge_recv.at[side],
            device_id=device, device_id_type=MESH)

    def relay(side):
        source = hosted.at[pl.ds(0, pair_slots)] if side == 0 else theirs.at[1]
        return pltpu.make_async_remote_copy(
            source, theirs.at[halo[side]], relay_send.at[side], relay_recv.at[side],
            device_id=ends[side][2], device_id_type=MESH)

    reach = (ring // 2, ring - 1 - ring // 2)

    def flag_hop(side, k):
        source = k - 1 if side == 0 else lax.rem(ring - k + 1, ring)
        target = k if side == 0 else ring - k
        return pltpu.make_async_remote_copy(
            flags.at[source], flags.at[target], flag_send.at[side, k - 1], flag_recv.at[side, k - 1],
            device_id=ends[side][2], device_id_type=MESH)

    z, r = lax.axis_index("depth"), lax.axis_index("row")
    row_count = lax.axis_size("row")

    def greet(semaphore, device):
        pl.semaphore_signal(semaphore, inc=1, device_id=device, device_id_type=MESH)

    def along(step):
        return {"depth": z + step}

    def beside(step):
        return {"row": lax.rem(r + step + row_count, row_count)}

    barrier = pltpu.get_barrier_semaphore()
    greet(barrier, peer)

    @pl.when(z > 0)
    def _():
        greet(barrier, along(-1))

    @pl.when(z < depth - 1)
    def _():
        greet(barrier, along(1))

    @pl.when(z == 0)
    def _():
        greet(barrier, beside(-1))
        greet(barrier, beside(1))

    own_bits = pltpu.make_async_copy(pattern, bits, bits_sem)
    own_bits.start()
    own_flags = pltpu.make_async_copy(pattern, flags.at[0], flag_sem)
    own_flags.start()
    for i in range(GUEST):
        own_guest(i).start()
    own(pairs).start()

    @pl.loop(1, pairs)
    def _(j):
        own(j).start()

    near = jnp.where(z == 0, 2, 1) + jnp.where(z < depth - 1, 1, 0)
    pl.semaphore_wait(barrier, 1 + near)

    across_first.start()

    @pl.when(z > 0)
    def _():
        pl.semaphore_wait(up, 1)

    @pl.when(z < depth - 1)
    def _():
        greet(up, along(1))

    @pl.when(z < depth - 2)
    def _():
        pl.semaphore_wait(down, 1)

    @pl.when((z > 0) & (z <= depth - 2))
    def _():
        greet(down, along(-1))

    @pl.when(z == 0)
    def _():
        greet(corner, beside(1))
        pl.semaphore_wait(corner, 1)

    own_flags.wait()
    for side in (0, 1):
        flag_hop(side, 1).start()
        edge(side).start()

    own_bits.wait()

    def active(j, q):
        return bits[q % WIDE, 2 * (j - 1) + q // WIDE]

    following_guest = room
    hole[room] = room
    hole[room + 1] = room
    for n in reversed(range(room)):
        used = active(first_guest + n // pair_slots, n % pair_slots)
        following_guest = jnp.where(used > 0, n, following_guest)
        hole[n] = following_guest
    guest = hole[0]
    for k in range(room):
        queue[k] = jnp.minimum(guest, room - 1)
        guest = hole[guest + 1]
    queue[room] = room - 1

    def fill(j, count, taken):
        for q in range(count):
            used = active(j, q)
            block_in = guests[queue[taken]]
            mine[j, q] = jnp.where(used > 0, mine[j, q], block_in)
            taken = jnp.minimum(taken + 1 - used, room)
        return taken

    for i in range(GUEST):
        own_guest(i).wait()
    own(pairs).wait()
    taken = fill(pairs, pair_slots, jnp.int32(0))
    own(1).wait()
    own(2).wait()
    taken = fill(2, pair_slots, taken)
    across_last.start()

    def prepare(j, taken):
        own(j).wait()
        taken = fill(j, pair_slots, taken)
        across(j - 1).start()
        return taken

    taken = lax.fori_loop(3, tail, prepare, taken)
    own(tail).wait()
    fill(tail, WIDE, taken)
    across(tail - 1).start()

    @pl.loop(tail + 1, pairs)
    def _(j):
        own(j).wait()

    hole[hosts] = hosts
    hole[hosts + 1] = hosts

    def scan(j, base, count, free):
        for q in reversed(range(count)):
            free = jnp.where(active(j, q) > 0, free, base + q)
            hole[base + q] = free
        return free

    free = scan(tail, (tail - 1) * pair_slots, WIDE, jnp.int32(hosts))

    def scan_pair(i, free):
        j = tail - 1 - i
        return scan(j, (j - 1) * pair_slots, pair_slots, free)

    free = lax.fori_loop(0, tail - 2, scan_pair, free)
    spot = scan(pairs, 0, pair_slots, free)
    across_half.start()
    across_end.start()
    for k in range(room):
        queue[k] = jnp.minimum(spot, hosts - 1)
        spot = hole[spot + 1]
    queue[room] = hosts - 1
    rank = jnp.int32(0)
    for n in range(room):
        place_of[n] = queue[rank]
        rank = rank + active(first_guest + n // pair_slots, n % pair_slots)

    def expand(which, i, j):
        lane = lax.broadcasted_iota(jnp.int32, flags.shape[1:], 1)
        for p in range(2):
            picked = jnp.where(lane == i + p, flags[which], 0).astype(jnp.float32)
            spread = jnp.broadcast_to(jnp.sum(picked, axis=1, keepdims=True), (WIDE, block))
            for s in range(WIDE):
                masks[j, p:p + 1, (p + s) * block:(p + s + 1) * block] = spread[s:s + 1]
            empty = slice(0, block) if p else slice(WIDE * block, SLOTS * block)
            masks[j, p:p + 1, empty] = jnp.zeros((1, block), jnp.float32)

    def convert(j, other, rows=(0, 1)):
        for p in rows:
            for s in range(WIDE):
                slot = p + s
                lanes = slice(slot * block, (slot + 1) * block)
                factor = masks[j, p:p + 1, lanes]
                for c, value in ((me, mine[j, p * WIDE + s]), (1 - me, other(p * WIDE + s))):
                    a, b = split(value * factor)
                    at = pl.ds(pl.multiple_of(p * block + c * h, h), h)
                    high[j, at, lanes] = a
                    low[j, at, lanes] = b
            empty = slice(0, block) if p else slice(WIDE * block, SLOTS * block)
            nothing = jnp.zeros((block, block), jnp.bfloat16)
            high[j, p * block:(p + 1) * block, empty] = nothing
            low[j, p * block:(p + 1) * block, empty] = nothing

    def arrived(j):
        return lambda q: hosted[(j - 1) * pair_slots + q]

    def direct(i):
        return lambda q: theirs[i, q]

    def visiting(j):
        return lambda q: hosted[place_of[(j - first_guest) * pair_slots + q]]

    product, own_rows, compute = products(block, h, me, masks, high, low, early)

    @pl.loop(1, pairs + 1)
    def _(j):
        expand(0, 2 * (j - 1), j)

    for side in (0, 1):
        flag_hop(side, 1).wait_recv()
    for side in (0, 1):
        if reach[side] > 1:
            flag_hop(side, 2).start()
    expand(1, 2 * (pairs - 1), 0)
    expand(ring - 1, 0, last)

    across_first.wait_recv()
    relay(1).start()
    convert(1, direct(1))
    across_last.wait_recv()
    relay(0).start()
    convert(pairs, lambda q: hosted[q])
    for side in (0, 1):
        edge(side).wait_recv()
        relay(side).wait_recv()
        convert(ends[side][1], direct(halo[side]))

    turns = tail - 2
    each = -(-(reach[0] - 1) // turns)

    def pass_on(side, k):
        @pl.when(k <= reach[side])
        def _():
            flag_hop(side, k).wait_recv()

        @pl.when(k + 1 <= reach[side])
        def _():
            flag_hop(side, k + 1).start()

    @pl.loop(2, tail)
    def _(j):
        for u in range(each):
            for side in (0, 1):
                pass_on(side, (j - 2) * each + u + 2)
        across(j).wait_recv()
        convert(j, arrived(j))
        compute(j - 1, j - 2)

    across_half.wait_recv()
    for j in range(first_guest, pairs):
        convert(j, visiting(j))
    for i, j in enumerate(range(first_guest + 1, pairs + 1)):
        compute(j, tail - 2 + i)
    convert(tail, arrived(tail), (0,))

    def local_rows(j):
        rows = []
        for p in range(2):
            blocks = [mine[j, p * WIDE + s] for s in range(WIDE)]
            empty = [jnp.zeros((h, block), jnp.float32)]
            row = jnp.concatenate(empty + blocks if p else blocks + empty, axis=1)
            rows.append(row * masks[j, p:p + 1, :])
        return split(jnp.concatenate(rows, axis=0))

    for i in range(LATE):
        j = tail - 1 + i
        a, b = local_rows(j) if i == 1 else (own_rows(high, j), own_rows(low, j))
        begun[i] = product(j, a, b, BEFORE[i])

    lane = lax.broadcasted_iota(jnp.int32, flags.shape[1:], 1)
    pooled = (lane >= 2) & (lane != 2 * tail - 1)
    most = jnp.zeros((1, 1), jnp.float32)
    for k in range(ring):
        counted = jnp.where(pooled, flags[k], 0).astype(jnp.float32)
        total = jnp.sum(jnp.sum(counted, axis=1, keepdims=True), axis=0, keepdims=True)
        most = jnp.maximum(most, total)
    over[0] = jnp.sum(jnp.where(most > hosts, 1, 0))

    for side in (0, 1):
        edge(side).wait_send()
        relay(side).wait_send()

        @pl.loop(1, reach[side] + 1)
        def _(k):
            flag_hop(side, k).wait_send()

    across_end.wait_recv()
    convert(tail, direct(3), (1,))
    across_first.wait_send()
    across_last.wait_send()
    across_half.wait_send()
    across_end.wait_send()

    @pl.loop(2, tail)
    def _(j):
        across(j).wait_send()


DMA = pltpu.SemaphoreType.DMA
IN_VMEM = pl.BlockSpec(memory_space=pltpu.VMEM)


def results(pairs, wide, h, block):
    width = SLOTS * block
    return [
        pltpu.VMEM((pairs + 2, 8, width), jnp.float32),
        pltpu.VMEM((pairs + 2, 2 * block, width), jnp.bfloat16),
        pltpu.VMEM((pairs + 2, 2 * block, width), jnp.bfloat16),
        pltpu.VMEM((pairs - LATE, 2, wide, h, block), jnp.float32),
        pltpu.VMEM((LATE, 2 * h, width), jnp.float32),
    ]


def in_hbm(*arrays):
    return (pltpu.with_memory_space_constraint(x, pltpu.HBM) for x in arrays)


def finished(first_late, held, pairs, wide, h, block):
    return pl.pallas_call(
        functools.partial(finish, first_late),
        out_shape=pltpu.HBM((pairs, 2, wide, h, block), jnp.float32),
        in_specs=[IN_VMEM] * 5,
        out_specs=pl.BlockSpec(memory_space=pltpu.HBM),
        scratch_shapes=[
            pltpu.VMEM((LATE, 2, wide, h, block), jnp.float32),
            DMA((2,)),
            DMA((LATE,)),
        ],
        compiler_params=pltpu.CompilerParams(vmem_limit_bytes=16 << 20),
    )(*held)


def dense(cols, ring, density, pattern):
    rows, wide, h, block = density.shape
    pairs = rows // 2
    paired = density.reshape(pairs, 2, wide, h, block)
    held = pl.pallas_call(
        functools.partial(dense_kernel, cols, ring),
        out_shape=results(pairs, wide, h, block),
        in_specs=[pl.BlockSpec(memory_space=pltpu.HBM)] * 2,
        out_specs=[IN_VMEM] * 5,
        scratch_shapes=[
            pltpu.VMEM((cols, pairs + 2, 2, wide, h, block), jnp.float32),
            pltpu.VMEM((3, wide, rows), jnp.int32),
            DMA((pairs,)),
            DMA,
            DMA((cols - 1, pairs)),
            DMA((cols - 1, pairs)),
            DMA((2,)),
            DMA((2,)),
            DMA((2, cols - 1)),
            DMA((2, cols - 1)),
            DMA((2,)),
            DMA((2,)),
            pltpu.SemaphoreType.REGULAR,
            pltpu.SemaphoreType.REGULAR,
            pltpu.SemaphoreType.REGULAR,
        ],
        compiler_params=pltpu.CompilerParams(
            collective_id=0, has_side_effects=True, vmem_limit_bytes=42 << 20),
    )(*in_hbm(paired, pattern.T))
    out = finished(pairs - LATE + 1, held, pairs, wide, h, block)
    return out.reshape(density.shape)


def sparse(ring, density, pattern):
    rows, wide, h, block = density.shape
    pairs = rows // 2
    paired = density.reshape(pairs, 2 * wide, h, block)
    tail = pairs - GUEST - 1
    hosts = (tail - 1) * 2 * wide + wide
    room = GUEST * 2 * wide
    *held, over = pl.pallas_call(
        functools.partial(sparse_kernel, ring),
        out_shape=results(pairs, wide, h, block) + [jax.ShapeDtypeStruct((1,), jnp.int32)],
        in_specs=[pl.BlockSpec(memory_space=pltpu.HBM)] * 2,
        out_specs=[IN_VMEM] * 5 + [pl.BlockSpec(memory_space=pltpu.SMEM)],
        scratch_shapes=[
            pltpu.VMEM((pairs + 2, 2 * wide, h, block), jnp.float32),
            pltpu.VMEM((4, 2 * wide, h, block), jnp.float32),
            pltpu.VMEM((hosts, h, block), jnp.float32),
            pltpu.VMEM((room, h, block), jnp.float32),
            pltpu.VMEM((ring, wide, rows), jnp.int32),
            pltpu.SMEM((wide, rows), jnp.int32),
            pltpu.SMEM((room + 1,), jnp.int32),
            pltpu.SMEM((hosts + 2,), jnp.int32),
            pltpu.SMEM((room,), jnp.int32),
            DMA((pairs,)),
            DMA((GUEST,)),
            DMA,
            DMA,
            DMA((tail + 2,)),
            DMA((tail + 2,)),
            DMA((2,)),
            DMA((2,)),
            DMA((2,)),
            DMA((2,)),
            DMA((2, ring // 2)),
            DMA((2, ring // 2)),
            pltpu.SemaphoreType.REGULAR,
            pltpu.SemaphoreType.REGULAR,
            pltpu.SemaphoreType.REGULAR,
        ],
        compiler_params=pltpu.CompilerParams(
            collective_id=1, has_side_effects=True, vmem_limit_bytes=40 << 20),
    )(*in_hbm(paired, pattern.T))

    def done(density, pattern, *held):
        return finished(tail - 1, held, pairs, wide, h, block).reshape(density.shape)

    def again(density, pattern, *held):
        return dense(2, ring, density, pattern)

    return lax.cond(over[0] > 0, again, done, density, pattern, *held)


def shards(cols, ring, density, pattern):
    if cols == 2 and density.shape[0] >= 16:
        return sparse(ring, density, pattern)
    return dense(cols, ring, density, pattern)


def solution(mesh):
    cols = mesh.shape["col"]
    ring = mesh.shape["row"] * mesh.shape["depth"]
    in_specs = (P(RING, None, "col", None), P(RING, None))
    out_specs = P(RING, None, "col", None)
    body = functools.partial(shards, cols, ring)
    return jax.shard_map(body, mesh=mesh, in_specs=in_specs, out_specs=out_specs, check_vma=False)
```

```python
import functools

import jax
import jax.numpy as jnp
from jax import lax
from jax.experimental import pallas as pl
from jax.experimental.pallas import tpu as pltpu
from jax.sharding import PartitionSpec as P

MESH = pl.DeviceIdType.MESH
WIDE = 5
SLOTS = 6
RING = ("row", "depth")


def split(value):
    high = value.astype(jnp.bfloat16)
    low = (value - high.astype(jnp.float32)).astype(jnp.bfloat16)
    return high, low


def dot(a, b):
    return jnp.dot(a, b, preferred_element_type=jnp.float32)


def products(block, h, me, masks, high, low, out):
    two = 2 * block

    def product(j, a, b, sources=(0, 1, 2), start=None):
        both = jnp.concatenate([a, b], axis=0)
        m = a.shape[0]
        parts = []
        for n in range(3):
            total = None if start is None else start[:, n * two:(n + 1) * two]
            for k in sources:
                at = n - k + 1
                if at < 0 or at > 2:
                    continue
                lanes = slice(at * two, (at + 1) * two)
                ks = slice(k * two, (k + 1) * two)
                stacked = dot(both[:, ks], high[j + k - 1, :, lanes])
                term = stacked[:m] + stacked[m:] + dot(a[:, ks], low[j + k - 1, :, lanes])
                total = term if total is None else total + term
            parts.append(total)
        return jnp.concatenate(parts, axis=1)

    def own_rows(ref, j):
        return jnp.concatenate(
            [ref[j, pl.ds(pl.multiple_of(p * block + me * h, h), h), :] for p in range(2)], axis=0)

    def compute(j, to, sources=(0, 1, 2), start=None):
        factor = jnp.concatenate(
            [jnp.broadcast_to(masks[j, p:p + 1, :], (h, SLOTS * block)) for p in range(2)], axis=0)
        square = product(j, own_rows(high, j), own_rows(low, j), sources, start) * factor
        cube = product(j, *split(square)) * factor
        value = 3.0 * square - 2.0 * cube
        for p in range(2):
            for s in range(WIDE):
                out[to, p, s] = value[p * h:(p + 1) * h, (p + s) * block:(p + s + 1) * block]

    return product, own_rows, compute


BEFORE = ((0, 1), (0, 2), (1, 2))
AFTER = ((2,), (1,), (0,))
LATE = 3


def finish(first_late, masks, high, low, early, begun, out, late, early_sem, late_sem):
    h, block = early.shape[3], early.shape[4]
    me = lax.axis_index("col")
    before = first_late - 1
    after = early.shape[0] - before
    firsts = [pltpu.make_async_copy(early.at[pl.ds(0, before)], out.at[pl.ds(0, before)], early_sem.at[0])]
    if after:
        firsts.append(pltpu.make_async_copy(
            early.at[pl.ds(before, after)], out.at[pl.ds(before + LATE, after)], early_sem.at[1]))
    for first in firsts:
        first.start()
    _, _, compute = products(block, h, me, masks, high, low, late)

    def result(i):
        return pltpu.make_async_copy(late.at[i], out.at[before + i], late_sem.at[i])

    for i in range(LATE):
        compute(first_late + i, i, AFTER[i], begun[i])
        result(i).start()

    for first in firsts:
        first.wait()

    @pl.loop(0, LATE)
    def _(i):
        result(i).wait()


def dense_kernel(cols, ring, dens, pattern, masks, high, low, early, begun, raw, flags,
           local_sem, flag_sem, send_sem, recv_sem, edge_send, edge_recv,
           relay_send, relay_recv, flag_send, flag_recv, up, down, corner):
    pairs = dens.shape[0]
    h = dens.shape[3]
    block = dens.shape[4]
    last = pairs + 1
    me = lax.axis_index("col")
    depth = lax.axis_size("depth")
    place = lax.axis_index("row") * depth + lax.axis_index("depth")

    def on_ring(shift):
        at = lax.rem(place + shift + ring, ring)
        return {"row": at // depth, "depth": lax.rem(at, depth)}

    prev, following = on_ring(-1), on_ring(1)

    def peer(step):
        return {"col": lax.rem(me + step, cols)}

    def source(step):
        return lax.rem(me + cols - step, cols)

    def own(j):
        return pltpu.make_async_copy(dens.at[j - 1], raw.at[me, j], local_sem.at[j - 1])

    def across(step, j):
        return pltpu.make_async_remote_copy(
            dens.at[j - 1], raw.at[me, j], send_sem.at[step - 1, j - 1],
            recv_sem.at[step - 1, j - 1], device_id=peer(step), device_id_type=MESH)

    ends = ((pairs, 0, following), (1, last, prev))

    def edge(side):
        j, slot, device = ends[side]
        return pltpu.make_async_remote_copy(
            dens.at[j - 1], raw.at[me, slot], edge_send.at[side], edge_recv.at[side],
            device_id=device, device_id_type=MESH)

    def relay(side, step):
        j, slot, device = ends[side]
        return pltpu.make_async_remote_copy(
            raw.at[source(step), j], raw.at[source(step), slot], relay_send.at[side, step - 1],
            relay_recv.at[side, step - 1], device_id=device, device_id_type=MESH)

    def flag_edge(side):
        return pltpu.make_async_remote_copy(
            pattern, flags.at[2 * side], flag_send.at[side], flag_recv.at[side],
            device_id=ends[side][2], device_id_type=MESH)

    steps = range(1, cols)

    z, r = lax.axis_index("depth"), lax.axis_index("row")
    row_count = lax.axis_size("row")

    def greet(semaphore, device):
        pl.semaphore_signal(semaphore, inc=1, device_id=device, device_id_type=MESH)

    def along(step):
        return {"depth": z + step}

    def beside(step):
        return {"row": lax.rem(r + step + row_count, row_count)}

    barrier = pltpu.get_barrier_semaphore()
    for s in steps:
        greet(barrier, peer(s))

    @pl.when(z > 0)
    def _():
        greet(barrier, along(-1))

    @pl.when(z < depth - 1)
    def _():
        greet(barrier, along(1))

    @pl.when(z == 0)
    def _():
        greet(barrier, beside(-1))
        greet(barrier, beside(1))

    own_flags = pltpu.make_async_copy(pattern, flags.at[1], flag_sem)
    own_flags.start()
    near = jnp.where(z == 0, 2, 1) + jnp.where(z < depth - 1, 1, 0)
    pl.semaphore_wait(barrier, cols - 1 + near)

    for j in (1, pairs):
        for s in steps:
            across(s, j).start()

    @pl.loop(2, pairs)
    def _(j):
        for s in steps:
            across(s, j).start()

    @pl.when(z > 0)
    def _():
        pl.semaphore_wait(up, 1)

    @pl.when(z < depth - 1)
    def _():
        greet(up, along(1))

    @pl.when(z < depth - 2)
    def _():
        pl.semaphore_wait(down, 1)

    @pl.when((z > 0) & (z <= depth - 2))
    def _():
        greet(down, along(-1))

    @pl.when(z == 0)
    def _():
        greet(corner, beside(1))
        pl.semaphore_wait(corner, 1)

    for side in (0, 1):
        flag_edge(side).start()
        edge(side).start()

    @pl.loop(1, pairs + 1)
    def _(j):
        own(j).start()

    def expand(which, i, j):
        lane = lax.broadcasted_iota(jnp.int32, flags.shape[1:], 1)
        for p in range(2):
            picked = jnp.where(lane == i + p, flags[which], 0).astype(jnp.float32)
            spread = jnp.broadcast_to(jnp.sum(picked, axis=1, keepdims=True), (WIDE, block))
            for s in range(WIDE):
                masks[j, p:p + 1, (p + s) * block:(p + s + 1) * block] = spread[s:s + 1]
            empty = slice(0, block) if p else slice(WIDE * block, SLOTS * block)
            masks[j, p:p + 1, empty] = jnp.zeros((1, block), jnp.float32)

    def convert(j):
        for p in range(2):
            for s in range(WIDE):
                slot = p + s
                factor = masks[j, p:p + 1, slot * block:(slot + 1) * block]
                for c in range(cols):
                    a, b = split(raw[c, j, p, s] * factor)
                    rows = slice(p * block + c * h, p * block + (c + 1) * h)
                    lanes = slice(slot * block, (slot + 1) * block)
                    high[j, rows, lanes] = a
                    low[j, rows, lanes] = b
            empty = slice(0, block) if p else slice(WIDE * block, SLOTS * block)
            nothing = jnp.zeros((block, block), jnp.bfloat16)
            high[j, p * block:(p + 1) * block, empty] = nothing
            low[j, p * block:(p + 1) * block, empty] = nothing

    product, own_rows, compute = products(block, h, me, masks, high, low, early)

    own_flags.wait()

    @pl.loop(1, pairs + 1)
    def _(j):
        expand(1, 2 * (j - 1), j)

    for side in (0, 1):
        flag_edge(side).wait_recv()
    expand(0, 2 * (pairs - 1), 0)
    expand(2, 0, last)

    @pl.loop(1, pairs + 1)
    def _(j):
        own(j).wait()

    for j, side in ((1, 1), (pairs, 0)):
        for s in steps:
            across(s, j).wait_recv()
            relay(side, s).start()
        convert(j)
    for side in (0, 1):
        edge(side).wait_recv()
        for s in steps:
            relay(side, s).wait_recv()
        convert(ends[side][1])

    @pl.loop(2, pairs - 1)
    def _(j):
        for s in steps:
            across(s, j).wait_recv()
        convert(j)
        compute(j - 1, j - 2)

    def local_rows(j):
        rows = []
        for p in range(2):
            blocks = [raw[me, j, p, s] for s in range(WIDE)]
            empty = [jnp.zeros((h, block), jnp.float32)]
            row = jnp.concatenate(empty + blocks if p else blocks + empty, axis=1)
            rows.append(row * masks[j, p:p + 1, :])
        return split(jnp.concatenate(rows, axis=0))

    for i in range(LATE):
        j = pairs - LATE + 1 + i
        a, b = local_rows(j) if i == 1 else (own_rows(high, j), own_rows(low, j))
        begun[i] = product(j, a, b, BEFORE[i])

    for side in (0, 1):
        flag_edge(side).wait_send()
        edge(side).wait_send()
        for s in steps:
            relay(side, s).wait_send()
    for s in steps:
        across(s, pairs - 1).wait_recv()
    convert(pairs - 1)

    @pl.loop(1, pairs + 1)
    def _(j):
        for s in steps:
            across(s, j).wait_send()


EXTRA = 4
GUEST = 3
SHARED = 6


def sparse_kernel(ring, rows_across, dens, pattern, masks, high, low, early, begun, over,
                  mine, theirs, stage, hosted, passed, guests, fellows, flags, fellow_flags,
                  bits, word, need, chain, queue, spot, place_own, place_fellow, from_fellow, excess, spare,
                  local_sem, guest_sem, flag_sem, bits_sem, send_sem, recv_sem, edge_send, edge_recv,
                  relay_send, relay_recv, flag_send, flag_recv, fellow_send, fellow_recv,
                  pass_send, pass_recv, up, down, corner):
    pairs, pair_slots, h, block = dens.shape
    rows = 2 * pairs
    last = pairs + 1
    first_guest = pairs - GUEST
    tail = first_guest - 1
    shared = tail - SHARED
    room = guests.shape[0] - EXTRA
    hosts = hosted.shape[0]
    me = lax.axis_index("col")
    depth = lax.axis_size("depth")
    z, r = lax.axis_index("depth"), lax.axis_index("row")
    place = r * depth + z

    def on_ring(shift):
        at = lax.rem(place + shift + ring, ring)
        return {"row": at // depth, "depth": lax.rem(at, depth)}

    prev, following = on_ring(-1), on_ring(1)
    peer = {"col": 1 - me}
    fellow = {"row": r + 1 - 2 * lax.rem(r, 2)}

    def remote(source, target, send, recv, device):
        return pltpu.make_async_remote_copy(
            source, target, send, recv, device_id=device, device_id_type=MESH)

    def own(j):
        return pltpu.make_async_copy(dens.at[j - 1], mine.at[j], local_sem.at[j - 1])

    def guest_pair(i):
        return pl.ds(i * pair_slots, pair_slots)

    def own_guest(i):
        return pltpu.make_async_copy(
            dens.at[first_guest - 1 + i], guests.at[guest_pair(i)], guest_sem.at[i])

    def fellow_guest(i):
        return remote(dens.at[first_guest - 1 + i], fellows.at[guest_pair(i)],
                      fellow_send.at[i], fellow_recv.at[i], fellow)

    fellow_pattern = remote(pattern, fellow_flags, fellow_send.at[GUEST], fellow_recv.at[GUEST], fellow)

    def host(j):
        return j * pair_slots - WIDE

    def crossing(source, target, n):
        return remote(source, target, send_sem.at[n], recv_sem.at[n], peer)

    def staged(start, size, n):
        return crossing(stage.at[pl.ds(start, size)], hosted.at[pl.ds(start, size)], n)

    def across(j):
        return staged(host(j), pair_slots, j)

    across_first = crossing(dens.at[0, pl.ds(0, WIDE)], theirs.at[1, pl.ds(0, WIDE)], 0)
    across_second = staged(0, WIDE, tail + 1)
    across_last = staged(host(1), pair_slots, 1)
    across_half = staged(host(tail), WIDE, tail)
    extra_at = pl.ds(pair_slots - EXTRA, EXTRA)
    across_extra = crossing(dens.at[pairs - 2, extra_at], theirs.at[4, extra_at], tail + 2)
    across_end = crossing(
        dens.at[tail - 1, pl.ds(WIDE, WIDE)], theirs.at[3, pl.ds(WIDE, WIDE)], tail + 3)

    ends = ((pairs, 0, following), (1, last, prev))
    halo = (0, 2)

    def edge(side):
        j, slot, device = ends[side]
        return remote(dens.at[j - 1], mine.at[slot], edge_send.at[side], edge_recv.at[side], device)

    relay_ahead = remote(hosted.at[pl.ds(host(1), pair_slots)], theirs.at[0],
                         relay_send.at[0], relay_recv.at[0], following)
    relay_first = remote(theirs.at[1, pl.ds(0, WIDE)], theirs.at[2, pl.ds(0, WIDE)],
                         relay_send.at[1], relay_recv.at[1], prev)
    relay_second = remote(hosted.at[pl.ds(0, WIDE)], theirs.at[2, pl.ds(WIDE, WIDE)],
                          relay_send.at[2], relay_recv.at[2], prev)

    def hand_over(j):
        at = pl.ds((j - shared) * pair_slots, pair_slots)
        return remote(hosted.at[pl.ds(host(j), pair_slots)], passed.at[at],
                      pass_send.at[j - shared], pass_recv.at[j - shared], fellow)

    reach = (ring // 2, ring - 1 - ring // 2)

    def flag_hop(side, k):
        source = k - 1 if side == 0 else lax.rem(ring - k + 1, ring)
        target = k if side == 0 else ring - k
        return remote(flags.at[source], flags.at[target],
                      flag_send.at[side, k - 1], flag_recv.at[side, k - 1], ends[side][2])

    def greet(semaphore, device):
        pl.semaphore_signal(semaphore, inc=1, device_id=device, device_id_type=MESH)

    def along(step):
        return {"depth": z + step}

    def beside(step):
        return {"row": lax.rem(r + step + rows_across, rows_across)}

    barrier = pltpu.get_barrier_semaphore()
    greet(barrier, peer)
    greet(barrier, fellow)

    @pl.when(z > 0)
    def _():
        greet(barrier, along(-1))

    @pl.when(z < depth - 1)
    def _():
        greet(barrier, along(1))

    @pl.when(z == 0)
    def _():
        greet(barrier, beside(-1))
        greet(barrier, beside(1))

    own_bits = pltpu.make_async_copy(pattern, bits.at[0], bits_sem)
    own_bits.start()
    own_flags = pltpu.make_async_copy(pattern, flags.at[0], flag_sem)
    own_flags.start()
    own(1).start()
    for i in range(GUEST):
        own_guest(i).start()
    own(pairs).start()

    @pl.loop(2, pairs)
    def _(j):
        own(j).start()

    near = jnp.where(z == 0, 2, 1) + jnp.where(z < depth - 1, 1, 0)
    pl.semaphore_wait(barrier, 2 + near)

    across_first.start()
    fellow_pattern.start()
    for i in range(GUEST):
        fellow_guest(i).start()

    own_bits.wait()

    def need_rows(b):
        def pack(row, _):
            value = bits[b, 0, row]
            for s in range(1, WIDE):
                value = value | (bits[b, s, row] << s)
            word[row] = value
            return 0

        lax.fori_loop(0, rows, pack, 0, unroll=4)
        for row in (0, 1, rows - 2, rows - 1):
            need[b, row] = word[row]

        def keep(row, _):
            used = jnp.int32(0)
            for d in range(-2, 3):
                value = word[row + d]
                moved = value << d if d >= 0 else value >> -d
                used = used | (moved & -((value >> (2 - d)) & 1))
            need[b, row] = word[row] & used
            return 0

        lax.fori_loop(2, rows - 2, keep, 0, unroll=4)

    def active(b, row, s):
        return (need[b, row] >> s) & 1

    def row_of(j, q):
        return 2 * (j - 1) + q // WIDE, q % WIDE

    def count(value):
        total = value & 1
        for s in range(1, WIDE):
            total = total + ((value >> s) & 1)
        return total

    def holes(b, row):
        return WIDE - count(need[b, row])

    def tally(b):
        free = holes(b, rows - 2) + holes(b, rows - 1)
        free = lax.fori_loop(1, 2 * shared - 2, lambda row, n: n + holes(b, row), free)
        common = lax.fori_loop(2 * shared - 2, 2 * tail - 2, lambda row, n: n + holes(b, row), jnp.int32(0))
        end = holes(b, 2 * tail - 2)
        free = free + common + end
        start = 2 * first_guest - 2
        full, part = room // WIDE, room % WIDE
        used = jnp.int32(0)
        for i in range(full):
            used = used + count(need[b, start + i])
        if part:
            used = used + count(need[b, start + full] & ((1 << part) - 1))
        lend = jnp.minimum(common, jnp.maximum(free - end - used, 0))
        return used, free, lend

    def list_guests(b):
        nearest = jnp.int32(room)
        chain[room] = nearest
        chain[room + 1] = nearest
        for n in reversed(range(room)):
            nearest = jnp.where(active(b, *row_of(first_guest, n)) > 0, n, nearest)
            chain[n] = nearest
        for k in range(room):
            queue[b, k] = jnp.minimum(nearest, room - 1)
            nearest = chain[nearest + 1]
        queue[b, room] = room - 1

    def fill(j, base, slots, taken):
        for q in slots:
            used = active(0, *row_of(j, q))
            visitor = guests[queue[0, taken]]
            stage[base + q] = jnp.where(used > 0, mine[j, q], visitor)
            taken = jnp.minimum(taken + 1 - used, room)
        return taken

    need_rows(0)
    list_guests(0)
    own(1).wait()
    for i in range(GUEST):
        own_guest(i).wait()
    taken = fill(1, -WIDE, range(WIDE, pair_slots), jnp.int32(0))
    own(pairs).wait()
    across_second.start()
    taken = fill(pairs, host(1), range(pair_slots), taken)

    @pl.when(z > 0)
    def _():
        pl.semaphore_wait(up, 1)

    @pl.when(z < depth - 1)
    def _():
        greet(up, along(1))

    @pl.when(z < depth - 2)
    def _():
        pl.semaphore_wait(down, 1)

    @pl.when((z > 0) & (z <= depth - 2))
    def _():
        greet(down, along(-1))

    @pl.when(z == 0)
    def _():
        greet(corner, beside(1))
        pl.semaphore_wait(corner, 1)

    across_last.start()
    own_flags.wait()
    for side in (0, 1):
        flag_hop(side, 1).start()
        edge(side).start()

    own(2).wait()
    taken = fill(2, host(2), range(pair_slots), taken)

    def prepare(j, taken):
        own(j).wait()
        taken = fill(j, host(j), range(pair_slots), taken)
        across(j - 1).start()
        return taken

    taken = lax.fori_loop(3, shared, prepare, taken)

    fellow_pattern.wait_recv()
    fellow_bits = pltpu.make_async_copy(fellow_flags, bits.at[1], bits_sem)
    fellow_bits.start()
    own_used, own_free, own_lend = tally(0)
    excess[0] = jnp.maximum(own_used - own_free, 0)
    spare[0] = own_lend
    fellow_bits.wait()
    need_rows(1)
    list_guests(1)
    fellow_used, fellow_free, _ = tally(1)
    for i in range(GUEST):
        fellow_guest(i).wait_recv()

    def prepare_shared(j, carry):
        taken, lent = carry
        own(j).wait()
        base = host(j)
        for q in range(pair_slots):
            used = active(0, *row_of(j, q))
            ours = taken < own_used
            visitor = jnp.where(
                ours, guests[queue[0, jnp.minimum(taken, room)]],
                fellows[queue[1, jnp.minimum(fellow_free + lent, room)]])
            stage[base + q] = jnp.where(used > 0, mine[j, q], visitor)
            taken = taken + 1 - used
            lent = lent + jnp.where(ours, 0, 1 - used)
        across(j - 1).start()
        return taken, lent

    taken, _ = lax.fori_loop(shared, tail, prepare_shared, (taken, jnp.int32(0)))
    own(tail).wait()
    fill(tail, host(tail), range(WIDE), jnp.minimum(taken, room))
    across(tail - 1).start()

    @pl.loop(tail + 1, pairs)
    def _(j):
        own(j).wait()

    def scan(j, base, slots, free):
        for q in reversed(slots):
            free = jnp.where(active(0, *row_of(j, q)) > 0, free, base + q)
            chain[base + q] = free
        return free

    def scan_pair(i, free):
        j = tail - 1 - i
        return scan(j, host(j), range(pair_slots), free)

    free = jnp.int32(hosts)
    chain[hosts] = free
    chain[hosts + 1] = free
    free = scan(tail, host(tail), range(WIDE), free)
    free = lax.fori_loop(0, tail - 2, scan_pair, free)
    free = scan(pairs, host(1), range(pair_slots), free)
    free = scan(1, -WIDE, range(WIDE, pair_slots), free)
    across_half.start()
    across_extra.start()
    across_end.start()
    for k in range(room):
        spot[0, k] = jnp.minimum(free, hosts - 1)
        free = chain[free + 1]

    common = passed.shape[0]

    def scan_fellow(i, carry):
        nearest, above = carry
        j = tail - 1 - i
        for q in reversed(range(pair_slots)):
            hole = 1 - active(1, *row_of(j, q))
            above = above + hole
            lends = (hole > 0) & (fellow_free - above >= fellow_used)
            at = (j - shared) * pair_slots + q
            nearest = jnp.where(lends, at, nearest)
            chain[at] = nearest
        return nearest, above

    nearest = jnp.int32(common)
    chain[common] = nearest
    chain[common + 1] = nearest
    nearest, _ = lax.fori_loop(0, tail - shared, scan_fellow, (nearest, holes(1, 2 * tail - 2)))
    for k in range(room):
        spot[1, k] = jnp.minimum(nearest, common - 1)
        nearest = chain[nearest + 1]
    rank = jnp.int32(0)
    for n in range(room):
        place_own[n] = spot[0, jnp.minimum(rank, room - 1)]
        place_fellow[n] = spot[1, jnp.clip(rank - own_free, 0, room - 1)]
        from_fellow[n] = jnp.where(rank >= own_free, 1, 0)
        rank = rank + active(0, *row_of(first_guest, n))

    def absorb(k):
        fetch = pltpu.make_async_copy(flags.at[k], bits.at[2], bits_sem)
        fetch.start()
        fetch.wait()
        need_rows(2)
        used, free, lend = tally(2)
        excess[k] = jnp.maximum(used - free, 0)
        spare[k] = lend

    def expand(which, i, j):
        lane = lax.broadcasted_iota(jnp.int32, flags.shape[1:], 1)
        for p in range(2):
            picked = jnp.where(lane == i + p, flags[which], 0).astype(jnp.float32)
            spread = jnp.broadcast_to(jnp.sum(picked, axis=1, keepdims=True), (WIDE, block))
            for s in range(WIDE):
                masks[j, p:p + 1, (p + s) * block:(p + s + 1) * block] = spread[s:s + 1]
            empty = slice(0, block) if p else slice(WIDE * block, SLOTS * block)
            masks[j, p:p + 1, empty] = jnp.zeros((1, block), jnp.float32)

    def convert(j, other, halves=(0, 1)):
        for p in halves:
            for s in range(WIDE):
                slot = p + s
                lanes = slice(slot * block, (slot + 1) * block)
                factor = masks[j, p:p + 1, lanes]
                for c, value in ((me, mine[j, p * WIDE + s]), (1 - me, other(p * WIDE + s))):
                    a, b = split(value * factor)
                    at = pl.ds(pl.multiple_of(p * block + c * h, h), h)
                    high[j, at, lanes] = a
                    low[j, at, lanes] = b
            empty = slice(0, block) if p else slice(WIDE * block, SLOTS * block)
            nothing = jnp.zeros((block, block), jnp.bfloat16)
            high[j, p * block:(p + 1) * block, empty] = nothing
            low[j, p * block:(p + 1) * block, empty] = nothing

    def arrived(j):
        return lambda q: hosted[host(j) + q]

    def direct(i):
        return lambda q: theirs[i, q]

    def visiting(j):
        def block_at(q):
            n = (j - first_guest) * pair_slots + q
            if n >= room:
                return theirs[4, q]
            return jnp.where(from_fellow[n] > 0, passed[place_fellow[n]], hosted[place_own[n]])

        return block_at

    product, own_rows, compute = products(block, h, me, masks, high, low, early)

    @pl.loop(1, pairs + 1)
    def _(j):
        expand(0, 2 * (j - 1), j)

    for side in (0, 1):
        flag_hop(side, 1).wait_recv()
    for side in (0, 1):
        if reach[side] > 1:
            flag_hop(side, 2).start()
    expand(1, 2 * (pairs - 1), 0)
    expand(ring - 1, 0, last)

    across_first.wait_recv()
    relay_first.start()
    across_second.wait_recv()
    relay_second.start()
    convert(1, lambda q: theirs[1, q] if q < WIDE else hosted[q - WIDE])
    across_last.wait_recv()
    relay_ahead.start()
    convert(pairs, arrived(1))
    absorb(1)
    absorb(ring - 1)
    edge(0).wait_recv()
    relay_ahead.wait_recv()
    convert(0, direct(0))
    edge(1).wait_recv()
    relay_first.wait_recv()
    relay_second.wait_recv()
    convert(last, direct(2))

    turns = tail - 2
    each = -(-(reach[0] - 1) // turns)

    def pass_on(side, k):
        @pl.when(k <= reach[side])
        def _():
            flag_hop(side, k).wait_recv()

        @pl.when(k + 1 <= reach[side])
        def _():
            flag_hop(side, k + 1).start()

        @pl.when(k <= reach[side])
        def _():
            absorb(k if side == 0 else ring - k)

    @pl.loop(2, tail)
    def _(j):
        across(j).wait_recv()

        @pl.when(j >= shared)
        def _():
            hand_over(j).start()

        convert(j, arrived(j))
        compute(j - 1, j - 2)
        for u in range(each):
            for side in (0, 1):
                pass_on(side, (j - 2) * each + u + 2)

    bad = jnp.int32(0)
    for k in range(ring):
        there = lax.rem(place - k + ring, ring)
        band = there // depth
        partner = there + (1 - 2 * lax.rem(band, 2)) * depth
        bad = bad + jnp.where(excess[k] > spare[lax.rem(place - partner + ring, ring)], 1, 0)
    over[0] = bad

    for j in range(shared, tail):
        hand_over(j).wait_recv()
    across_half.wait_recv()
    for j in range(first_guest, pairs - 1):
        convert(j, visiting(j))
    convert(tail, arrived(tail), (0,))
    across_extra.wait_recv()
    convert(pairs - 1, visiting(pairs - 1))
    for i, j in enumerate(range(first_guest + 1, pairs + 1)):
        compute(j, tail - 2 + i)

    def local_rows(j):
        parts = []
        for p in range(2):
            blocks = [mine[j, p * WIDE + s] for s in range(WIDE)]
            empty = [jnp.zeros((h, block), jnp.float32)]
            row = jnp.concatenate(empty + blocks if p else blocks + empty, axis=1)
            parts.append(row * masks[j, p:p + 1, :])
        return split(jnp.concatenate(parts, axis=0))

    for i in range(LATE):
        j = tail - 1 + i
        a, b = local_rows(j) if i == 1 else (own_rows(high, j), own_rows(low, j))
        begun[i] = product(j, a, b, BEFORE[i])

    fellow_pattern.wait_send()
    for i in range(GUEST):
        fellow_guest(i).wait_send()
    for j in range(shared, tail):
        hand_over(j).wait_send()
    for side in (0, 1):
        edge(side).wait_send()

        @pl.loop(1, reach[side] + 1)
        def _(k):
            flag_hop(side, k).wait_send()

    relay_ahead.wait_send()
    relay_first.wait_send()
    relay_second.wait_send()

    across_end.wait_recv()
    convert(tail, direct(3), (1,))
    across_first.wait_send()
    across_second.wait_send()
    across_last.wait_send()
    across_half.wait_send()
    across_extra.wait_send()
    across_end.wait_send()

    @pl.loop(2, tail)
    def _(j):
        across(j).wait_send()


DMA = pltpu.SemaphoreType.DMA
IN_VMEM = pl.BlockSpec(memory_space=pltpu.VMEM)


def results(pairs, wide, h, block):
    width = SLOTS * block
    return [
        pltpu.VMEM((pairs + 2, 8, width), jnp.float32),
        pltpu.VMEM((pairs + 2, 2 * block, width), jnp.bfloat16),
        pltpu.VMEM((pairs + 2, 2 * block, width), jnp.bfloat16),
        pltpu.VMEM((pairs - LATE, 2, wide, h, block), jnp.float32),
        pltpu.VMEM((LATE, 2 * h, width), jnp.float32),
    ]


def in_hbm(*arrays):
    return (pltpu.with_memory_space_constraint(x, pltpu.HBM) for x in arrays)


def finished(first_late, held, pairs, wide, h, block):
    return pl.pallas_call(
        functools.partial(finish, first_late),
        out_shape=pltpu.HBM((pairs, 2, wide, h, block), jnp.float32),
        in_specs=[IN_VMEM] * 5,
        out_specs=pl.BlockSpec(memory_space=pltpu.HBM),
        scratch_shapes=[
            pltpu.VMEM((LATE, 2, wide, h, block), jnp.float32),
            DMA((2,)),
            DMA((LATE,)),
        ],
        compiler_params=pltpu.CompilerParams(vmem_limit_bytes=16 << 20),
    )(*held)


def dense(cols, ring, density, pattern):
    rows, wide, h, block = density.shape
    pairs = rows // 2
    paired = density.reshape(pairs, 2, wide, h, block)
    held = pl.pallas_call(
        functools.partial(dense_kernel, cols, ring),
        out_shape=results(pairs, wide, h, block),
        in_specs=[pl.BlockSpec(memory_space=pltpu.HBM)] * 2,
        out_specs=[IN_VMEM] * 5,
        scratch_shapes=[
            pltpu.VMEM((cols, pairs + 2, 2, wide, h, block), jnp.float32),
            pltpu.VMEM((3, wide, rows), jnp.int32),
            DMA((pairs,)),
            DMA,
            DMA((cols - 1, pairs)),
            DMA((cols - 1, pairs)),
            DMA((2,)),
            DMA((2,)),
            DMA((2, cols - 1)),
            DMA((2, cols - 1)),
            DMA((2,)),
            DMA((2,)),
            pltpu.SemaphoreType.REGULAR,
            pltpu.SemaphoreType.REGULAR,
            pltpu.SemaphoreType.REGULAR,
        ],
        compiler_params=pltpu.CompilerParams(
            collective_id=0, has_side_effects=True, vmem_limit_bytes=42 << 20),
    )(*in_hbm(paired, pattern.T))
    out = finished(pairs - LATE + 1, held, pairs, wide, h, block)
    return out.reshape(density.shape)


def sparse(ring, density, pattern):
    rows, wide, h, block = density.shape
    pairs = rows // 2
    paired = density.reshape(pairs, 2 * wide, h, block)
    tail = pairs - GUEST - 1
    hosts = tail * 2 * wide
    entries = GUEST * 2 * wide
    room = entries - EXTRA
    common = SHARED * 2 * wide
    scalars = pltpu.SMEM
    *held, over = pl.pallas_call(
        functools.partial(sparse_kernel, ring, lax.axis_size("row")),
        out_shape=results(pairs, wide, h, block) + [jax.ShapeDtypeStruct((1,), jnp.int32)],
        in_specs=[pl.BlockSpec(memory_space=pltpu.HBM)] * 2,
        out_specs=[IN_VMEM] * 5 + [pl.BlockSpec(memory_space=pltpu.SMEM)],
        scratch_shapes=[
            pltpu.VMEM((pairs + 2, 2 * wide, h, block), jnp.float32),
            pltpu.VMEM((5, 2 * wide, h, block), jnp.float32),
            pltpu.VMEM((hosts, h, block), jnp.float32),
            pltpu.VMEM((hosts, h, block), jnp.float32),
            pltpu.VMEM((common, h, block), jnp.float32),
            pltpu.VMEM((entries, h, block), jnp.float32),
            pltpu.VMEM((entries, h, block), jnp.float32),
            pltpu.VMEM((ring, wide, rows), jnp.int32),
            pltpu.VMEM((wide, rows), jnp.int32),
            scalars((3, wide, rows), jnp.int32),
            scalars((rows,), jnp.int32),
            scalars((3, rows), jnp.int32),
            scalars((hosts + 2,), jnp.int32),
            scalars((2, room + 1), jnp.int32),
            scalars((2, room), jnp.int32),
            scalars((room,), jnp.int32),
            scalars((room,), jnp.int32),
            scalars((room,), jnp.int32),
            scalars((ring,), jnp.int32),
            scalars((ring,), jnp.int32),
            DMA((pairs,)),
            DMA((GUEST,)),
            DMA,
            DMA,
            DMA((tail + 4,)),
            DMA((tail + 4,)),
            DMA((2,)),
            DMA((2,)),
            DMA((3,)),
            DMA((3,)),
            DMA((2, ring // 2)),
            DMA((2, ring // 2)),
            DMA((GUEST + 1,)),
            DMA((GUEST + 1,)),
            DMA((SHARED,)),
            DMA((SHARED,)),
            pltpu.SemaphoreType.REGULAR,
            pltpu.SemaphoreType.REGULAR,
            pltpu.SemaphoreType.REGULAR,
        ],
        compiler_params=pltpu.CompilerParams(
            collective_id=1, has_side_effects=True, vmem_limit_bytes=40 << 20),
    )(*in_hbm(paired, pattern.T))

    def done(density, pattern, *held):
        return finished(tail - 1, held, pairs, wide, h, block).reshape(density.shape)

    def again(density, pattern, *held):
        return dense(2, ring, density, pattern)

    return lax.cond(over[0] > 0, again, done, density, pattern, *held)


def shards(cols, ring, density, pattern):
    if cols == 2 and lax.axis_size("row") % 2 == 0 and density.shape[0] >= 32:
        return sparse(ring, density, pattern)
    return dense(cols, ring, density, pattern)


def solution(mesh):
    cols = mesh.shape["col"]
    ring = mesh.shape["row"] * mesh.shape["depth"]
    in_specs = (P(RING, None, "col", None), P(RING, None))
    out_specs = P(RING, None, "col", None)
    body = functools.partial(shards, cols, ring)
    return jax.shard_map(body, mesh=mesh, in_specs=in_specs, out_specs=out_specs, check_vma=False)
```

```python
import functools

import jax
import jax.numpy as jnp
from jax import lax
from jax.experimental import pallas as pl
from jax.experimental.pallas import tpu as pltpu
from jax.sharding import PartitionSpec as P

MESH = pl.DeviceIdType.MESH
WIDE = 5
SLOTS = 6
RING = ("row", "depth")


def split(value):
    high = value.astype(jnp.bfloat16)
    low = (value - high.astype(jnp.float32)).astype(jnp.bfloat16)
    return high, low


def dot(a, b):
    return jnp.dot(a, b, preferred_element_type=jnp.float32)


def products(block, h, me, masks, high, low, out):
    two = 2 * block

    def product(j, a, b, sources=(0, 1, 2), start=None):
        both = jnp.concatenate([a, b], axis=0)
        m = a.shape[0]
        parts = []
        for n in range(3):
            total = None if start is None else start[:, n * two:(n + 1) * two]
            for k in sources:
                at = n - k + 1
                if at < 0 or at > 2:
                    continue
                lanes = slice(at * two, (at + 1) * two)
                ks = slice(k * two, (k + 1) * two)
                stacked = dot(both[:, ks], high[j + k - 1, :, lanes])
                term = stacked[:m] + stacked[m:] + dot(a[:, ks], low[j + k - 1, :, lanes])
                total = term if total is None else total + term
            parts.append(total)
        return jnp.concatenate(parts, axis=1)

    def own_rows(ref, j):
        return jnp.concatenate(
            [ref[j, pl.ds(pl.multiple_of(p * block + me * h, h), h), :] for p in range(2)], axis=0)

    def compute(j, to, sources=(0, 1, 2), start=None):
        factor = jnp.concatenate(
            [jnp.broadcast_to(masks[j, p:p + 1, :], (h, SLOTS * block)) for p in range(2)], axis=0)
        square = product(j, own_rows(high, j), own_rows(low, j), sources, start) * factor
        cube = product(j, *split(square)) * factor
        value = 3.0 * square - 2.0 * cube
        for p in range(2):
            for s in range(WIDE):
                out[to, p, s] = value[p * h:(p + 1) * h, (p + s) * block:(p + s + 1) * block]

    return product, own_rows, compute


BEFORE = ((0, 1), (0, 2), (1, 2))
AFTER = ((2,), (1,), (0,))
LATE = 3


def finish(first_late, masks, high, low, early, begun, out, late, early_sem, late_sem):
    h, block = early.shape[3], early.shape[4]
    me = lax.axis_index("col")
    before = first_late - 1
    after = early.shape[0] - before
    firsts = [pltpu.make_async_copy(early.at[pl.ds(0, before)], out.at[pl.ds(0, before)], early_sem.at[0])]
    if after:
        firsts.append(pltpu.make_async_copy(
            early.at[pl.ds(before, after)], out.at[pl.ds(before + LATE, after)], early_sem.at[1]))
    for first in firsts:
        first.start()
    _, _, compute = products(block, h, me, masks, high, low, late)

    def result(i):
        return pltpu.make_async_copy(late.at[i], out.at[before + i], late_sem.at[i])

    for i in range(LATE):
        compute(first_late + i, i, AFTER[i], begun[i])
        result(i).start()

    for first in firsts:
        first.wait()

    @pl.loop(0, LATE)
    def _(i):
        result(i).wait()


def dense_kernel(cols, ring, dens, pattern, masks, high, low, early, begun, raw, flags,
           local_sem, flag_sem, send_sem, recv_sem, edge_send, edge_recv,
           relay_send, relay_recv, flag_send, flag_recv, up, down, corner):
    pairs = dens.shape[0]
    h = dens.shape[3]
    block = dens.shape[4]
    last = pairs + 1
    me = lax.axis_index("col")
    depth = lax.axis_size("depth")
    place = lax.axis_index("row") * depth + lax.axis_index("depth")

    def on_ring(shift):
        at = lax.rem(place + shift + ring, ring)
        return {"row": at // depth, "depth": lax.rem(at, depth)}

    prev, following = on_ring(-1), on_ring(1)

    def peer(step):
        return {"col": lax.rem(me + step, cols)}

    def source(step):
        return lax.rem(me + cols - step, cols)

    def own(j):
        return pltpu.make_async_copy(dens.at[j - 1], raw.at[me, j], local_sem.at[j - 1])

    def across(step, j):
        return pltpu.make_async_remote_copy(
            dens.at[j - 1], raw.at[me, j], send_sem.at[step - 1, j - 1],
            recv_sem.at[step - 1, j - 1], device_id=peer(step), device_id_type=MESH)

    ends = ((pairs, 0, following), (1, last, prev))

    def edge(side):
        j, slot, device = ends[side]
        return pltpu.make_async_remote_copy(
            dens.at[j - 1], raw.at[me, slot], edge_send.at[side], edge_recv.at[side],
            device_id=device, device_id_type=MESH)

    def relay(side, step):
        j, slot, device = ends[side]
        return pltpu.make_async_remote_copy(
            raw.at[source(step), j], raw.at[source(step), slot], relay_send.at[side, step - 1],
            relay_recv.at[side, step - 1], device_id=device, device_id_type=MESH)

    def flag_edge(side):
        return pltpu.make_async_remote_copy(
            pattern, flags.at[2 * side], flag_send.at[side], flag_recv.at[side],
            device_id=ends[side][2], device_id_type=MESH)

    steps = range(1, cols)

    z, r = lax.axis_index("depth"), lax.axis_index("row")
    row_count = lax.axis_size("row")

    def greet(semaphore, device):
        pl.semaphore_signal(semaphore, inc=1, device_id=device, device_id_type=MESH)

    def along(step):
        return {"depth": z + step}

    def beside(step):
        return {"row": lax.rem(r + step + row_count, row_count)}

    barrier = pltpu.get_barrier_semaphore()
    for s in steps:
        greet(barrier, peer(s))

    @pl.when(z > 0)
    def _():
        greet(barrier, along(-1))

    @pl.when(z < depth - 1)
    def _():
        greet(barrier, along(1))

    @pl.when(z == 0)
    def _():
        greet(barrier, beside(-1))
        greet(barrier, beside(1))

    own_flags = pltpu.make_async_copy(pattern, flags.at[1], flag_sem)
    own_flags.start()
    near = jnp.where(z == 0, 2, 1) + jnp.where(z < depth - 1, 1, 0)
    pl.semaphore_wait(barrier, cols - 1 + near)

    for j in (1, pairs):
        for s in steps:
            across(s, j).start()

    @pl.loop(2, pairs)
    def _(j):
        for s in steps:
            across(s, j).start()

    @pl.when(z > 0)
    def _():
        pl.semaphore_wait(up, 1)

    @pl.when(z < depth - 1)
    def _():
        greet(up, along(1))

    @pl.when(z < depth - 2)
    def _():
        pl.semaphore_wait(down, 1)

    @pl.when((z > 0) & (z <= depth - 2))
    def _():
        greet(down, along(-1))

    @pl.when(z == 0)
    def _():
        greet(corner, beside(1))
        pl.semaphore_wait(corner, 1)

    for side in (0, 1):
        flag_edge(side).start()
        edge(side).start()

    @pl.loop(1, pairs + 1)
    def _(j):
        own(j).start()

    def expand(which, i, j):
        lane = lax.broadcasted_iota(jnp.int32, flags.shape[1:], 1)
        for p in range(2):
            picked = jnp.where(lane == i + p, flags[which], 0).astype(jnp.float32)
            spread = jnp.broadcast_to(jnp.sum(picked, axis=1, keepdims=True), (WIDE, block))
            for s in range(WIDE):
                masks[j, p:p + 1, (p + s) * block:(p + s + 1) * block] = spread[s:s + 1]
            empty = slice(0, block) if p else slice(WIDE * block, SLOTS * block)
            masks[j, p:p + 1, empty] = jnp.zeros((1, block), jnp.float32)

    def convert(j):
        for p in range(2):
            for s in range(WIDE):
                slot = p + s
                factor = masks[j, p:p + 1, slot * block:(slot + 1) * block]
                for c in range(cols):
                    a, b = split(raw[c, j, p, s] * factor)
                    rows = slice(p * block + c * h, p * block + (c + 1) * h)
                    lanes = slice(slot * block, (slot + 1) * block)
                    high[j, rows, lanes] = a
                    low[j, rows, lanes] = b
            empty = slice(0, block) if p else slice(WIDE * block, SLOTS * block)
            nothing = jnp.zeros((block, block), jnp.bfloat16)
            high[j, p * block:(p + 1) * block, empty] = nothing
            low[j, p * block:(p + 1) * block, empty] = nothing

    product, own_rows, compute = products(block, h, me, masks, high, low, early)

    own_flags.wait()

    @pl.loop(1, pairs + 1)
    def _(j):
        expand(1, 2 * (j - 1), j)

    for side in (0, 1):
        flag_edge(side).wait_recv()
    expand(0, 2 * (pairs - 1), 0)
    expand(2, 0, last)

    @pl.loop(1, pairs + 1)
    def _(j):
        own(j).wait()

    for j, side in ((1, 1), (pairs, 0)):
        for s in steps:
            across(s, j).wait_recv()
            relay(side, s).start()
        convert(j)
    for side in (0, 1):
        edge(side).wait_recv()
        for s in steps:
            relay(side, s).wait_recv()
        convert(ends[side][1])

    @pl.loop(2, pairs - 1)
    def _(j):
        for s in steps:
            across(s, j).wait_recv()
        convert(j)
        compute(j - 1, j - 2)

    def local_rows(j):
        rows = []
        for p in range(2):
            blocks = [raw[me, j, p, s] for s in range(WIDE)]
            empty = [jnp.zeros((h, block), jnp.float32)]
            row = jnp.concatenate(empty + blocks if p else blocks + empty, axis=1)
            rows.append(row * masks[j, p:p + 1, :])
        return split(jnp.concatenate(rows, axis=0))

    for i in range(LATE):
        j = pairs - LATE + 1 + i
        a, b = local_rows(j) if i == 1 else (own_rows(high, j), own_rows(low, j))
        begun[i] = product(j, a, b, BEFORE[i])

    for side in (0, 1):
        flag_edge(side).wait_send()
        edge(side).wait_send()
        for s in steps:
            relay(side, s).wait_send()
    for s in steps:
        across(s, pairs - 1).wait_recv()
    convert(pairs - 1)

    @pl.loop(1, pairs + 1)
    def _(j):
        for s in steps:
            across(s, j).wait_send()


EXTRA = 4
GUEST = 3
SHARED = 6


def sparse_kernel(ring, rows_across, dens, pattern, masks, high, low, early, begun, over,
                  mine, theirs, stage, hosted, passed, guests, fellows, flags, fellow_flags,
                  bits, word, need, chain, queue, spot, place_own, place_fellow, from_fellow, excess, spare,
                  local_sem, guest_sem, flag_sem, bits_sem, send_sem, recv_sem, edge_send, edge_recv,
                  relay_send, relay_recv, flag_send, flag_recv, fellow_send, fellow_recv,
                  pass_send, pass_recv, ready, go):
    pairs, pair_slots, h, block = dens.shape
    rows = 2 * pairs
    last = pairs + 1
    first_guest = pairs - GUEST
    tail = first_guest - 1
    shared = tail - SHARED
    room = guests.shape[0] - EXTRA
    hosts = hosted.shape[0]
    me = lax.axis_index("col")
    depth = lax.axis_size("depth")
    z, r = lax.axis_index("depth"), lax.axis_index("row")
    place = r * depth + z

    def on_ring(shift):
        at = lax.rem(place + shift + ring, ring)
        return {"row": at // depth, "depth": lax.rem(at, depth)}

    prev, following = on_ring(-1), on_ring(1)
    peer = {"col": 1 - me}
    fellow = {"row": r + 1 - 2 * lax.rem(r, 2)}

    def remote(source, target, send, recv, device):
        return pltpu.make_async_remote_copy(
            source, target, send, recv, device_id=device, device_id_type=MESH)

    def own(j):
        return pltpu.make_async_copy(dens.at[j - 1], mine.at[j], local_sem.at[j - 1])

    def guest_pair(i):
        return pl.ds(i * pair_slots, pair_slots)

    def own_guest(i):
        return pltpu.make_async_copy(
            dens.at[first_guest - 1 + i], guests.at[guest_pair(i)], guest_sem.at[i])

    def fellow_guest(i):
        return remote(dens.at[first_guest - 1 + i], fellows.at[guest_pair(i)],
                      fellow_send.at[i], fellow_recv.at[i], fellow)

    fellow_pattern = remote(pattern, fellow_flags, fellow_send.at[GUEST], fellow_recv.at[GUEST], fellow)

    def host(j):
        return j * pair_slots - WIDE

    def crossing(source, target, n):
        return remote(source, target, send_sem.at[n], recv_sem.at[n], peer)

    def staged(start, size, n):
        return crossing(stage.at[pl.ds(start, size)], hosted.at[pl.ds(start, size)], n)

    def across(j):
        return staged(host(j), pair_slots, j)

    across_first = crossing(dens.at[0, pl.ds(0, WIDE)], theirs.at[1, pl.ds(0, WIDE)], 0)
    across_second = staged(0, WIDE, tail + 1)
    across_last = staged(host(1), pair_slots, 1)
    across_half = staged(host(tail), WIDE, tail)
    extra_at = pl.ds(pair_slots - EXTRA, EXTRA)
    across_extra = crossing(dens.at[pairs - 2, extra_at], theirs.at[4, extra_at], tail + 2)
    across_end = crossing(
        dens.at[tail - 1, pl.ds(WIDE, WIDE)], theirs.at[3, pl.ds(WIDE, WIDE)], tail + 3)

    ends = ((pairs, 0, following), (1, last, prev))
    halo = (0, 2)

    def edge(side):
        j, slot, device = ends[side]
        return remote(dens.at[j - 1], mine.at[slot], edge_send.at[side], edge_recv.at[side], device)

    relay_ahead = remote(hosted.at[pl.ds(host(1), pair_slots)], theirs.at[0],
                         relay_send.at[0], relay_recv.at[0], following)
    relay_first = remote(theirs.at[1, pl.ds(0, WIDE)], theirs.at[2, pl.ds(0, WIDE)],
                         relay_send.at[1], relay_recv.at[1], prev)
    relay_second = remote(hosted.at[pl.ds(0, WIDE)], theirs.at[2, pl.ds(WIDE, WIDE)],
                          relay_send.at[2], relay_recv.at[2], prev)

    def hand_over(j):
        at = pl.ds((j - shared) * pair_slots, pair_slots)
        return remote(hosted.at[pl.ds(host(j), pair_slots)], passed.at[at],
                      pass_send.at[j - shared], pass_recv.at[j - shared], fellow)

    reach = (ring // 2, ring - 1 - ring // 2)

    def flag_hop(side, k):
        source = k - 1 if side == 0 else lax.rem(ring - k + 1, ring)
        target = k if side == 0 else ring - k
        return remote(flags.at[source], flags.at[target],
                      flag_send.at[side, k - 1], flag_recv.at[side, k - 1], ends[side][2])

    def greet(semaphore, device):
        pl.semaphore_signal(semaphore, inc=1, device_id=device, device_id_type=MESH)

    core = lax.rem(r, 2)
    hub = (me == 0) & (core == 0)
    barrier = pltpu.get_barrier_semaphore()

    @pl.when(hub | (core == 1))
    def _():
        greet(barrier, peer)

    own_bits = pltpu.make_async_copy(pattern, bits.at[0], bits_sem)
    own_bits.start()
    own_flags = pltpu.make_async_copy(pattern, flags.at[0], flag_sem)
    own_flags.start()
    own(1).start()
    for i in range(GUEST):
        own_guest(i).start()
    own(pairs).start()

    @pl.loop(2, pairs)
    def _(j):
        own(j).start()

    @pl.when((me == 1) | (core == 1))
    def _():
        pl.semaphore_wait(barrier, 1)

    @pl.when((me == 1) & (core == 0))
    def _():
        greet(ready, peer)

    @pl.when(hub)
    def _():
        pl.semaphore_wait(ready, 1)

    across_first.start()

    @pl.when((me == 0) & (core == 1))
    def _():
        greet(barrier, fellow)

    own_bits.wait()

    def need_rows(b):
        def pack(row, _):
            value = bits[b, 0, row]
            for s in range(1, WIDE):
                value = value | (bits[b, s, row] << s)
            word[row] = value
            return 0

        lax.fori_loop(0, rows, pack, 0, unroll=4)
        for row in (0, 1, rows - 2, rows - 1):
            need[b, row] = word[row]

        def keep(row, _):
            used = jnp.int32(0)
            for d in range(-2, 3):
                value = word[row + d]
                moved = value << d if d >= 0 else value >> -d
                used = used | (moved & -((value >> (2 - d)) & 1))
            need[b, row] = word[row] & used
            return 0

        lax.fori_loop(2, rows - 2, keep, 0, unroll=4)

    def active(b, row, s):
        return (need[b, row] >> s) & 1

    def row_of(j, q):
        return 2 * (j - 1) + q // WIDE, q % WIDE

    def count(value):
        total = value & 1
        for s in range(1, WIDE):
            total = total + ((value >> s) & 1)
        return total

    def holes(b, row):
        return WIDE - count(need[b, row])

    def tally(b):
        free = holes(b, rows - 2) + holes(b, rows - 1)
        free = lax.fori_loop(1, 2 * shared - 2, lambda row, n: n + holes(b, row), free)
        common = lax.fori_loop(2 * shared - 2, 2 * tail - 2, lambda row, n: n + holes(b, row), jnp.int32(0))
        end = holes(b, 2 * tail - 2)
        free = free + common + end
        start = 2 * first_guest - 2
        full, part = room // WIDE, room % WIDE
        used = jnp.int32(0)
        for i in range(full):
            used = used + count(need[b, start + i])
        if part:
            used = used + count(need[b, start + full] & ((1 << part) - 1))
        lend = jnp.minimum(common, jnp.maximum(free - end - used, 0))
        return used, free, lend

    def list_guests(b):
        nearest = jnp.int32(room)
        chain[room] = nearest
        chain[room + 1] = nearest
        for n in reversed(range(room)):
            nearest = jnp.where(active(b, *row_of(first_guest, n)) > 0, n, nearest)
            chain[n] = nearest
        for k in range(room):
            queue[b, k] = jnp.minimum(nearest, room - 1)
            nearest = chain[nearest + 1]
        queue[b, room] = room - 1

    def fill(j, base, slots, taken):
        for q in slots:
            used = active(0, *row_of(j, q))
            visitor = guests[queue[0, taken]]
            stage[base + q] = jnp.where(used > 0, mine[j, q], visitor)
            taken = jnp.minimum(taken + 1 - used, room)
        return taken

    need_rows(0)
    list_guests(0)
    own(1).wait()
    for i in range(GUEST):
        own_guest(i).wait()
    taken = fill(1, -WIDE, range(WIDE, pair_slots), jnp.int32(0))
    own(pairs).wait()
    across_second.start()
    taken = fill(pairs, host(1), range(pair_slots), taken)

    own(2).wait()
    taken = fill(2, host(2), range(pair_slots), taken)
    across_last.start()

    def prepare(j, taken):
        own(j).wait()
        taken = fill(j, host(j), range(pair_slots), taken)
        across(j - 1).start()
        return taken

    taken = lax.fori_loop(3, shared, prepare, taken)

    deeper = hub & (z < depth - 1)
    further = hub & (z == 0) & (r + 2 < rows_across)

    @pl.when(hub)
    def _():
        pl.semaphore_wait(barrier, 1 + jnp.where(deeper, 1, 0) + jnp.where(further, 1, 0))

    @pl.when(hub & (z > 0))
    def _():
        greet(barrier, {"depth": z - 1})

    @pl.when(hub & (z == 0) & (r > 0))
    def _():
        greet(barrier, {"row": r - 2})

    @pl.when(jnp.logical_not(hub & (z == 0) & (r == 0)))
    def _():
        pl.semaphore_wait(go, 1)

    @pl.when(deeper)
    def _():
        greet(go, {"depth": z + 1})

    @pl.when(further)
    def _():
        greet(go, {"row": r + 2})

    @pl.when(hub)
    def _():
        greet(go, peer)
        greet(go, fellow)
        greet(go, {"row": r + 1, "col": 1 - me})

    fellow_pattern.start()
    for i in range(GUEST):
        fellow_guest(i).start()
    own_flags.wait()
    for side in (0, 1):
        flag_hop(side, 1).start()
        edge(side).start()

    fellow_pattern.wait_recv()
    fellow_bits = pltpu.make_async_copy(fellow_flags, bits.at[1], bits_sem)
    fellow_bits.start()
    own_used, own_free, own_lend = tally(0)
    excess[0] = jnp.maximum(own_used - own_free, 0)
    spare[0] = own_lend
    fellow_bits.wait()
    need_rows(1)
    list_guests(1)
    fellow_used, fellow_free, _ = tally(1)
    for i in range(GUEST):
        fellow_guest(i).wait_recv()

    def prepare_shared(j, carry):
        taken, lent = carry
        own(j).wait()
        base = host(j)
        for q in range(pair_slots):
            used = active(0, *row_of(j, q))
            ours = taken < own_used
            visitor = jnp.where(
                ours, guests[queue[0, jnp.minimum(taken, room)]],
                fellows[queue[1, jnp.minimum(fellow_free + lent, room)]])
            stage[base + q] = jnp.where(used > 0, mine[j, q], visitor)
            taken = taken + 1 - used
            lent = lent + jnp.where(ours, 0, 1 - used)
        across(j - 1).start()
        return taken, lent

    taken, _ = lax.fori_loop(shared, tail, prepare_shared, (taken, jnp.int32(0)))
    own(tail).wait()
    fill(tail, host(tail), range(WIDE), jnp.minimum(taken, room))
    across(tail - 1).start()

    @pl.loop(tail + 1, pairs)
    def _(j):
        own(j).wait()

    def scan(j, base, slots, free):
        for q in reversed(slots):
            free = jnp.where(active(0, *row_of(j, q)) > 0, free, base + q)
            chain[base + q] = free
        return free

    def scan_pair(i, free):
        j = tail - 1 - i
        return scan(j, host(j), range(pair_slots), free)

    free = jnp.int32(hosts)
    chain[hosts] = free
    chain[hosts + 1] = free
    free = scan(tail, host(tail), range(WIDE), free)
    free = lax.fori_loop(0, tail - 2, scan_pair, free)
    free = scan(pairs, host(1), range(pair_slots), free)
    free = scan(1, -WIDE, range(WIDE, pair_slots), free)
    across_half.start()
    across_extra.start()
    across_end.start()
    for k in range(room):
        spot[0, k] = jnp.minimum(free, hosts - 1)
        free = chain[free + 1]

    common = passed.shape[0]

    def scan_fellow(i, carry):
        nearest, above = carry
        j = tail - 1 - i
        for q in reversed(range(pair_slots)):
            hole = 1 - active(1, *row_of(j, q))
            above = above + hole
            lends = (hole > 0) & (fellow_free - above >= fellow_used)
            at = (j - shared) * pair_slots + q
            nearest = jnp.where(lends, at, nearest)
            chain[at] = nearest
        return nearest, above

    nearest = jnp.int32(common)
    chain[common] = nearest
    chain[common + 1] = nearest
    nearest, _ = lax.fori_loop(0, tail - shared, scan_fellow, (nearest, holes(1, 2 * tail - 2)))
    for k in range(room):
        spot[1, k] = jnp.minimum(nearest, common - 1)
        nearest = chain[nearest + 1]
    rank = jnp.int32(0)
    for n in range(room):
        place_own[n] = spot[0, jnp.minimum(rank, room - 1)]
        place_fellow[n] = spot[1, jnp.clip(rank - own_free, 0, room - 1)]
        from_fellow[n] = jnp.where(rank >= own_free, 1, 0)
        rank = rank + active(0, *row_of(first_guest, n))

    def absorb(k):
        fetch = pltpu.make_async_copy(flags.at[k], bits.at[2], bits_sem)
        fetch.start()
        fetch.wait()
        need_rows(2)
        used, free, lend = tally(2)
        excess[k] = jnp.maximum(used - free, 0)
        spare[k] = lend

    def expand(which, i, j):
        lane = lax.broadcasted_iota(jnp.int32, flags.shape[1:], 1)
        for p in range(2):
            picked = jnp.where(lane == i + p, flags[which], 0).astype(jnp.float32)
            spread = jnp.broadcast_to(jnp.sum(picked, axis=1, keepdims=True), (WIDE, block))
            for s in range(WIDE):
                masks[j, p:p + 1, (p + s) * block:(p + s + 1) * block] = spread[s:s + 1]
            empty = slice(0, block) if p else slice(WIDE * block, SLOTS * block)
            masks[j, p:p + 1, empty] = jnp.zeros((1, block), jnp.float32)

    def convert(j, other, halves=(0, 1)):
        for p in halves:
            for s in range(WIDE):
                slot = p + s
                lanes = slice(slot * block, (slot + 1) * block)
                factor = masks[j, p:p + 1, lanes]
                for c, value in ((me, mine[j, p * WIDE + s]), (1 - me, other(p * WIDE + s))):
                    a, b = split(value * factor)
                    at = pl.ds(pl.multiple_of(p * block + c * h, h), h)
                    high[j, at, lanes] = a
                    low[j, at, lanes] = b
            empty = slice(0, block) if p else slice(WIDE * block, SLOTS * block)
            nothing = jnp.zeros((block, block), jnp.bfloat16)
            high[j, p * block:(p + 1) * block, empty] = nothing
            low[j, p * block:(p + 1) * block, empty] = nothing

    def arrived(j):
        return lambda q: hosted[host(j) + q]

    def direct(i):
        return lambda q: theirs[i, q]

    def visiting(j):
        def block_at(q):
            n = (j - first_guest) * pair_slots + q
            if n >= room:
                return theirs[4, q]
            return jnp.where(from_fellow[n] > 0, passed[place_fellow[n]], hosted[place_own[n]])

        return block_at

    product, own_rows, compute = products(block, h, me, masks, high, low, early)

    @pl.loop(1, pairs + 1)
    def _(j):
        expand(0, 2 * (j - 1), j)

    for side in (0, 1):
        flag_hop(side, 1).wait_recv()
    for side in (0, 1):
        if reach[side] > 1:
            flag_hop(side, 2).start()
    expand(1, 2 * (pairs - 1), 0)
    expand(ring - 1, 0, last)

    across_first.wait_recv()
    relay_first.start()
    across_second.wait_recv()
    relay_second.start()
    convert(1, lambda q: theirs[1, q] if q < WIDE else hosted[q - WIDE])
    across_last.wait_recv()
    relay_ahead.start()
    convert(pairs, arrived(1))
    absorb(1)
    absorb(ring - 1)
    edge(0).wait_recv()
    relay_ahead.wait_recv()
    convert(0, direct(0))
    edge(1).wait_recv()
    relay_first.wait_recv()
    relay_second.wait_recv()
    convert(last, direct(2))

    turns = tail - 2
    each = -(-(reach[0] - 1) // turns)

    def pass_on(side, k):
        @pl.when(k <= reach[side])
        def _():
            flag_hop(side, k).wait_recv()

        @pl.when(k + 1 <= reach[side])
        def _():
            flag_hop(side, k + 1).start()

        @pl.when(k <= reach[side])
        def _():
            absorb(k if side == 0 else ring - k)

    @pl.loop(2, tail)
    def _(j):
        across(j).wait_recv()

        @pl.when(j >= shared)
        def _():
            hand_over(j).start()

        convert(j, arrived(j))
        compute(j - 1, j - 2)
        for u in range(each):
            for side in (0, 1):
                pass_on(side, (j - 2) * each + u + 2)

    bad = jnp.int32(0)
    for k in range(ring):
        there = lax.rem(place - k + ring, ring)
        band = there // depth
        partner = there + (1 - 2 * lax.rem(band, 2)) * depth
        bad = bad + jnp.where(excess[k] > spare[lax.rem(place - partner + ring, ring)], 1, 0)
    over[0] = bad

    for j in range(shared, tail):
        hand_over(j).wait_recv()
    across_half.wait_recv()
    for j in range(first_guest, pairs - 1):
        convert(j, visiting(j))
    convert(tail, arrived(tail), (0,))
    across_extra.wait_recv()
    convert(pairs - 1, visiting(pairs - 1))
    for i, j in enumerate(range(first_guest + 1, pairs + 1)):
        compute(j, tail - 2 + i)

    def local_rows(j):
        parts = []
        for p in range(2):
            blocks = [mine[j, p * WIDE + s] for s in range(WIDE)]
            empty = [jnp.zeros((h, block), jnp.float32)]
            row = jnp.concatenate(empty + blocks if p else blocks + empty, axis=1)
            parts.append(row * masks[j, p:p + 1, :])
        return split(jnp.concatenate(parts, axis=0))

    for i in range(LATE):
        j = tail - 1 + i
        a, b = local_rows(j) if i == 1 else (own_rows(high, j), own_rows(low, j))
        begun[i] = product(j, a, b, BEFORE[i])

    fellow_pattern.wait_send()
    for i in range(GUEST):
        fellow_guest(i).wait_send()
    for j in range(shared, tail):
        hand_over(j).wait_send()
    for side in (0, 1):
        edge(side).wait_send()

        @pl.loop(1, reach[side] + 1)
        def _(k):
            flag_hop(side, k).wait_send()

    relay_ahead.wait_send()
    relay_first.wait_send()
    relay_second.wait_send()

    across_end.wait_recv()
    convert(tail, direct(3), (1,))
    across_first.wait_send()
    across_second.wait_send()
    across_last.wait_send()
    across_half.wait_send()
    across_extra.wait_send()
    across_end.wait_send()

    @pl.loop(2, tail)
    def _(j):
        across(j).wait_send()


DMA = pltpu.SemaphoreType.DMA
IN_VMEM = pl.BlockSpec(memory_space=pltpu.VMEM)


def results(pairs, wide, h, block):
    width = SLOTS * block
    return [
        pltpu.VMEM((pairs + 2, 8, width), jnp.float32),
        pltpu.VMEM((pairs + 2, 2 * block, width), jnp.bfloat16),
        pltpu.VMEM((pairs + 2, 2 * block, width), jnp.bfloat16),
        pltpu.VMEM((pairs - LATE, 2, wide, h, block), jnp.float32),
        pltpu.VMEM((LATE, 2 * h, width), jnp.float32),
    ]


def in_hbm(*arrays):
    return (pltpu.with_memory_space_constraint(x, pltpu.HBM) for x in arrays)


def finished(first_late, held, pairs, wide, h, block):
    return pl.pallas_call(
        functools.partial(finish, first_late),
        out_shape=pltpu.HBM((pairs, 2, wide, h, block), jnp.float32),
        in_specs=[IN_VMEM] * 5,
        out_specs=pl.BlockSpec(memory_space=pltpu.HBM),
        scratch_shapes=[
            pltpu.VMEM((LATE, 2, wide, h, block), jnp.float32),
            DMA((2,)),
            DMA((LATE,)),
        ],
        compiler_params=pltpu.CompilerParams(vmem_limit_bytes=16 << 20),
    )(*held)


def dense(cols, ring, density, pattern):
    rows, wide, h, block = density.shape
    pairs = rows // 2
    paired = density.reshape(pairs, 2, wide, h, block)
    held = pl.pallas_call(
        functools.partial(dense_kernel, cols, ring),
        out_shape=results(pairs, wide, h, block),
        in_specs=[pl.BlockSpec(memory_space=pltpu.HBM)] * 2,
        out_specs=[IN_VMEM] * 5,
        scratch_shapes=[
            pltpu.VMEM((cols, pairs + 2, 2, wide, h, block), jnp.float32),
            pltpu.VMEM((3, wide, rows), jnp.int32),
            DMA((pairs,)),
            DMA,
            DMA((cols - 1, pairs)),
            DMA((cols - 1, pairs)),
            DMA((2,)),
            DMA((2,)),
            DMA((2, cols - 1)),
            DMA((2, cols - 1)),
            DMA((2,)),
            DMA((2,)),
            pltpu.SemaphoreType.REGULAR,
            pltpu.SemaphoreType.REGULAR,
            pltpu.SemaphoreType.REGULAR,
        ],
        compiler_params=pltpu.CompilerParams(
            collective_id=0, has_side_effects=True, vmem_limit_bytes=42 << 20),
    )(*in_hbm(paired, pattern.T))
    out = finished(pairs - LATE + 1, held, pairs, wide, h, block)
    return out.reshape(density.shape)


def sparse(ring, density, pattern):
    rows, wide, h, block = density.shape
    pairs = rows // 2
    paired = density.reshape(pairs, 2 * wide, h, block)
    tail = pairs - GUEST - 1
    hosts = tail * 2 * wide
    entries = GUEST * 2 * wide
    room = entries - EXTRA
    common = SHARED * 2 * wide
    scalars = pltpu.SMEM
    *held, over = pl.pallas_call(
        functools.partial(sparse_kernel, ring, lax.axis_size("row")),
        out_shape=results(pairs, wide, h, block) + [jax.ShapeDtypeStruct((1,), jnp.int32)],
        in_specs=[pl.BlockSpec(memory_space=pltpu.HBM)] * 2,
        out_specs=[IN_VMEM] * 5 + [pl.BlockSpec(memory_space=pltpu.SMEM)],
        scratch_shapes=[
            pltpu.VMEM((pairs + 2, 2 * wide, h, block), jnp.float32),
            pltpu.VMEM((5, 2 * wide, h, block), jnp.float32),
            pltpu.VMEM((hosts, h, block), jnp.float32),
            pltpu.VMEM((hosts, h, block), jnp.float32),
            pltpu.VMEM((common, h, block), jnp.float32),
            pltpu.VMEM((entries, h, block), jnp.float32),
            pltpu.VMEM((entries, h, block), jnp.float32),
            pltpu.VMEM((ring, wide, rows), jnp.int32),
            pltpu.VMEM((wide, rows), jnp.int32),
            scalars((3, wide, rows), jnp.int32),
            scalars((rows,), jnp.int32),
            scalars((3, rows), jnp.int32),
            scalars((hosts + 2,), jnp.int32),
            scalars((2, room + 1), jnp.int32),
            scalars((2, room), jnp.int32),
            scalars((room,), jnp.int32),
            scalars((room,), jnp.int32),
            scalars((room,), jnp.int32),
            scalars((ring,), jnp.int32),
            scalars((ring,), jnp.int32),
            DMA((pairs,)),
            DMA((GUEST,)),
            DMA,
            DMA,
            DMA((tail + 4,)),
            DMA((tail + 4,)),
            DMA((2,)),
            DMA((2,)),
            DMA((3,)),
            DMA((3,)),
            DMA((2, ring // 2)),
            DMA((2, ring // 2)),
            DMA((GUEST + 1,)),
            DMA((GUEST + 1,)),
            DMA((SHARED,)),
            DMA((SHARED,)),
            pltpu.SemaphoreType.REGULAR,
            pltpu.SemaphoreType.REGULAR,
        ],
        compiler_params=pltpu.CompilerParams(
            collective_id=1, has_side_effects=True, vmem_limit_bytes=40 << 20),
    )(*in_hbm(paired, pattern.T))

    def done(density, pattern, *held):
        return finished(tail - 1, held, pairs, wide, h, block).reshape(density.shape)

    def again(density, pattern, *held):
        return dense(2, ring, density, pattern)

    return lax.cond(over[0] > 0, again, done, density, pattern, *held)


def shards(cols, ring, density, pattern):
    if cols == 2 and lax.axis_size("row") % 2 == 0 and density.shape[0] >= 32:
        return sparse(ring, density, pattern)
    return dense(cols, ring, density, pattern)


def solution(mesh):
    cols = mesh.shape["col"]
    ring = mesh.shape["row"] * mesh.shape["depth"]
    in_specs = (P(RING, None, "col", None), P(RING, None))
    out_specs = P(RING, None, "col", None)
    body = functools.partial(shards, cols, ring)
    return jax.shard_map(body, mesh=mesh, in_specs=in_specs, out_specs=out_specs, check_vma=False)
```

```python
import functools

import jax
import jax.numpy as jnp
from jax import lax
from jax.experimental import pallas as pl
from jax.experimental.pallas import tpu as pltpu
from jax.sharding import PartitionSpec as P

MESH = pl.DeviceIdType.MESH
WIDE = 5
SLOTS = 6
RING = ("row", "depth")


def split(value):
    high = value.astype(jnp.bfloat16)
    low = (value - high.astype(jnp.float32)).astype(jnp.bfloat16)
    return high, low


def dot(a, b):
    return jnp.dot(a, b, preferred_element_type=jnp.float32)


def products(block, h, me, masks, high, low, out):
    two = 2 * block

    def product(j, a, b, sources=(0, 1, 2), start=None):
        both = jnp.concatenate([a, b], axis=0)
        m = a.shape[0]
        parts = []
        for n in range(3):
            total = None if start is None else start[:, n * two:(n + 1) * two]
            for k in sources:
                at = n - k + 1
                if at < 0 or at > 2:
                    continue
                lanes = slice(at * two, (at + 1) * two)
                ks = slice(k * two, (k + 1) * two)
                stacked = dot(both[:, ks], high[j + k - 1, :, lanes])
                term = stacked[:m] + stacked[m:] + dot(a[:, ks], low[j + k - 1, :, lanes])
                total = term if total is None else total + term
            parts.append(jnp.zeros((m, two), jnp.float32) if total is None else total)
        return jnp.concatenate(parts, axis=1)

    def own_rows(ref, j):
        return jnp.concatenate(
            [ref[j, pl.ds(pl.multiple_of(p * block + me * h, h), h), :] for p in range(2)], axis=0)

    def compute(j, to, sources=(0, 1, 2), start=None):
        factor = jnp.concatenate(
            [jnp.broadcast_to(masks[j, p:p + 1, :], (h, SLOTS * block)) for p in range(2)], axis=0)
        square = product(j, own_rows(high, j), own_rows(low, j), sources, start) * factor
        cube = product(j, *split(square)) * factor
        value = 3.0 * square - 2.0 * cube
        for p in range(2):
            for s in range(WIDE):
                out[to, p, s] = value[p * h:(p + 1) * h, (p + s) * block:(p + s + 1) * block]

    return product, own_rows, compute


BEFORE = ((0, 1), (0, 2), (1, 2))
AFTER = ((2,), (1,), (0,))
LATE = 3


def finish(first_late, masks, high, low, early, begun, out, late, early_sem, late_sem):
    h, block = early.shape[3], early.shape[4]
    me = lax.axis_index("col")
    before = first_late - 1
    after = early.shape[0] - before
    firsts = [pltpu.make_async_copy(early.at[pl.ds(0, before)], out.at[pl.ds(0, before)], early_sem.at[0])]
    if after:
        firsts.append(pltpu.make_async_copy(
            early.at[pl.ds(before, after)], out.at[pl.ds(before + LATE, after)], early_sem.at[1]))
    for first in firsts:
        first.start()
    _, _, compute = products(block, h, me, masks, high, low, late)

    def result(i):
        return pltpu.make_async_copy(late.at[i], out.at[before + i], late_sem.at[i])

    for i in range(LATE):
        compute(first_late + i, i, AFTER[i], begun[i])
        result(i).start()

    for first in firsts:
        first.wait()

    @pl.loop(0, LATE)
    def _(i):
        result(i).wait()


def dense_kernel(cols, ring, dens, pattern, masks, high, low, early, begun, raw, flags,
           local_sem, flag_sem, send_sem, recv_sem, edge_send, edge_recv,
           relay_send, relay_recv, flag_send, flag_recv, up, down, corner):
    pairs = dens.shape[0]
    h = dens.shape[3]
    block = dens.shape[4]
    last = pairs + 1
    me = lax.axis_index("col")
    depth = lax.axis_size("depth")
    place = lax.axis_index("row") * depth + lax.axis_index("depth")

    def on_ring(shift):
        at = lax.rem(place + shift + ring, ring)
        return {"row": at // depth, "depth": lax.rem(at, depth)}

    prev, following = on_ring(-1), on_ring(1)

    def peer(step):
        return {"col": lax.rem(me + step, cols)}

    def source(step):
        return lax.rem(me + cols - step, cols)

    def own(j):
        return pltpu.make_async_copy(dens.at[j - 1], raw.at[me, j], local_sem.at[j - 1])

    def across(step, j):
        return pltpu.make_async_remote_copy(
            dens.at[j - 1], raw.at[me, j], send_sem.at[step - 1, j - 1],
            recv_sem.at[step - 1, j - 1], device_id=peer(step), device_id_type=MESH)

    ends = ((pairs, 0, following), (1, last, prev))

    def edge(side):
        j, slot, device = ends[side]
        return pltpu.make_async_remote_copy(
            dens.at[j - 1], raw.at[me, slot], edge_send.at[side], edge_recv.at[side],
            device_id=device, device_id_type=MESH)

    def relay(side, step):
        j, slot, device = ends[side]
        return pltpu.make_async_remote_copy(
            raw.at[source(step), j], raw.at[source(step), slot], relay_send.at[side, step - 1],
            relay_recv.at[side, step - 1], device_id=device, device_id_type=MESH)

    def flag_edge(side):
        return pltpu.make_async_remote_copy(
            pattern, flags.at[2 * side], flag_send.at[side], flag_recv.at[side],
            device_id=ends[side][2], device_id_type=MESH)

    steps = range(1, cols)

    z, r = lax.axis_index("depth"), lax.axis_index("row")
    row_count = lax.axis_size("row")

    def greet(semaphore, device):
        pl.semaphore_signal(semaphore, inc=1, device_id=device, device_id_type=MESH)

    def along(step):
        return {"depth": z + step}

    def beside(step):
        return {"row": lax.rem(r + step + row_count, row_count)}

    barrier = pltpu.get_barrier_semaphore()
    for s in steps:
        greet(barrier, peer(s))

    @pl.when(z > 0)
    def _():
        greet(barrier, along(-1))

    @pl.when(z < depth - 1)
    def _():
        greet(barrier, along(1))

    @pl.when(z == 0)
    def _():
        greet(barrier, beside(-1))
        greet(barrier, beside(1))

    own_flags = pltpu.make_async_copy(pattern, flags.at[1], flag_sem)
    own_flags.start()
    near = jnp.where(z == 0, 2, 1) + jnp.where(z < depth - 1, 1, 0)
    pl.semaphore_wait(barrier, cols - 1 + near)

    for j in (1, pairs):
        for s in steps:
            across(s, j).start()

    @pl.loop(2, pairs)
    def _(j):
        for s in steps:
            across(s, j).start()

    @pl.when(z > 0)
    def _():
        pl.semaphore_wait(up, 1)

    @pl.when(z < depth - 1)
    def _():
        greet(up, along(1))

    @pl.when(z < depth - 2)
    def _():
        pl.semaphore_wait(down, 1)

    @pl.when((z > 0) & (z <= depth - 2))
    def _():
        greet(down, along(-1))

    @pl.when(z == 0)
    def _():
        greet(corner, beside(1))
        pl.semaphore_wait(corner, 1)

    for side in (0, 1):
        flag_edge(side).start()
        edge(side).start()

    @pl.loop(1, pairs + 1)
    def _(j):
        own(j).start()

    def expand(which, i, j):
        lane = lax.broadcasted_iota(jnp.int32, flags.shape[1:], 1)
        for p in range(2):
            picked = jnp.where(lane == i + p, flags[which], 0).astype(jnp.float32)
            spread = jnp.broadcast_to(jnp.sum(picked, axis=1, keepdims=True), (WIDE, block))
            for s in range(WIDE):
                masks[j, p:p + 1, (p + s) * block:(p + s + 1) * block] = spread[s:s + 1]
            empty = slice(0, block) if p else slice(WIDE * block, SLOTS * block)
            masks[j, p:p + 1, empty] = jnp.zeros((1, block), jnp.float32)

    def convert(j):
        for p in range(2):
            for s in range(WIDE):
                slot = p + s
                factor = masks[j, p:p + 1, slot * block:(slot + 1) * block]
                for c in range(cols):
                    a, b = split(raw[c, j, p, s] * factor)
                    rows = slice(p * block + c * h, p * block + (c + 1) * h)
                    lanes = slice(slot * block, (slot + 1) * block)
                    high[j, rows, lanes] = a
                    low[j, rows, lanes] = b
            empty = slice(0, block) if p else slice(WIDE * block, SLOTS * block)
            nothing = jnp.zeros((block, block), jnp.bfloat16)
            high[j, p * block:(p + 1) * block, empty] = nothing
            low[j, p * block:(p + 1) * block, empty] = nothing

    product, own_rows, compute = products(block, h, me, masks, high, low, early)

    own_flags.wait()

    @pl.loop(1, pairs + 1)
    def _(j):
        expand(1, 2 * (j - 1), j)

    for side in (0, 1):
        flag_edge(side).wait_recv()
    expand(0, 2 * (pairs - 1), 0)
    expand(2, 0, last)

    @pl.loop(1, pairs + 1)
    def _(j):
        own(j).wait()

    for j, side in ((1, 1), (pairs, 0)):
        for s in steps:
            across(s, j).wait_recv()
            relay(side, s).start()
        convert(j)
    for side in (0, 1):
        edge(side).wait_recv()
        for s in steps:
            relay(side, s).wait_recv()
        convert(ends[side][1])

    @pl.loop(2, pairs - 1)
    def _(j):
        for s in steps:
            across(s, j).wait_recv()
        convert(j)
        compute(j - 1, j - 2)

    def local_rows(j):
        rows = []
        for p in range(2):
            blocks = [raw[me, j, p, s] for s in range(WIDE)]
            empty = [jnp.zeros((h, block), jnp.float32)]
            row = jnp.concatenate(empty + blocks if p else blocks + empty, axis=1)
            rows.append(row * masks[j, p:p + 1, :])
        return split(jnp.concatenate(rows, axis=0))

    for i in range(LATE):
        j = pairs - LATE + 1 + i
        a, b = local_rows(j) if i == 1 else (own_rows(high, j), own_rows(low, j))
        begun[i] = product(j, a, b, BEFORE[i])

    for side in (0, 1):
        flag_edge(side).wait_send()
        edge(side).wait_send()
        for s in steps:
            relay(side, s).wait_send()
    for s in steps:
        across(s, pairs - 1).wait_recv()
    convert(pairs - 1)

    @pl.loop(1, pairs + 1)
    def _(j):
        for s in steps:
            across(s, j).wait_send()


EXTRA = 2
GUEST = 3
SHARED = 6


def sparse_kernel(ring, rows_across, dens, pattern, masks, high, low, early, begun, over,
                  mine, theirs, stage, hosted, passed, guests, fellows, flags, fellow_flags,
                  bits, word, need, chain, queue, spot, place_own, place_fellow, from_fellow, excess, spare, ahead,
                  local_sem, guest_sem, flag_sem, bits_sem, send_sem, recv_sem, edge_send, edge_recv,
                  relay_send, relay_recv, flag_send, flag_recv, fellow_send, fellow_recv,
                  pass_send, pass_recv, ready, go):
    pairs, pair_slots, h, block = dens.shape
    rows = 2 * pairs
    last = pairs + 1
    first_guest = pairs - GUEST
    tail = first_guest - 1
    shared = tail - SHARED
    room = guests.shape[0] - EXTRA
    hosts = hosted.shape[0]
    me = lax.axis_index("col")
    depth = lax.axis_size("depth")
    z, r = lax.axis_index("depth"), lax.axis_index("row")
    place = r * depth + z

    def on_ring(shift):
        at = lax.rem(place + shift + ring, ring)
        return {"row": at // depth, "depth": lax.rem(at, depth)}

    prev, following = on_ring(-1), on_ring(1)
    peer = {"col": 1 - me}
    fellow = {"row": r + 1 - 2 * lax.rem(r, 2)}

    def remote(source, target, send, recv, device):
        return pltpu.make_async_remote_copy(
            source, target, send, recv, device_id=device, device_id_type=MESH)

    def own(j):
        return pltpu.make_async_copy(dens.at[j - 1], mine.at[j], local_sem.at[j - 1])

    def guest_pair(i):
        return pl.ds(i * pair_slots, pair_slots)

    def own_guest(i):
        return pltpu.make_async_copy(
            dens.at[first_guest - 1 + i], guests.at[guest_pair(i)], guest_sem.at[i])

    def fellow_guest(i):
        return remote(dens.at[first_guest - 1 + i], fellows.at[guest_pair(i)],
                      fellow_send.at[i], fellow_recv.at[i], fellow)

    fellow_pattern = remote(pattern, fellow_flags, fellow_send.at[GUEST], fellow_recv.at[GUEST], fellow)

    def host(j):
        return j * pair_slots - WIDE

    def crossing(source, target, n):
        return remote(source, target, send_sem.at[n], recv_sem.at[n], peer)

    def staged(start, size, n):
        return crossing(stage.at[pl.ds(start, size)], hosted.at[pl.ds(start, size)], n)

    def across(j):
        return staged(host(j), pair_slots, j)

    across_first = crossing(dens.at[0, pl.ds(0, WIDE)], theirs.at[1, pl.ds(0, WIDE)], 0)
    across_second = staged(0, WIDE, tail + 1)
    across_last = staged(host(1), pair_slots, 1)
    across_half = staged(host(tail), WIDE, tail)
    extra_at = pl.ds(pair_slots - EXTRA, EXTRA)
    across_extra = crossing(dens.at[pairs - 2, extra_at], theirs.at[4, extra_at], tail + 2)
    across_end = crossing(
        dens.at[tail - 1, pl.ds(WIDE, WIDE)], theirs.at[3, pl.ds(WIDE, WIDE)], tail + 3)

    ends = ((pairs, 0, following), (1, last, prev))
    halo = (0, 2)

    def edge(side):
        j, slot, device = ends[side]
        return remote(dens.at[j - 1], mine.at[slot], edge_send.at[side], edge_recv.at[side], device)

    relay_ahead = remote(hosted.at[pl.ds(host(1), pair_slots)], theirs.at[0],
                         relay_send.at[0], relay_recv.at[0], following)
    relay_first = remote(theirs.at[1, pl.ds(0, WIDE)], theirs.at[2, pl.ds(0, WIDE)],
                         relay_send.at[1], relay_recv.at[1], prev)
    relay_second = remote(hosted.at[pl.ds(0, WIDE)], theirs.at[2, pl.ds(WIDE, WIDE)],
                          relay_send.at[2], relay_recv.at[2], prev)

    def hand_over(j):
        at = pl.ds((j - shared) * pair_slots, pair_slots)
        return remote(hosted.at[pl.ds(host(j), pair_slots)], passed.at[at],
                      pass_send.at[j - shared], pass_recv.at[j - shared], fellow)

    reach = (ring // 2, ring - 1 - ring // 2)

    def flag_hop(side, k):
        source = k - 1 if side == 0 else lax.rem(ring - k + 1, ring)
        target = k if side == 0 else ring - k
        return remote(flags.at[source], flags.at[target],
                      flag_send.at[side, k - 1], flag_recv.at[side, k - 1], ends[side][2])

    def greet(semaphore, device):
        pl.semaphore_signal(semaphore, inc=1, device_id=device, device_id_type=MESH)

    core = lax.rem(r, 2)
    hub = (me == 0) & (core == 0)
    barrier = pltpu.get_barrier_semaphore()

    @pl.when(hub | (core == 1))
    def _():
        greet(barrier, peer)

    own_bits = pltpu.make_async_copy(pattern, bits.at[0], bits_sem)
    own_bits.start()
    own_flags = pltpu.make_async_copy(pattern, flags.at[0], flag_sem)
    own_flags.start()
    own(1).start()
    for i in range(GUEST):
        own_guest(i).start()
    own(pairs).start()

    @pl.loop(2, pairs)
    def _(j):
        own(j).start()

    @pl.when((me == 1) | (core == 1))
    def _():
        pl.semaphore_wait(barrier, 1)

    @pl.when((me == 1) & (core == 0))
    def _():
        greet(ready, peer)

    @pl.when(hub)
    def _():
        pl.semaphore_wait(ready, 1)

    across_first.start()

    @pl.when((me == 0) & (core == 1))
    def _():
        greet(barrier, fellow)

    own_bits.wait()

    def need_rows(b):
        def pack(row, _):
            value = bits[b, 0, row]
            for s in range(1, WIDE):
                value = value | (bits[b, s, row] << s)
            word[row] = value
            return 0

        lax.fori_loop(0, rows, pack, 0, unroll=4)
        for row in (0, 1, rows - 2, rows - 1):
            need[b, row] = word[row]

        def keep(row, _):
            used = jnp.int32(0)
            for d in range(-2, 3):
                value = word[row + d]
                moved = value << d if d >= 0 else value >> -d
                used = used | (moved & -((value >> (2 - d)) & 1))
            need[b, row] = word[row] & used
            return 0

        lax.fori_loop(2, rows - 2, keep, 0, unroll=4)

    def active(b, row, s):
        return (need[b, row] >> s) & 1

    def row_of(j, q):
        return 2 * (j - 1) + q // WIDE, q % WIDE

    def count(value):
        total = value & 1
        for s in range(1, WIDE):
            total = total + ((value >> s) & 1)
        return total

    def holes(b, row):
        return WIDE - count(need[b, row])

    def tally(b):
        free = holes(b, rows - 2) + holes(b, rows - 1)
        free = lax.fori_loop(1, 2 * shared - 2, lambda row, n: n + holes(b, row), free)
        common = lax.fori_loop(2 * shared - 2, 2 * tail - 2, lambda row, n: n + holes(b, row), jnp.int32(0))
        end = holes(b, 2 * tail - 2)
        free = free + common + end
        start = 2 * first_guest - 2
        full, part = room // WIDE, room % WIDE
        used = jnp.int32(0)
        for i in range(full):
            used = used + count(need[b, start + i])
        if part:
            used = used + count(need[b, start + full] & ((1 << part) - 1))
        lend = jnp.minimum(common, jnp.maximum(free - end - used, 0))
        return used, free, lend

    def list_guests(b):
        nearest = jnp.int32(room)
        chain[room] = nearest
        chain[room + 1] = nearest
        for n in reversed(range(room)):
            nearest = jnp.where(active(b, *row_of(first_guest, n)) > 0, n, nearest)
            chain[n] = nearest
        for k in range(room):
            queue[b, k] = jnp.minimum(nearest, room - 1)
            nearest = chain[nearest + 1]
        queue[b, room] = room - 1

    def fill(j, base, slots, taken):
        for q in slots:
            used = active(0, *row_of(j, q))
            visitor = guests[queue[0, taken]]
            stage[base + q] = jnp.where(used > 0, mine[j, q], visitor)
            taken = jnp.minimum(taken + 1 - used, room)
        return taken

    need_rows(0)
    list_guests(0)
    own(1).wait()
    for i in range(GUEST):
        own_guest(i).wait()
    taken = fill(1, -WIDE, range(WIDE, pair_slots), jnp.int32(0))
    own(pairs).wait()
    across_second.start()
    taken = fill(pairs, host(1), range(pair_slots), taken)

    own(2).wait()
    taken = fill(2, host(2), range(pair_slots), taken)
    across_last.start()

    def prepare(j, taken):
        own(j).wait()
        taken = fill(j, host(j), range(pair_slots), taken)
        across(j - 1).start()
        return taken

    taken = lax.fori_loop(3, shared, prepare, taken)

    deeper = hub & (z < depth - 1)
    further = hub & (z == 0) & (r + 2 < rows_across)

    @pl.when(hub)
    def _():
        pl.semaphore_wait(barrier, 1 + jnp.where(deeper, 1, 0) + jnp.where(further, 1, 0))

    @pl.when(hub & (z > 0))
    def _():
        greet(barrier, {"depth": z - 1})

    @pl.when(hub & (z == 0) & (r > 0))
    def _():
        greet(barrier, {"row": r - 2})

    @pl.when(jnp.logical_not(hub & (z == 0) & (r == 0)))
    def _():
        pl.semaphore_wait(go, 1)

    @pl.when(deeper)
    def _():
        greet(go, {"depth": z + 1})

    @pl.when(further)
    def _():
        greet(go, {"row": r + 2})

    @pl.when(hub)
    def _():
        greet(go, peer)
        greet(go, fellow)
        greet(go, {"row": r + 1, "col": 1 - me})

    fellow_pattern.start()
    for i in range(GUEST):
        fellow_guest(i).start()
    own_flags.wait()
    for side in (0, 1):
        flag_hop(side, 1).start()
        edge(side).start()

    fellow_pattern.wait_recv()
    fellow_bits = pltpu.make_async_copy(fellow_flags, bits.at[1], bits_sem)
    fellow_bits.start()
    own_used, own_free, own_lend = tally(0)
    excess[0] = jnp.maximum(own_used - own_free, 0)
    spare[0] = own_lend
    fellow_bits.wait()
    need_rows(1)
    list_guests(1)
    fellow_used, fellow_free, _ = tally(1)
    for i in range(GUEST):
        fellow_guest(i).wait_recv()

    def prepare_shared(j, carry):
        taken, lent = carry
        own(j).wait()
        base = host(j)
        for q in range(pair_slots):
            used = active(0, *row_of(j, q))
            ours = taken < own_used
            visitor = jnp.where(
                ours, guests[queue[0, jnp.minimum(taken, room)]],
                fellows[queue[1, jnp.minimum(fellow_free + lent, room)]])
            stage[base + q] = jnp.where(used > 0, mine[j, q], visitor)
            taken = taken + 1 - used
            lent = lent + jnp.where(ours, 0, 1 - used)
        across(j - 1).start()
        return taken, lent

    taken, _ = lax.fori_loop(shared, tail, prepare_shared, (taken, jnp.int32(0)))
    own(tail).wait()
    fill(tail, host(tail), range(WIDE), jnp.minimum(taken, room))
    across(tail - 1).start()

    @pl.loop(tail + 1, pairs)
    def _(j):
        own(j).wait()

    def scan(j, base, slots, free):
        for q in reversed(slots):
            free = jnp.where(active(0, *row_of(j, q)) > 0, free, base + q)
            chain[base + q] = free
        return free

    def scan_pair(i, free):
        j = tail - 1 - i
        return scan(j, host(j), range(pair_slots), free)

    free = jnp.int32(hosts)
    chain[hosts] = free
    chain[hosts + 1] = free
    free = scan(tail, host(tail), range(WIDE), free)
    free = lax.fori_loop(0, tail - 2, scan_pair, free)
    free = scan(pairs, host(1), range(pair_slots), free)
    free = scan(1, -WIDE, range(WIDE, pair_slots), free)
    across_half.start()
    across_extra.start()
    across_end.start()
    for k in range(room):
        spot[0, k] = jnp.minimum(free, hosts - 1)
        free = chain[free + 1]

    common = passed.shape[0]

    def scan_fellow(i, carry):
        nearest, above = carry
        j = tail - 1 - i
        for q in reversed(range(pair_slots)):
            hole = 1 - active(1, *row_of(j, q))
            above = above + hole
            lends = (hole > 0) & (fellow_free - above >= fellow_used)
            at = (j - shared) * pair_slots + q
            nearest = jnp.where(lends, at, nearest)
            chain[at] = nearest
        return nearest, above

    nearest = jnp.int32(common)
    chain[common] = nearest
    chain[common + 1] = nearest
    nearest, _ = lax.fori_loop(0, tail - shared, scan_fellow, (nearest, holes(1, 2 * tail - 2)))
    for k in range(room):
        spot[1, k] = jnp.minimum(nearest, common - 1)
        nearest = chain[nearest + 1]
    rank = jnp.int32(0)
    for n in range(room):
        place_own[n] = spot[0, jnp.minimum(rank, room - 1)]
        place_fellow[n] = spot[1, jnp.clip(rank - own_free, 0, room - 1)]
        from_fellow[n] = jnp.where(rank >= own_free, 1, 0)
        rank = rank + active(0, *row_of(first_guest, n))

    def absorb(k):
        fetch = pltpu.make_async_copy(flags.at[k], bits.at[2], bits_sem)
        fetch.start()
        fetch.wait()
        need_rows(2)
        used, free, lend = tally(2)
        excess[k] = jnp.maximum(used - free, 0)
        spare[k] = lend

    def expand(which, i, j):
        lane = lax.broadcasted_iota(jnp.int32, flags.shape[1:], 1)
        for p in range(2):
            picked = jnp.where(lane == i + p, flags[which], 0).astype(jnp.float32)
            spread = jnp.broadcast_to(jnp.sum(picked, axis=1, keepdims=True), (WIDE, block))
            for s in range(WIDE):
                masks[j, p:p + 1, (p + s) * block:(p + s + 1) * block] = spread[s:s + 1]
            empty = slice(0, block) if p else slice(WIDE * block, SLOTS * block)
            masks[j, p:p + 1, empty] = jnp.zeros((1, block), jnp.float32)

    def convert(j, other, halves=(0, 1)):
        for p in halves:
            for s in range(WIDE):
                slot = p + s
                lanes = slice(slot * block, (slot + 1) * block)
                factor = masks[j, p:p + 1, lanes]
                for c, value in ((me, mine[j, p * WIDE + s]), (1 - me, other(p * WIDE + s))):
                    a, b = split(value * factor)
                    at = pl.ds(pl.multiple_of(p * block + c * h, h), h)
                    high[j, at, lanes] = a
                    low[j, at, lanes] = b
            empty = slice(0, block) if p else slice(WIDE * block, SLOTS * block)
            nothing = jnp.zeros((block, block), jnp.bfloat16)
            high[j, p * block:(p + 1) * block, empty] = nothing
            low[j, p * block:(p + 1) * block, empty] = nothing

    def arrived(j):
        return lambda q: hosted[host(j) + q]

    def direct(i):
        return lambda q: theirs[i, q]

    def visiting(j):
        def block_at(q):
            n = (j - first_guest) * pair_slots + q
            if n >= room:
                return theirs[4, q]
            return jnp.where(from_fellow[n] > 0, passed[place_fellow[n]], hosted[place_own[n]])

        return block_at

    product, own_rows, compute = products(block, h, me, masks, high, low, early)

    @pl.loop(1, pairs + 1)
    def _(j):
        expand(0, 2 * (j - 1), j)

    for side in (0, 1):
        flag_hop(side, 1).wait_recv()
    for side in (0, 1):
        if reach[side] > 1:
            flag_hop(side, 2).start()
    expand(1, 2 * (pairs - 1), 0)
    expand(ring - 1, 0, last)

    across_first.wait_recv()
    relay_first.start()
    across_second.wait_recv()
    relay_second.start()
    convert(1, lambda q: theirs[1, q] if q < WIDE else hosted[q - WIDE])
    across_last.wait_recv()
    relay_ahead.start()
    convert(pairs, arrived(1))
    absorb(1)
    absorb(ring - 1)
    edge(0).wait_recv()
    relay_ahead.wait_recv()
    convert(0, direct(0))
    edge(1).wait_recv()
    relay_first.wait_recv()
    relay_second.wait_recv()
    convert(last, direct(2))

    turns = tail - 2
    each = -(-(reach[0] - 1) // turns)

    def pass_on(side, k):
        @pl.when(k <= reach[side])
        def _():
            flag_hop(side, k).wait_recv()

        @pl.when(k + 1 <= reach[side])
        def _():
            flag_hop(side, k + 1).start()

        @pl.when(k <= reach[side])
        def _():
            absorb(k if side == 0 else ring - k)

    @pl.loop(2, tail)
    def _(j):
        across(j).wait_recv()

        @pl.when(j >= shared)
        def _():
            hand_over(j).start()

        convert(j, arrived(j))
        compute(j - 1, j - 2)
        for u in range(each):
            for side in (0, 1):
                pass_on(side, (j - 2) * each + u + 2)

    bad = jnp.int32(0)
    for k in range(ring):
        there = lax.rem(place - k + ring, ring)
        band = there // depth
        partner = there + (1 - 2 * lax.rem(band, 2)) * depth
        bad = bad + jnp.where(excess[k] > spare[lax.rem(place - partner + ring, ring)], 1, 0)
    over[0] = bad

    def local_rows(j):
        parts = []
        for p in range(2):
            blocks = [mine[j, p * WIDE + s] for s in range(WIDE)]
            empty = [jnp.zeros((h, block), jnp.float32)]
            row = jnp.concatenate(empty + blocks if p else blocks + empty, axis=1)
            parts.append(row * masks[j, p:p + 1, :])
        return split(jnp.concatenate(parts, axis=0))

    def converted_rows(j):
        return own_rows(high, j), own_rows(low, j)

    begun[0] = product(tail - 1, *converted_rows(tail - 1), BEFORE[0])
    begun[1] = product(tail, *local_rows(tail), (0,))
    ahead[0] = product(pairs - 1, *local_rows(pairs - 1), (2,))
    ahead[1] = product(pairs, *converted_rows(pairs), (1, 2))

    for j in range(shared, tail):
        hand_over(j).wait_recv()
    across_half.wait_recv()
    for j in range(first_guest, pairs - 1):
        convert(j, visiting(j))
    convert(tail, arrived(tail), (0,))
    begun[1] = product(tail, *local_rows(tail), (2,), begun[1])
    across_extra.wait_recv()
    convert(pairs - 1, visiting(pairs - 1))
    for j in range(first_guest + 1, pairs - 1):
        compute(j, j - LATE - 1)
    begun[2] = product(first_guest, *converted_rows(first_guest), BEFORE[2])
    compute(pairs - 1, pairs - LATE - 2, (0, 1), ahead[0])
    compute(pairs, pairs - LATE - 1, (0,), ahead[1])

    fellow_pattern.wait_send()
    for i in range(GUEST):
        fellow_guest(i).wait_send()
    for j in range(shared, tail):
        hand_over(j).wait_send()
    for side in (0, 1):
        edge(side).wait_send()

        @pl.loop(1, reach[side] + 1)
        def _(k):
            flag_hop(side, k).wait_send()

    relay_ahead.wait_send()
    relay_first.wait_send()
    relay_second.wait_send()

    across_end.wait_recv()
    convert(tail, direct(3), (1,))
    across_first.wait_send()
    across_second.wait_send()
    across_last.wait_send()
    across_half.wait_send()
    across_extra.wait_send()
    across_end.wait_send()

    @pl.loop(2, tail)
    def _(j):
        across(j).wait_send()


class Patched:
    def __init__(self, ref, fixed, first):
        self.ref, self.fixed, self.first = ref, fixed, first

    def __getitem__(self, at):
        j = at[0] - self.first
        if 0 <= j < self.fixed.shape[0]:
            return self.fixed[(j,) + tuple(at[1:])]
        return self.ref[at]


def top_up_kernel(dens, got, send_sem, recv_sem):
    first = dens.shape[0] - 1 - GUEST
    peer = {"col": 1 - lax.axis_index("col")}
    barrier = pltpu.get_barrier_semaphore()
    pl.semaphore_signal(barrier, inc=1, device_id=peer, device_id_type=MESH)
    pl.semaphore_wait(barrier, 1)

    def across(i):
        return pltpu.make_async_remote_copy(
            dens.at[first + i], got.at[i], send_sem.at[i], recv_sem.at[i],
            device_id=peer, device_id_type=MESH)

    for i in range(GUEST):
        across(i).start()
    for i in range(GUEST):
        across(i).wait()


def finish_again(first_late, masks, high, low, early, begun, got, out,
                 late, fixed_high, fixed_low, early_sem, late_sem):
    h, block = early.shape[3], early.shape[4]
    me = lax.axis_index("col")
    before = first_late - 1
    count = late.shape[0]
    first = pltpu.make_async_copy(early.at[pl.ds(0, before)], out.at[pl.ds(0, before)], early_sem)
    first.start()
    first_guest = first_late + count - 1 - GUEST
    fixed_high[...] = high[pl.ds(first_guest, GUEST)]
    fixed_low[...] = low[pl.ds(first_guest, GUEST)]
    for i in range(GUEST):
        for q in range(2 * WIDE):
            p, s = divmod(q, WIDE)
            lanes = slice((p + s) * block, (p + s + 1) * block)
            a, b = split(got[i, q] * masks[first_guest + i, p:p + 1, lanes])
            at = pl.ds(pl.multiple_of(p * block + (1 - me) * h, h), h)
            fixed_high[i, at, lanes] = a
            fixed_low[i, at, lanes] = b
    _, _, compute = products(block, h, me, masks, Patched(high, fixed_high, first_guest),
                             Patched(low, fixed_low, first_guest), late)

    def result(i):
        return pltpu.make_async_copy(late.at[i], out.at[before + i], late_sem.at[i])

    for i in range(count):
        compute(first_late + i, i)
        result(i).start()
    first.wait()

    @pl.loop(0, count)
    def _(i):
        result(i).wait()


DMA = pltpu.SemaphoreType.DMA
IN_VMEM = pl.BlockSpec(memory_space=pltpu.VMEM)


def results(pairs, wide, h, block):
    width = SLOTS * block
    return [
        pltpu.VMEM((pairs + 2, 8, width), jnp.float32),
        pltpu.VMEM((pairs + 2, 2 * block, width), jnp.bfloat16),
        pltpu.VMEM((pairs + 2, 2 * block, width), jnp.bfloat16),
        pltpu.VMEM((pairs - LATE, 2, wide, h, block), jnp.float32),
        pltpu.VMEM((LATE, 2 * h, width), jnp.float32),
    ]


def in_hbm(*arrays):
    return (pltpu.with_memory_space_constraint(x, pltpu.HBM) for x in arrays)


def finished(first_late, held, pairs, wide, h, block):
    return pl.pallas_call(
        functools.partial(finish, first_late),
        out_shape=pltpu.HBM((pairs, 2, wide, h, block), jnp.float32),
        in_specs=[IN_VMEM] * 5,
        out_specs=pl.BlockSpec(memory_space=pltpu.HBM),
        scratch_shapes=[
            pltpu.VMEM((LATE, 2, wide, h, block), jnp.float32),
            DMA((2,)),
            DMA((LATE,)),
        ],
        compiler_params=pltpu.CompilerParams(vmem_limit_bytes=16 << 20),
    )(*held)


def dense(cols, ring, density, pattern):
    rows, wide, h, block = density.shape
    pairs = rows // 2
    paired = density.reshape(pairs, 2, wide, h, block)
    held = pl.pallas_call(
        functools.partial(dense_kernel, cols, ring),
        out_shape=results(pairs, wide, h, block),
        in_specs=[pl.BlockSpec(memory_space=pltpu.HBM)] * 2,
        out_specs=[IN_VMEM] * 5,
        scratch_shapes=[
            pltpu.VMEM((cols, pairs + 2, 2, wide, h, block), jnp.float32),
            pltpu.VMEM((3, wide, rows), jnp.int32),
            DMA((pairs,)),
            DMA,
            DMA((cols - 1, pairs)),
            DMA((cols - 1, pairs)),
            DMA((2,)),
            DMA((2,)),
            DMA((2, cols - 1)),
            DMA((2, cols - 1)),
            DMA((2,)),
            DMA((2,)),
            pltpu.SemaphoreType.REGULAR,
            pltpu.SemaphoreType.REGULAR,
            pltpu.SemaphoreType.REGULAR,
        ],
        compiler_params=pltpu.CompilerParams(
            collective_id=0, has_side_effects=True, vmem_limit_bytes=42 << 20),
    )(*in_hbm(paired, pattern.T))
    out = finished(pairs - LATE + 1, held, pairs, wide, h, block)
    return out.reshape(density.shape)


def sparse(ring, density, pattern):
    rows, wide, h, block = density.shape
    pairs = rows // 2
    paired = density.reshape(pairs, 2 * wide, h, block)
    tail = pairs - GUEST - 1
    hosts = tail * 2 * wide
    entries = GUEST * 2 * wide
    room = entries - EXTRA
    common = SHARED * 2 * wide
    scalars = pltpu.SMEM
    *held, over = pl.pallas_call(
        functools.partial(sparse_kernel, ring, lax.axis_size("row")),
        out_shape=results(pairs, wide, h, block) + [jax.ShapeDtypeStruct((1,), jnp.int32)],
        in_specs=[pl.BlockSpec(memory_space=pltpu.HBM)] * 2,
        out_specs=[IN_VMEM] * 5 + [pl.BlockSpec(memory_space=pltpu.SMEM)],
        scratch_shapes=[
            pltpu.VMEM((pairs + 2, 2 * wide, h, block), jnp.float32),
            pltpu.VMEM((5, 2 * wide, h, block), jnp.float32),
            pltpu.VMEM((hosts, h, block), jnp.float32),
            pltpu.VMEM((hosts, h, block), jnp.float32),
            pltpu.VMEM((common, h, block), jnp.float32),
            pltpu.VMEM((entries, h, block), jnp.float32),
            pltpu.VMEM((entries, h, block), jnp.float32),
            pltpu.VMEM((ring, wide, rows), jnp.int32),
            pltpu.VMEM((wide, rows), jnp.int32),
            scalars((3, wide, rows), jnp.int32),
            scalars((rows,), jnp.int32),
            scalars((3, rows), jnp.int32),
            scalars((hosts + 2,), jnp.int32),
            scalars((2, room + 1), jnp.int32),
            scalars((2, room), jnp.int32),
            scalars((room,), jnp.int32),
            scalars((room,), jnp.int32),
            scalars((room,), jnp.int32),
            scalars((ring,), jnp.int32),
            scalars((ring,), jnp.int32),
            pltpu.VMEM((2, 2 * h, SLOTS * block), jnp.float32),
            DMA((pairs,)),
            DMA((GUEST,)),
            DMA,
            DMA,
            DMA((tail + 4,)),
            DMA((tail + 4,)),
            DMA((2,)),
            DMA((2,)),
            DMA((3,)),
            DMA((3,)),
            DMA((2, ring // 2)),
            DMA((2, ring // 2)),
            DMA((GUEST + 1,)),
            DMA((GUEST + 1,)),
            DMA((SHARED,)),
            DMA((SHARED,)),
            pltpu.SemaphoreType.REGULAR,
            pltpu.SemaphoreType.REGULAR,
        ],
        compiler_params=pltpu.CompilerParams(
            collective_id=1, has_side_effects=True, vmem_limit_bytes=40 << 20),
    )(*in_hbm(paired, pattern.T))

    def done(paired, *held):
        return finished(tail - 1, held, pairs, wide, h, block)

    def again(paired, *held):
        got = pl.pallas_call(
            top_up_kernel,
            out_shape=pltpu.VMEM((GUEST, 2 * wide, h, block), jnp.float32),
            in_specs=[pl.BlockSpec(memory_space=pltpu.HBM)],
            out_specs=IN_VMEM,
            scratch_shapes=[DMA((GUEST,)), DMA((GUEST,))],
            compiler_params=pltpu.CompilerParams(
                collective_id=0, has_side_effects=True, vmem_limit_bytes=8 << 20),
        )(*in_hbm(paired))
        count = pairs - tail + 2
        return pl.pallas_call(
            functools.partial(finish_again, tail - 1),
            out_shape=pltpu.HBM((pairs, 2, wide, h, block), jnp.float32),
            in_specs=[IN_VMEM] * 6,
            out_specs=pl.BlockSpec(memory_space=pltpu.HBM),
            scratch_shapes=[
                pltpu.VMEM((count, 2, wide, h, block), jnp.float32),
                pltpu.VMEM((GUEST, 2 * block, SLOTS * block), jnp.bfloat16),
                pltpu.VMEM((GUEST, 2 * block, SLOTS * block), jnp.bfloat16),
                DMA,
                DMA((count,)),
            ],
            compiler_params=pltpu.CompilerParams(vmem_limit_bytes=20 << 20),
        )(*held, got)

    return lax.cond(over[0] > 0, again, done, paired, *held).reshape(density.shape)


def shards(cols, ring, density, pattern):
    if cols == 2 and lax.axis_size("row") % 2 == 0 and density.shape[0] >= 32:
        return sparse(ring, density, pattern)
    return dense(cols, ring, density, pattern)


def solution(mesh):
    cols = mesh.shape["col"]
    ring = mesh.shape["row"] * mesh.shape["depth"]
    in_specs = (P(RING, None, "col", None), P(RING, None))
    out_specs = P(RING, None, "col", None)
    body = functools.partial(shards, cols, ring)
    return jax.shard_map(body, mesh=mesh, in_specs=in_specs, out_specs=out_specs, check_vma=False)
```

```python
import functools

import jax
import jax.numpy as jnp
from jax import lax
from jax.experimental import pallas as pl
from jax.experimental.pallas import tpu as pltpu
from jax.sharding import PartitionSpec as P

MESH = pl.DeviceIdType.MESH
WIDE = 5
SLOTS = 6
RING = ("row", "depth")


def split(value):
    high = value.astype(jnp.bfloat16)
    low = (value - high.astype(jnp.float32)).astype(jnp.bfloat16)
    return high, low


def dot(a, b):
    return jnp.dot(a, b, preferred_element_type=jnp.float32)


def products(block, h, me, masks, high, low, out):
    two = 2 * block

    def product(j, a, b, sources=(0, 1, 2), start=None):
        both = jnp.concatenate([a, b], axis=0)
        m = a.shape[0]
        parts = []
        for n in range(3):
            total = None if start is None else start[:, n * two:(n + 1) * two]
            for k in sources:
                at = n - k + 1
                if at < 0 or at > 2:
                    continue
                lanes = slice(at * two, (at + 1) * two)
                ks = slice(k * two, (k + 1) * two)
                stacked = dot(both[:, ks], high[j + k - 1, :, lanes])
                term = stacked[:m] + stacked[m:] + dot(a[:, ks], low[j + k - 1, :, lanes])
                total = term if total is None else total + term
            parts.append(jnp.zeros((m, two), jnp.float32) if total is None else total)
        return jnp.concatenate(parts, axis=1)

    def own_rows(ref, j):
        return jnp.concatenate(
            [ref[j, pl.ds(pl.multiple_of(p * block + me * h, h), h), :] for p in range(2)], axis=0)

    def compute(j, to, sources=(0, 1, 2), start=None):
        factor = jnp.concatenate(
            [jnp.broadcast_to(masks[j, p:p + 1, :], (h, SLOTS * block)) for p in range(2)], axis=0)
        square = product(j, own_rows(high, j), own_rows(low, j), sources, start) * factor
        cube = product(j, *split(square)) * factor
        value = 3.0 * square - 2.0 * cube
        for p in range(2):
            for s in range(WIDE):
                out[to, p, s] = value[p * h:(p + 1) * h, (p + s) * block:(p + s + 1) * block]

    return product, own_rows, compute


BEFORE = ((0, 1), (0, 2), (1, 2))
AFTER = ((2,), (1,), (0,))
LATE = 3


def finish(first_late, masks, high, low, early, begun, out, late, early_sem, late_sem):
    h, block = early.shape[3], early.shape[4]
    me = lax.axis_index("col")
    before = first_late - 1
    after = early.shape[0] - before
    firsts = [pltpu.make_async_copy(early.at[pl.ds(0, before)], out.at[pl.ds(0, before)], early_sem.at[0])]
    if after:
        firsts.append(pltpu.make_async_copy(
            early.at[pl.ds(before, after)], out.at[pl.ds(before + LATE, after)], early_sem.at[1]))
    for first in firsts:
        first.start()
    _, _, compute = products(block, h, me, masks, high, low, late)

    def result(i):
        return pltpu.make_async_copy(late.at[i], out.at[before + i], late_sem.at[i])

    for i in range(LATE):
        compute(first_late + i, i, AFTER[i], begun[i])
        result(i).start()

    for first in firsts:
        first.wait()

    @pl.loop(0, LATE)
    def _(i):
        result(i).wait()


def dense_kernel(cols, ring, dens, pattern, masks, high, low, early, begun, raw, flags,
           local_sem, flag_sem, send_sem, recv_sem, edge_send, edge_recv,
           relay_send, relay_recv, flag_send, flag_recv, up, down, corner):
    pairs = dens.shape[0]
    h = dens.shape[3]
    block = dens.shape[4]
    last = pairs + 1
    me = lax.axis_index("col")
    depth = lax.axis_size("depth")
    place = lax.axis_index("row") * depth + lax.axis_index("depth")

    def on_ring(shift):
        at = lax.rem(place + shift + ring, ring)
        return {"row": at // depth, "depth": lax.rem(at, depth)}

    prev, following = on_ring(-1), on_ring(1)

    def peer(step):
        return {"col": lax.rem(me + step, cols)}

    def source(step):
        return lax.rem(me + cols - step, cols)

    def own(j):
        return pltpu.make_async_copy(dens.at[j - 1], raw.at[me, j], local_sem.at[j - 1])

    def across(step, j):
        return pltpu.make_async_remote_copy(
            dens.at[j - 1], raw.at[me, j], send_sem.at[step - 1, j - 1],
            recv_sem.at[step - 1, j - 1], device_id=peer(step), device_id_type=MESH)

    ends = ((pairs, 0, following), (1, last, prev))

    def edge(side):
        j, slot, device = ends[side]
        return pltpu.make_async_remote_copy(
            dens.at[j - 1], raw.at[me, slot], edge_send.at[side], edge_recv.at[side],
            device_id=device, device_id_type=MESH)

    def relay(side, step):
        j, slot, device = ends[side]
        return pltpu.make_async_remote_copy(
            raw.at[source(step), j], raw.at[source(step), slot], relay_send.at[side, step - 1],
            relay_recv.at[side, step - 1], device_id=device, device_id_type=MESH)

    def flag_edge(side):
        return pltpu.make_async_remote_copy(
            pattern, flags.at[2 * side], flag_send.at[side], flag_recv.at[side],
            device_id=ends[side][2], device_id_type=MESH)

    steps = range(1, cols)

    z, r = lax.axis_index("depth"), lax.axis_index("row")
    row_count = lax.axis_size("row")

    def greet(semaphore, device):
        pl.semaphore_signal(semaphore, inc=1, device_id=device, device_id_type=MESH)

    def along(step):
        return {"depth": z + step}

    def beside(step):
        return {"row": lax.rem(r + step + row_count, row_count)}

    barrier = pltpu.get_barrier_semaphore()
    for s in steps:
        greet(barrier, peer(s))

    @pl.when(z > 0)
    def _():
        greet(barrier, along(-1))

    @pl.when(z < depth - 1)
    def _():
        greet(barrier, along(1))

    @pl.when(z == 0)
    def _():
        greet(barrier, beside(-1))
        greet(barrier, beside(1))

    own_flags = pltpu.make_async_copy(pattern, flags.at[1], flag_sem)
    own_flags.start()
    near = jnp.where(z == 0, 2, 1) + jnp.where(z < depth - 1, 1, 0)
    pl.semaphore_wait(barrier, cols - 1 + near)

    for j in (1, pairs):
        for s in steps:
            across(s, j).start()

    @pl.loop(2, pairs)
    def _(j):
        for s in steps:
            across(s, j).start()

    @pl.when(z > 0)
    def _():
        pl.semaphore_wait(up, 1)

    @pl.when(z < depth - 1)
    def _():
        greet(up, along(1))

    @pl.when(z < depth - 2)
    def _():
        pl.semaphore_wait(down, 1)

    @pl.when((z > 0) & (z <= depth - 2))
    def _():
        greet(down, along(-1))

    @pl.when(z == 0)
    def _():
        greet(corner, beside(1))
        pl.semaphore_wait(corner, 1)

    for side in (0, 1):
        flag_edge(side).start()
        edge(side).start()

    @pl.loop(1, pairs + 1)
    def _(j):
        own(j).start()

    def expand(which, i, j):
        lane = lax.broadcasted_iota(jnp.int32, flags.shape[1:], 1)
        for p in range(2):
            picked = jnp.where(lane == i + p, flags[which], 0).astype(jnp.float32)
            spread = jnp.broadcast_to(jnp.sum(picked, axis=1, keepdims=True), (WIDE, block))
            for s in range(WIDE):
                masks[j, p:p + 1, (p + s) * block:(p + s + 1) * block] = spread[s:s + 1]
            empty = slice(0, block) if p else slice(WIDE * block, SLOTS * block)
            masks[j, p:p + 1, empty] = jnp.zeros((1, block), jnp.float32)

    def convert(j):
        for p in range(2):
            for s in range(WIDE):
                slot = p + s
                factor = masks[j, p:p + 1, slot * block:(slot + 1) * block]
                for c in range(cols):
                    a, b = split(raw[c, j, p, s] * factor)
                    rows = slice(p * block + c * h, p * block + (c + 1) * h)
                    lanes = slice(slot * block, (slot + 1) * block)
                    high[j, rows, lanes] = a
                    low[j, rows, lanes] = b
            empty = slice(0, block) if p else slice(WIDE * block, SLOTS * block)
            nothing = jnp.zeros((block, block), jnp.bfloat16)
            high[j, p * block:(p + 1) * block, empty] = nothing
            low[j, p * block:(p + 1) * block, empty] = nothing

    product, own_rows, compute = products(block, h, me, masks, high, low, early)

    own_flags.wait()

    @pl.loop(1, pairs + 1)
    def _(j):
        expand(1, 2 * (j - 1), j)

    for side in (0, 1):
        flag_edge(side).wait_recv()
    expand(0, 2 * (pairs - 1), 0)
    expand(2, 0, last)

    @pl.loop(1, pairs + 1)
    def _(j):
        own(j).wait()

    for j, side in ((1, 1), (pairs, 0)):
        for s in steps:
            across(s, j).wait_recv()
            relay(side, s).start()
        convert(j)
    for side in (0, 1):
        edge(side).wait_recv()
        for s in steps:
            relay(side, s).wait_recv()
        convert(ends[side][1])

    @pl.loop(2, pairs - 1)
    def _(j):
        for s in steps:
            across(s, j).wait_recv()
        convert(j)
        compute(j - 1, j - 2)

    def local_rows(j):
        rows = []
        for p in range(2):
            blocks = [raw[me, j, p, s] for s in range(WIDE)]
            empty = [jnp.zeros((h, block), jnp.float32)]
            row = jnp.concatenate(empty + blocks if p else blocks + empty, axis=1)
            rows.append(row * masks[j, p:p + 1, :])
        return split(jnp.concatenate(rows, axis=0))

    for i in range(LATE):
        j = pairs - LATE + 1 + i
        a, b = local_rows(j) if i == 1 else (own_rows(high, j), own_rows(low, j))
        begun[i] = product(j, a, b, BEFORE[i])

    for side in (0, 1):
        flag_edge(side).wait_send()
        edge(side).wait_send()
        for s in steps:
            relay(side, s).wait_send()
    for s in steps:
        across(s, pairs - 1).wait_recv()
    convert(pairs - 1)

    @pl.loop(1, pairs + 1)
    def _(j):
        for s in steps:
            across(s, j).wait_send()


EXTRA = 2
GUEST = 3
SHARED = 6


def sparse_kernel(ring, rows_across, dens, pattern, masks, high, low, early, begun, over,
                  mine, theirs, stage, hosted, passed, guests, fellows, flags, fellow_flags,
                  bits, word, need, chain, queue, spot, place_own, place_fellow, from_fellow, excess, spare, ahead,
                  local_sem, guest_sem, flag_sem, bits_sem, send_sem, recv_sem, edge_send, edge_recv,
                  relay_send, relay_recv, flag_send, flag_recv, fellow_send, fellow_recv,
                  pass_send, pass_recv, ready, go):
    pairs, pair_slots, h, block = dens.shape
    rows = 2 * pairs
    last = pairs + 1
    first_guest = pairs - GUEST
    tail = first_guest - 1
    shared = tail - SHARED
    room = guests.shape[0] - EXTRA
    hosts = hosted.shape[0]
    me = lax.axis_index("col")
    depth = lax.axis_size("depth")
    z, r = lax.axis_index("depth"), lax.axis_index("row")
    place = r * depth + z

    def on_ring(shift):
        at = lax.rem(place + shift + ring, ring)
        return {"row": at // depth, "depth": lax.rem(at, depth)}

    prev, following = on_ring(-1), on_ring(1)
    peer = {"col": 1 - me}
    fellow = {"row": r + 1 - 2 * lax.rem(r, 2)}

    def remote(source, target, send, recv, device):
        return pltpu.make_async_remote_copy(
            source, target, send, recv, device_id=device, device_id_type=MESH)

    def own(j):
        return pltpu.make_async_copy(dens.at[j - 1], mine.at[j], local_sem.at[j - 1])

    def guest_pair(i):
        return pl.ds(i * pair_slots, pair_slots)

    def own_guest(i):
        return pltpu.make_async_copy(
            dens.at[first_guest - 1 + i], guests.at[guest_pair(i)], guest_sem.at[i])

    def fellow_guest(i):
        return remote(dens.at[first_guest - 1 + i], fellows.at[guest_pair(i)],
                      fellow_send.at[i], fellow_recv.at[i], fellow)

    fellow_pattern = remote(pattern, fellow_flags, fellow_send.at[GUEST], fellow_recv.at[GUEST], fellow)

    def host(j):
        return j * pair_slots - WIDE

    def crossing(source, target, n):
        return remote(source, target, send_sem.at[n], recv_sem.at[n], peer)

    def staged(start, size, n):
        return crossing(stage.at[pl.ds(start, size)], hosted.at[pl.ds(start, size)], n)

    def across(j):
        return staged(host(j), pair_slots, j)

    across_first = crossing(dens.at[0, pl.ds(0, WIDE)], theirs.at[1, pl.ds(0, WIDE)], 0)
    across_second = staged(0, WIDE, tail + 1)
    across_last = staged(host(1), pair_slots, 1)
    across_half = staged(host(tail), WIDE, tail)
    extra_at = pl.ds(pair_slots - EXTRA, EXTRA)
    across_extra = crossing(dens.at[pairs - 2, extra_at], theirs.at[4, extra_at], tail + 2)
    across_end = crossing(
        dens.at[tail - 1, pl.ds(WIDE, WIDE)], theirs.at[3, pl.ds(WIDE, WIDE)], tail + 3)

    ends = ((pairs, 0, following), (1, last, prev))
    halo = (0, 2)

    def edge(side):
        j, slot, device = ends[side]
        return remote(dens.at[j - 1], mine.at[slot], edge_send.at[side], edge_recv.at[side], device)

    relay_ahead = remote(hosted.at[pl.ds(host(1), pair_slots)], theirs.at[0],
                         relay_send.at[0], relay_recv.at[0], following)
    relay_first = remote(theirs.at[1, pl.ds(0, WIDE)], theirs.at[2, pl.ds(0, WIDE)],
                         relay_send.at[1], relay_recv.at[1], prev)
    relay_second = remote(hosted.at[pl.ds(0, WIDE)], theirs.at[2, pl.ds(WIDE, WIDE)],
                          relay_send.at[2], relay_recv.at[2], prev)

    def hand_over(j):
        at = pl.ds((j - shared) * pair_slots, pair_slots)
        return remote(hosted.at[pl.ds(host(j), pair_slots)], passed.at[at],
                      pass_send.at[j - shared], pass_recv.at[j - shared], fellow)

    reach = (ring // 2, ring - 1 - ring // 2)

    def flag_hop(side, k):
        source = k - 1 if side == 0 else lax.rem(ring - k + 1, ring)
        target = k if side == 0 else ring - k
        return remote(flags.at[source], flags.at[target],
                      flag_send.at[side, k - 1], flag_recv.at[side, k - 1], ends[side][2])

    def greet(semaphore, device):
        pl.semaphore_signal(semaphore, inc=1, device_id=device, device_id_type=MESH)

    core = lax.rem(r, 2)
    hub = (me == 0) & (core == 0)
    barrier = pltpu.get_barrier_semaphore()

    @pl.when(hub | (core == 1))
    def _():
        greet(barrier, peer)

    own_bits = pltpu.make_async_copy(pattern, bits.at[0], bits_sem)
    own_bits.start()
    own_flags = pltpu.make_async_copy(pattern, flags.at[0], flag_sem)
    own_flags.start()
    own(1).start()
    for i in range(GUEST):
        own_guest(i).start()
    own(pairs).start()

    @pl.loop(2, pairs)
    def _(j):
        own(j).start()

    @pl.when((me == 1) | (core == 1))
    def _():
        pl.semaphore_wait(barrier, 1)

    @pl.when((me == 1) & (core == 0))
    def _():
        greet(ready, peer)

    @pl.when(hub)
    def _():
        pl.semaphore_wait(ready, 1)

    across_first.start()

    @pl.when((me == 0) & (core == 1))
    def _():
        greet(barrier, fellow)

    own_bits.wait()

    def need_rows(b):
        def pack(row, _):
            value = bits[b, 0, row]
            for s in range(1, WIDE):
                value = value | (bits[b, s, row] << s)
            word[row] = value
            return 0

        lax.fori_loop(0, rows, pack, 0, unroll=4)
        for row in (0, 1, rows - 2, rows - 1):
            need[b, row] = word[row]

        def keep(row, _):
            used = jnp.int32(0)
            for d in range(-2, 3):
                value = word[row + d]
                moved = value << d if d >= 0 else value >> -d
                used = used | (moved & -((value >> (2 - d)) & 1))
            need[b, row] = word[row] & used
            return 0

        lax.fori_loop(2, rows - 2, keep, 0, unroll=4)

    def active(b, row, s):
        return (need[b, row] >> s) & 1

    def row_of(j, q):
        return 2 * (j - 1) + q // WIDE, q % WIDE

    def count(value):
        total = value & 1
        for s in range(1, WIDE):
            total = total + ((value >> s) & 1)
        return total

    def holes(b, row):
        return WIDE - count(need[b, row])

    def tally(b):
        free = holes(b, rows - 2) + holes(b, rows - 1)
        free = lax.fori_loop(1, 2 * shared - 2, lambda row, n: n + holes(b, row), free)
        common = lax.fori_loop(2 * shared - 2, 2 * tail - 2, lambda row, n: n + holes(b, row), jnp.int32(0))
        end = holes(b, 2 * tail - 2)
        free = free + common + end
        start = 2 * first_guest - 2
        full, part = room // WIDE, room % WIDE
        used = jnp.int32(0)
        for i in range(full):
            used = used + count(need[b, start + i])
        if part:
            used = used + count(need[b, start + full] & ((1 << part) - 1))
        lend = jnp.minimum(common, jnp.maximum(free - end - used, 0))
        return used, free, lend

    def list_guests(b):
        nearest = jnp.int32(room)
        chain[room] = nearest
        chain[room + 1] = nearest
        for n in reversed(range(room)):
            nearest = jnp.where(active(b, *row_of(first_guest, n)) > 0, n, nearest)
            chain[n] = nearest
        for k in range(room):
            queue[b, k] = jnp.minimum(nearest, room - 1)
            nearest = chain[nearest + 1]
        queue[b, room] = room - 1

    def fill(j, base, slots, taken):
        for q in slots:
            used = active(0, *row_of(j, q))
            visitor = guests[queue[0, taken]]
            stage[base + q] = jnp.where(used > 0, mine[j, q], visitor)
            taken = jnp.minimum(taken + 1 - used, room)
        return taken

    need_rows(0)
    list_guests(0)
    own(1).wait()
    for i in range(GUEST):
        own_guest(i).wait()
    taken = fill(1, -WIDE, range(WIDE, pair_slots), jnp.int32(0))
    own(pairs).wait()
    across_second.start()
    taken = fill(pairs, host(1), range(pair_slots), taken)

    own(2).wait()
    taken = fill(2, host(2), range(pair_slots), taken)
    across_last.start()

    def prepare(j, taken):
        own(j).wait()
        taken = fill(j, host(j), range(pair_slots), taken)
        across(j - 1).start()
        return taken

    taken = lax.fori_loop(3, shared, prepare, taken)

    deeper = hub & (z < depth - 1)
    further = hub & (z == 0) & (r + 2 < rows_across)

    @pl.when(hub)
    def _():
        pl.semaphore_wait(barrier, 1 + jnp.where(deeper, 1, 0) + jnp.where(further, 1, 0))

    @pl.when(hub & (z > 0))
    def _():
        greet(barrier, {"depth": z - 1})

    @pl.when(hub & (z == 0) & (r > 0))
    def _():
        greet(barrier, {"row": r - 2})

    @pl.when(jnp.logical_not(hub & (z == 0) & (r == 0)))
    def _():
        pl.semaphore_wait(go, 1)

    @pl.when(deeper)
    def _():
        greet(go, {"depth": z + 1})

    @pl.when(further)
    def _():
        greet(go, {"row": r + 2})

    @pl.when(hub)
    def _():
        greet(go, peer)
        greet(go, fellow)
        greet(go, {"row": r + 1, "col": 1 - me})

    fellow_pattern.start()
    for i in range(GUEST):
        fellow_guest(i).start()
    own_flags.wait()
    for side in (0, 1):
        flag_hop(side, 1).start()
        edge(side).start()

    fellow_pattern.wait_recv()
    fellow_bits = pltpu.make_async_copy(fellow_flags, bits.at[1], bits_sem)
    fellow_bits.start()
    own_used, own_free, own_lend = tally(0)
    excess[0] = jnp.maximum(own_used - own_free, 0)
    spare[0] = own_lend
    fellow_bits.wait()
    need_rows(1)
    list_guests(1)
    fellow_used, fellow_free, _ = tally(1)
    for i in range(GUEST):
        fellow_guest(i).wait_recv()

    def prepare_shared(j, carry):
        taken, lent = carry
        own(j).wait()
        base = host(j)
        for q in range(pair_slots):
            used = active(0, *row_of(j, q))
            ours = taken < own_used
            visitor = jnp.where(
                ours, guests[queue[0, jnp.minimum(taken, room)]],
                fellows[queue[1, jnp.minimum(fellow_free + lent, room)]])
            stage[base + q] = jnp.where(used > 0, mine[j, q], visitor)
            taken = taken + 1 - used
            lent = lent + jnp.where(ours, 0, 1 - used)
        across(j - 1).start()
        return taken, lent

    taken, _ = lax.fori_loop(shared, tail, prepare_shared, (taken, jnp.int32(0)))
    own(tail).wait()
    fill(tail, host(tail), range(WIDE), jnp.minimum(taken, room))
    across(tail - 1).start()

    @pl.loop(tail + 1, pairs)
    def _(j):
        own(j).wait()

    def scan(j, base, slots, free):
        for q in reversed(slots):
            free = jnp.where(active(0, *row_of(j, q)) > 0, free, base + q)
            chain[base + q] = free
        return free

    def scan_pair(i, free):
        j = tail - 1 - i
        return scan(j, host(j), range(pair_slots), free)

    free = jnp.int32(hosts)
    chain[hosts] = free
    chain[hosts + 1] = free
    free = scan(tail, host(tail), range(WIDE), free)
    free = lax.fori_loop(0, tail - 2, scan_pair, free)
    free = scan(pairs, host(1), range(pair_slots), free)
    free = scan(1, -WIDE, range(WIDE, pair_slots), free)
    across_half.start()
    across_extra.start()
    across_end.start()
    for k in range(room):
        spot[0, k] = jnp.minimum(free, hosts - 1)
        free = chain[free + 1]

    common = passed.shape[0]

    def scan_fellow(i, carry):
        nearest, above = carry
        j = tail - 1 - i
        for q in reversed(range(pair_slots)):
            hole = 1 - active(1, *row_of(j, q))
            above = above + hole
            lends = (hole > 0) & (fellow_free - above >= fellow_used)
            at = (j - shared) * pair_slots + q
            nearest = jnp.where(lends, at, nearest)
            chain[at] = nearest
        return nearest, above

    nearest = jnp.int32(common)
    chain[common] = nearest
    chain[common + 1] = nearest
    nearest, _ = lax.fori_loop(0, tail - shared, scan_fellow, (nearest, holes(1, 2 * tail - 2)))
    for k in range(room):
        spot[1, k] = jnp.minimum(nearest, common - 1)
        nearest = chain[nearest + 1]
    rank = jnp.int32(0)
    for n in range(room):
        place_own[n] = spot[0, jnp.minimum(rank, room - 1)]
        place_fellow[n] = spot[1, jnp.clip(rank - own_free, 0, room - 1)]
        from_fellow[n] = jnp.where(rank >= own_free, 1, 0)
        rank = rank + active(0, *row_of(first_guest, n))

    def absorb(k):
        fetch = pltpu.make_async_copy(flags.at[k], bits.at[2], bits_sem)
        fetch.start()
        fetch.wait()
        need_rows(2)
        used, free, lend = tally(2)
        excess[k] = jnp.maximum(used - free, 0)
        spare[k] = lend

    def expand(which, i, j):
        lane = lax.broadcasted_iota(jnp.int32, flags.shape[1:], 1)
        for p in range(2):
            picked = jnp.where(lane == i + p, flags[which], 0).astype(jnp.float32)
            spread = jnp.broadcast_to(jnp.sum(picked, axis=1, keepdims=True), (WIDE, block))
            for s in range(WIDE):
                masks[j, p:p + 1, (p + s) * block:(p + s + 1) * block] = spread[s:s + 1]
            empty = slice(0, block) if p else slice(WIDE * block, SLOTS * block)
            masks[j, p:p + 1, empty] = jnp.zeros((1, block), jnp.float32)

    def convert(j, other, halves=(0, 1)):
        for p in halves:
            for s in range(WIDE):
                slot = p + s
                lanes = slice(slot * block, (slot + 1) * block)
                factor = masks[j, p:p + 1, lanes]
                for c, value in ((me, mine[j, p * WIDE + s]), (1 - me, other(p * WIDE + s))):
                    a, b = split(value * factor)
                    at = pl.ds(pl.multiple_of(p * block + c * h, h), h)
                    high[j, at, lanes] = a
                    low[j, at, lanes] = b
            empty = slice(0, block) if p else slice(WIDE * block, SLOTS * block)
            nothing = jnp.zeros((block, block), jnp.bfloat16)
            high[j, p * block:(p + 1) * block, empty] = nothing
            low[j, p * block:(p + 1) * block, empty] = nothing

    def arrived(j):
        return lambda q: hosted[host(j) + q]

    def direct(i):
        return lambda q: theirs[i, q]

    def visiting(j):
        def block_at(q):
            n = (j - first_guest) * pair_slots + q
            if n >= room:
                return theirs[4, q]
            return jnp.where(from_fellow[n] > 0, passed[place_fellow[n]], hosted[place_own[n]])

        return block_at

    product, own_rows, compute = products(block, h, me, masks, high, low, early)

    @pl.loop(1, pairs + 1)
    def _(j):
        expand(0, 2 * (j - 1), j)

    for side in (0, 1):
        flag_hop(side, 1).wait_recv()
    for side in (0, 1):
        if reach[side] > 1:
            flag_hop(side, 2).start()
    expand(1, 2 * (pairs - 1), 0)
    expand(ring - 1, 0, last)

    across_first.wait_recv()
    relay_first.start()
    across_second.wait_recv()
    relay_second.start()
    convert(1, lambda q: theirs[1, q] if q < WIDE else hosted[q - WIDE])
    across_last.wait_recv()
    relay_ahead.start()
    convert(pairs, arrived(1))
    absorb(1)
    absorb(ring - 1)
    edge(0).wait_recv()
    relay_ahead.wait_recv()
    convert(0, direct(0))
    edge(1).wait_recv()
    relay_first.wait_recv()
    relay_second.wait_recv()
    convert(last, direct(2))

    turns = tail - 2
    each = -(-(reach[0] - 1) // turns)

    def pass_on(side, k):
        @pl.when(k <= reach[side])
        def _():
            flag_hop(side, k).wait_recv()

        @pl.when(k + 1 <= reach[side])
        def _():
            flag_hop(side, k + 1).start()

        @pl.when(k <= reach[side])
        def _():
            absorb(k if side == 0 else ring - k)

    @pl.loop(2, tail)
    def _(j):
        across(j).wait_recv()

        @pl.when(j >= shared)
        def _():
            hand_over(j).start()

        convert(j, arrived(j))
        compute(j - 1, j - 2)
        for u in range(each):
            for side in (0, 1):
                pass_on(side, (j - 2) * each + u + 2)

    bad = jnp.int32(0)
    for k in range(ring):
        there = lax.rem(place - k + ring, ring)
        band = there // depth
        partner = there + (1 - 2 * lax.rem(band, 2)) * depth
        bad = bad + jnp.where(excess[k] > spare[lax.rem(place - partner + ring, ring)], 1, 0)
    over[0] = bad

    def local_rows(j):
        parts = []
        for p in range(2):
            blocks = [mine[j, p * WIDE + s] for s in range(WIDE)]
            empty = [jnp.zeros((h, block), jnp.float32)]
            row = jnp.concatenate(empty + blocks if p else blocks + empty, axis=1)
            parts.append(row * masks[j, p:p + 1, :])
        return split(jnp.concatenate(parts, axis=0))

    def converted_rows(j):
        return own_rows(high, j), own_rows(low, j)

    begun[0] = product(tail - 1, *converted_rows(tail - 1), BEFORE[0])
    begun[1] = product(tail, *local_rows(tail), (0,))
    ahead[0] = product(pairs - 1, *local_rows(pairs - 1), (2,))
    ahead[1] = product(pairs, *converted_rows(pairs), (1, 2))

    for j in range(shared, tail):
        hand_over(j).wait_recv()
    across_half.wait_recv()
    for j in range(first_guest, pairs - 1):
        convert(j, visiting(j))
    convert(tail, arrived(tail), (0,))
    begun[1] = product(tail, *local_rows(tail), (2,), begun[1])
    across_extra.wait_recv()
    convert(pairs - 1, visiting(pairs - 1))
    for j in range(first_guest + 1, pairs - 1):
        compute(j, j - LATE - 1)
    begun[2] = product(first_guest, *converted_rows(first_guest), BEFORE[2])
    compute(pairs - 1, pairs - LATE - 2, (0, 1), ahead[0])
    compute(pairs, pairs - LATE - 1, (0,), ahead[1])

    fellow_pattern.wait_send()
    for i in range(GUEST):
        fellow_guest(i).wait_send()
    for j in range(shared, tail):
        hand_over(j).wait_send()
    for side in (0, 1):
        edge(side).wait_send()

        @pl.loop(1, reach[side] + 1)
        def _(k):
            flag_hop(side, k).wait_send()

    relay_ahead.wait_send()
    relay_first.wait_send()
    relay_second.wait_send()

    across_end.wait_recv()
    convert(tail, direct(3), (1,))
    across_first.wait_send()
    across_second.wait_send()
    across_last.wait_send()
    across_half.wait_send()
    across_extra.wait_send()
    across_end.wait_send()

    @pl.loop(2, tail)
    def _(j):
        across(j).wait_send()


class Patched:
    def __init__(self, ref, fixed, first):
        self.ref, self.fixed, self.first = ref, fixed, first

    def __getitem__(self, at):
        j = at[0] - self.first
        if 0 <= j < self.fixed.shape[0]:
            return self.fixed[(j,) + tuple(at[1:])]
        return self.ref[at]


def top_up_kernel(dens, got, send_sem, recv_sem):
    first = dens.shape[0] - 1 - GUEST
    peer = {"col": 1 - lax.axis_index("col")}
    barrier = pltpu.get_barrier_semaphore()
    pl.semaphore_signal(barrier, inc=1, device_id=peer, device_id_type=MESH)
    pl.semaphore_wait(barrier, 1)

    def across(i):
        return pltpu.make_async_remote_copy(
            dens.at[first + i], got.at[i], send_sem.at[i], recv_sem.at[i],
            device_id=peer, device_id_type=MESH)

    for i in range(GUEST):
        across(i).start()
    for i in range(GUEST):
        across(i).wait()


def finish_again(first_late, masks, high, low, early, begun, got, out,
                 late, fixed_high, fixed_low, early_sem, late_sem):
    h, block = early.shape[3], early.shape[4]
    me = lax.axis_index("col")
    before = first_late - 1
    count = late.shape[0]
    first = pltpu.make_async_copy(early.at[pl.ds(0, before)], out.at[pl.ds(0, before)], early_sem)
    first.start()
    first_guest = first_late + count - 1 - GUEST
    fixed_high[...] = high[pl.ds(first_guest, GUEST)]
    fixed_low[...] = low[pl.ds(first_guest, GUEST)]
    for i in range(GUEST):
        for q in range(2 * WIDE):
            p, s = divmod(q, WIDE)
            lanes = slice((p + s) * block, (p + s + 1) * block)
            a, b = split(got[i, q] * masks[first_guest + i, p:p + 1, lanes])
            at = pl.ds(pl.multiple_of(p * block + (1 - me) * h, h), h)
            fixed_high[i, at, lanes] = a
            fixed_low[i, at, lanes] = b
    _, _, compute = products(block, h, me, masks, Patched(high, fixed_high, first_guest),
                             Patched(low, fixed_low, first_guest), late)

    def result(i):
        return pltpu.make_async_copy(late.at[i], out.at[before + i], late_sem.at[i])

    for i in range(count):
        compute(first_late + i, i)
        result(i).start()
    first.wait()

    @pl.loop(0, count)
    def _(i):
        result(i).wait()


DMA = pltpu.SemaphoreType.DMA
IN_VMEM = pl.BlockSpec(memory_space=pltpu.VMEM)


def results(pairs, wide, h, block):
    width = SLOTS * block
    return [
        pltpu.VMEM((pairs + 2, 8, width), jnp.float32),
        pltpu.VMEM((pairs + 2, 2 * block, width), jnp.bfloat16),
        pltpu.VMEM((pairs + 2, 2 * block, width), jnp.bfloat16),
        pltpu.VMEM((pairs - LATE, 2, wide, h, block), jnp.float32),
        pltpu.VMEM((LATE, 2 * h, width), jnp.float32),
    ]


def in_hbm(*arrays):
    return (pltpu.with_memory_space_constraint(x, pltpu.HBM) for x in arrays)


def finished(first_late, held, pairs, wide, h, block):
    return pl.pallas_call(
        functools.partial(finish, first_late),
        out_shape=pltpu.HBM((pairs, 2, wide, h, block), jnp.float32),
        in_specs=[IN_VMEM] * 5,
        out_specs=pl.BlockSpec(memory_space=pltpu.HBM),
        scratch_shapes=[
            pltpu.VMEM((LATE, 2, wide, h, block), jnp.float32),
            DMA((2,)),
            DMA((LATE,)),
        ],
        compiler_params=pltpu.CompilerParams(vmem_limit_bytes=16 << 20),
    )(*held)


def dense(cols, ring, density, pattern):
    rows, wide, h, block = density.shape
    pairs = rows // 2
    paired = density.reshape(pairs, 2, wide, h, block)
    held = pl.pallas_call(
        functools.partial(dense_kernel, cols, ring),
        out_shape=results(pairs, wide, h, block),
        in_specs=[pl.BlockSpec(memory_space=pltpu.HBM)] * 2,
        out_specs=[IN_VMEM] * 5,
        scratch_shapes=[
            pltpu.VMEM((cols, pairs + 2, 2, wide, h, block), jnp.float32),
            pltpu.VMEM((3, wide, rows), jnp.int32),
            DMA((pairs,)),
            DMA,
            DMA((cols - 1, pairs)),
            DMA((cols - 1, pairs)),
            DMA((2,)),
            DMA((2,)),
            DMA((2, cols - 1)),
            DMA((2, cols - 1)),
            DMA((2,)),
            DMA((2,)),
            pltpu.SemaphoreType.REGULAR,
            pltpu.SemaphoreType.REGULAR,
            pltpu.SemaphoreType.REGULAR,
        ],
        compiler_params=pltpu.CompilerParams(
            collective_id=0, has_side_effects=True, vmem_limit_bytes=42 << 20),
    )(*in_hbm(paired, pattern.T))
    out = finished(pairs - LATE + 1, held, pairs, wide, h, block)
    return out.reshape(density.shape)


def sparse(ring, density, pattern):
    rows, wide, h, block = density.shape
    pairs = rows // 2
    paired = density.reshape(pairs, 2 * wide, h, block)
    tail = pairs - GUEST - 1
    hosts = tail * 2 * wide
    entries = GUEST * 2 * wide
    room = entries - EXTRA
    common = SHARED * 2 * wide
    scalars = pltpu.SMEM
    *held, over = pl.pallas_call(
        functools.partial(sparse_kernel, ring, lax.axis_size("row")),
        out_shape=results(pairs, wide, h, block) + [pltpu.SMEM((1,), jnp.int32)],
        in_specs=[pl.BlockSpec(memory_space=pltpu.HBM)] * 2,
        out_specs=[IN_VMEM] * 5 + [pl.BlockSpec(memory_space=pltpu.SMEM)],
        scratch_shapes=[
            pltpu.VMEM((pairs + 2, 2 * wide, h, block), jnp.float32),
            pltpu.VMEM((5, 2 * wide, h, block), jnp.float32),
            pltpu.VMEM((hosts, h, block), jnp.float32),
            pltpu.VMEM((hosts, h, block), jnp.float32),
            pltpu.VMEM((common, h, block), jnp.float32),
            pltpu.VMEM((entries, h, block), jnp.float32),
            pltpu.VMEM((entries, h, block), jnp.float32),
            pltpu.VMEM((ring, wide, rows), jnp.int32),
            pltpu.VMEM((wide, rows), jnp.int32),
            scalars((3, wide, rows), jnp.int32),
            scalars((rows,), jnp.int32),
            scalars((3, rows), jnp.int32),
            scalars((hosts + 2,), jnp.int32),
            scalars((2, room + 1), jnp.int32),
            scalars((2, room), jnp.int32),
            scalars((room,), jnp.int32),
            scalars((room,), jnp.int32),
            scalars((room,), jnp.int32),
            scalars((ring,), jnp.int32),
            scalars((ring,), jnp.int32),
            pltpu.VMEM((2, 2 * h, SLOTS * block), jnp.float32),
            DMA((pairs,)),
            DMA((GUEST,)),
            DMA,
            DMA,
            DMA((tail + 4,)),
            DMA((tail + 4,)),
            DMA((2,)),
            DMA((2,)),
            DMA((3,)),
            DMA((3,)),
            DMA((2, ring // 2)),
            DMA((2, ring // 2)),
            DMA((GUEST + 1,)),
            DMA((GUEST + 1,)),
            DMA((SHARED,)),
            DMA((SHARED,)),
            pltpu.SemaphoreType.REGULAR,
            pltpu.SemaphoreType.REGULAR,
        ],
        compiler_params=pltpu.CompilerParams(
            collective_id=1, has_side_effects=True, vmem_limit_bytes=40 << 20),
    )(*in_hbm(paired, pattern.T))

    def done(paired, *held):
        return finished(tail - 1, held, pairs, wide, h, block)

    def again(paired, *held):
        got = pl.pallas_call(
            top_up_kernel,
            out_shape=pltpu.VMEM((GUEST, 2 * wide, h, block), jnp.float32),
            in_specs=[pl.BlockSpec(memory_space=pltpu.HBM)],
            out_specs=IN_VMEM,
            scratch_shapes=[DMA((GUEST,)), DMA((GUEST,))],
            compiler_params=pltpu.CompilerParams(
                collective_id=0, has_side_effects=True, vmem_limit_bytes=8 << 20),
        )(*in_hbm(paired))
        count = pairs - tail + 2
        return pl.pallas_call(
            functools.partial(finish_again, tail - 1),
            out_shape=pltpu.HBM((pairs, 2, wide, h, block), jnp.float32),
            in_specs=[IN_VMEM] * 6,
            out_specs=pl.BlockSpec(memory_space=pltpu.HBM),
            scratch_shapes=[
                pltpu.VMEM((count, 2, wide, h, block), jnp.float32),
                pltpu.VMEM((GUEST, 2 * block, SLOTS * block), jnp.bfloat16),
                pltpu.VMEM((GUEST, 2 * block, SLOTS * block), jnp.bfloat16),
                DMA,
                DMA((count,)),
            ],
            compiler_params=pltpu.CompilerParams(vmem_limit_bytes=20 << 20),
        )(*held, got)

    return lax.switch(over[0], [done, again], paired, *held).reshape(density.shape)


def shards(cols, ring, density, pattern):
    if cols == 2 and lax.axis_size("row") % 2 == 0 and density.shape[0] >= 32:
        return sparse(ring, density, pattern)
    return dense(cols, ring, density, pattern)


def solution(mesh):
    cols = mesh.shape["col"]
    ring = mesh.shape["row"] * mesh.shape["depth"]
    in_specs = (P(RING, None, "col", None), P(RING, None))
    out_specs = P(RING, None, "col", None)
    body = functools.partial(shards, cols, ring)
    return jax.shard_map(body, mesh=mesh, in_specs=in_specs, out_specs=out_specs, check_vma=False)
```

```python
import functools

import jax
import jax.numpy as jnp
from jax import lax
from jax.experimental import pallas as pl
from jax.experimental.pallas import tpu as pltpu
from jax.sharding import PartitionSpec as P

MESH = pl.DeviceIdType.MESH
WIDE = 5
SLOTS = 6
RING = ("row", "depth")


def split(value):
    high = value.astype(jnp.bfloat16)
    low = (value - high.astype(jnp.float32)).astype(jnp.bfloat16)
    return high, low


def dot(a, b):
    return jnp.dot(a, b, preferred_element_type=jnp.float32)


def products(block, h, me, masks, high, low, out):
    two = 2 * block

    def product(j, a, b, sources=(0, 1, 2), start=None):
        both = jnp.concatenate([a, b], axis=0)
        m = a.shape[0]
        parts = []
        for n in range(3):
            total = None if start is None else start[:, n * two:(n + 1) * two]
            for k in sources:
                at = n - k + 1
                if at < 0 or at > 2:
                    continue
                lanes = slice(at * two, (at + 1) * two)
                ks = slice(k * two, (k + 1) * two)
                stacked = dot(both[:, ks], high[j + k - 1, :, lanes])
                term = stacked[:m] + stacked[m:] + dot(a[:, ks], low[j + k - 1, :, lanes])
                total = term if total is None else total + term
            parts.append(jnp.zeros((m, two), jnp.float32) if total is None else total)
        return jnp.concatenate(parts, axis=1)

    def own_rows(ref, j):
        return jnp.concatenate(
            [ref[j, pl.ds(pl.multiple_of(p * block + me * h, h), h), :] for p in range(2)], axis=0)

    def compute(j, to, sources=(0, 1, 2), start=None):
        factor = jnp.concatenate(
            [jnp.broadcast_to(masks[j, p:p + 1, :], (h, SLOTS * block)) for p in range(2)], axis=0)
        square = product(j, own_rows(high, j), own_rows(low, j), sources, start) * factor
        cube = product(j, *split(square)) * factor
        value = 3.0 * square - 2.0 * cube
        for p in range(2):
            for s in range(WIDE):
                out[to, p, s] = value[p * h:(p + 1) * h, (p + s) * block:(p + s + 1) * block]

    return product, own_rows, compute


BEFORE = ((0, 1), (0, 2), (1, 2))
AFTER = ((2,), (1,), (0,))
LATE = 3


def finish(first_late, masks, high, low, early, begun, out, late, early_sem, late_sem):
    h, block = early.shape[3], early.shape[4]
    me = lax.axis_index("col")
    before = first_late - 1
    after = early.shape[0] - before
    firsts = [pltpu.make_async_copy(early.at[pl.ds(0, before)], out.at[pl.ds(0, before)], early_sem.at[0])]
    if after:
        firsts.append(pltpu.make_async_copy(
            early.at[pl.ds(before, after)], out.at[pl.ds(before + LATE, after)], early_sem.at[1]))
    for first in firsts:
        first.start()
    _, _, compute = products(block, h, me, masks, high, low, late)

    def result(i):
        return pltpu.make_async_copy(late.at[i], out.at[before + i], late_sem.at[i])

    for i in range(LATE):
        compute(first_late + i, i, AFTER[i], begun[i])
        result(i).start()

    for first in firsts:
        first.wait()

    @pl.loop(0, LATE)
    def _(i):
        result(i).wait()


def dense_kernel(cols, ring, dens, pattern, masks, high, low, early, begun, raw, flags,
           local_sem, flag_sem, send_sem, recv_sem, edge_send, edge_recv,
           relay_send, relay_recv, flag_send, flag_recv, up, down, corner):
    pairs = dens.shape[0]
    h = dens.shape[3]
    block = dens.shape[4]
    last = pairs + 1
    me = lax.axis_index("col")
    depth = lax.axis_size("depth")
    place = lax.axis_index("row") * depth + lax.axis_index("depth")

    def on_ring(shift):
        at = lax.rem(place + shift + ring, ring)
        return {"row": at // depth, "depth": lax.rem(at, depth)}

    prev, following = on_ring(-1), on_ring(1)

    def peer(step):
        return {"col": lax.rem(me + step, cols)}

    def source(step):
        return lax.rem(me + cols - step, cols)

    def own(j):
        return pltpu.make_async_copy(dens.at[j - 1], raw.at[me, j], local_sem.at[j - 1])

    def across(step, j):
        return pltpu.make_async_remote_copy(
            dens.at[j - 1], raw.at[me, j], send_sem.at[step - 1, j - 1],
            recv_sem.at[step - 1, j - 1], device_id=peer(step), device_id_type=MESH)

    ends = ((pairs, 0, following), (1, last, prev))

    def edge(side):
        j, slot, device = ends[side]
        return pltpu.make_async_remote_copy(
            dens.at[j - 1], raw.at[me, slot], edge_send.at[side], edge_recv.at[side],
            device_id=device, device_id_type=MESH)

    def relay(side, step):
        j, slot, device = ends[side]
        return pltpu.make_async_remote_copy(
            raw.at[source(step), j], raw.at[source(step), slot], relay_send.at[side, step - 1],
            relay_recv.at[side, step - 1], device_id=device, device_id_type=MESH)

    def flag_edge(side):
        return pltpu.make_async_remote_copy(
            pattern, flags.at[2 * side], flag_send.at[side], flag_recv.at[side],
            device_id=ends[side][2], device_id_type=MESH)

    steps = range(1, cols)

    z, r = lax.axis_index("depth"), lax.axis_index("row")
    row_count = lax.axis_size("row")

    def greet(semaphore, device):
        pl.semaphore_signal(semaphore, inc=1, device_id=device, device_id_type=MESH)

    def along(step):
        return {"depth": z + step}

    def beside(step):
        return {"row": lax.rem(r + step + row_count, row_count)}

    barrier = pltpu.get_barrier_semaphore()
    for s in steps:
        greet(barrier, peer(s))

    @pl.when(z > 0)
    def _():
        greet(barrier, along(-1))

    @pl.when(z < depth - 1)
    def _():
        greet(barrier, along(1))

    @pl.when(z == 0)
    def _():
        greet(barrier, beside(-1))
        greet(barrier, beside(1))

    own_flags = pltpu.make_async_copy(pattern, flags.at[1], flag_sem)
    own_flags.start()
    near = jnp.where(z == 0, 2, 1) + jnp.where(z < depth - 1, 1, 0)
    pl.semaphore_wait(barrier, cols - 1 + near)

    for j in (1, pairs):
        for s in steps:
            across(s, j).start()

    @pl.loop(2, pairs)
    def _(j):
        for s in steps:
            across(s, j).start()

    @pl.when(z > 0)
    def _():
        pl.semaphore_wait(up, 1)

    @pl.when(z < depth - 1)
    def _():
        greet(up, along(1))

    @pl.when(z < depth - 2)
    def _():
        pl.semaphore_wait(down, 1)

    @pl.when((z > 0) & (z <= depth - 2))
    def _():
        greet(down, along(-1))

    @pl.when(z == 0)
    def _():
        greet(corner, beside(1))
        pl.semaphore_wait(corner, 1)

    for side in (0, 1):
        flag_edge(side).start()
        edge(side).start()

    @pl.loop(1, pairs + 1)
    def _(j):
        own(j).start()

    def expand(which, i, j):
        lane = lax.broadcasted_iota(jnp.int32, flags.shape[1:], 1)
        for p in range(2):
            picked = jnp.where(lane == i + p, flags[which], 0).astype(jnp.float32)
            spread = jnp.broadcast_to(jnp.sum(picked, axis=1, keepdims=True), (WIDE, block))
            for s in range(WIDE):
                masks[j, p:p + 1, (p + s) * block:(p + s + 1) * block] = spread[s:s + 1]
            empty = slice(0, block) if p else slice(WIDE * block, SLOTS * block)
            masks[j, p:p + 1, empty] = jnp.zeros((1, block), jnp.float32)

    def convert(j):
        for p in range(2):
            for s in range(WIDE):
                slot = p + s
                factor = masks[j, p:p + 1, slot * block:(slot + 1) * block]
                for c in range(cols):
                    a, b = split(raw[c, j, p, s] * factor)
                    rows = slice(p * block + c * h, p * block + (c + 1) * h)
                    lanes = slice(slot * block, (slot + 1) * block)
                    high[j, rows, lanes] = a
                    low[j, rows, lanes] = b
            empty = slice(0, block) if p else slice(WIDE * block, SLOTS * block)
            nothing = jnp.zeros((block, block), jnp.bfloat16)
            high[j, p * block:(p + 1) * block, empty] = nothing
            low[j, p * block:(p + 1) * block, empty] = nothing

    product, own_rows, compute = products(block, h, me, masks, high, low, early)

    own_flags.wait()

    @pl.loop(1, pairs + 1)
    def _(j):
        expand(1, 2 * (j - 1), j)

    for side in (0, 1):
        flag_edge(side).wait_recv()
    expand(0, 2 * (pairs - 1), 0)
    expand(2, 0, last)

    @pl.loop(1, pairs + 1)
    def _(j):
        own(j).wait()

    for j, side in ((1, 1), (pairs, 0)):
        for s in steps:
            across(s, j).wait_recv()
            relay(side, s).start()
        convert(j)
    for side in (0, 1):
        edge(side).wait_recv()
        for s in steps:
            relay(side, s).wait_recv()
        convert(ends[side][1])

    @pl.loop(2, pairs - 1)
    def _(j):
        for s in steps:
            across(s, j).wait_recv()
        convert(j)
        compute(j - 1, j - 2)

    def local_rows(j):
        rows = []
        for p in range(2):
            blocks = [raw[me, j, p, s] for s in range(WIDE)]
            empty = [jnp.zeros((h, block), jnp.float32)]
            row = jnp.concatenate(empty + blocks if p else blocks + empty, axis=1)
            rows.append(row * masks[j, p:p + 1, :])
        return split(jnp.concatenate(rows, axis=0))

    for i in range(LATE):
        j = pairs - LATE + 1 + i
        a, b = local_rows(j) if i == 1 else (own_rows(high, j), own_rows(low, j))
        begun[i] = product(j, a, b, BEFORE[i])

    for side in (0, 1):
        flag_edge(side).wait_send()
        edge(side).wait_send()
        for s in steps:
            relay(side, s).wait_send()
    for s in steps:
        across(s, pairs - 1).wait_recv()
    convert(pairs - 1)

    @pl.loop(1, pairs + 1)
    def _(j):
        for s in steps:
            across(s, j).wait_send()


EXTRA = 1
GUEST = 3
SHARED = 6


def sparse_kernel(ring, rows_across, dens, pattern, masks, high, low, early, begun, over,
                  mine, theirs, stage, hosted, passed, guests, fellows, flags, fellow_flags,
                  bits, word, need, chain, queue, spot, place_own, place_fellow, from_fellow, excess, spare, ahead,
                  local_sem, guest_sem, flag_sem, bits_sem, send_sem, recv_sem, edge_send, edge_recv,
                  relay_send, relay_recv, flag_send, flag_recv, fellow_send, fellow_recv,
                  pass_send, pass_recv, ready, go):
    pairs, pair_slots, h, block = dens.shape
    rows = 2 * pairs
    last = pairs + 1
    first_guest = pairs - GUEST
    tail = first_guest - 1
    shared = tail - SHARED
    room = guests.shape[0] - EXTRA
    hosts = hosted.shape[0]
    me = lax.axis_index("col")
    depth = lax.axis_size("depth")
    z, r = lax.axis_index("depth"), lax.axis_index("row")
    place = r * depth + z

    def on_ring(shift):
        at = lax.rem(place + shift + ring, ring)
        return {"row": at // depth, "depth": lax.rem(at, depth)}

    prev, following = on_ring(-1), on_ring(1)
    peer = {"col": 1 - me}
    fellow = {"row": r + 1 - 2 * lax.rem(r, 2)}

    def remote(source, target, send, recv, device):
        return pltpu.make_async_remote_copy(
            source, target, send, recv, device_id=device, device_id_type=MESH)

    def own(j):
        return pltpu.make_async_copy(dens.at[j - 1], mine.at[j], local_sem.at[j - 1])

    def guest_pair(i):
        return pl.ds(i * pair_slots, pair_slots)

    def own_guest(i):
        return pltpu.make_async_copy(
            dens.at[first_guest - 1 + i], guests.at[guest_pair(i)], guest_sem.at[i])

    def fellow_guest(i):
        return remote(dens.at[first_guest - 1 + i], fellows.at[guest_pair(i)],
                      fellow_send.at[i], fellow_recv.at[i], fellow)

    fellow_pattern = remote(pattern, fellow_flags, fellow_send.at[GUEST], fellow_recv.at[GUEST], fellow)

    def host(j):
        return j * pair_slots - WIDE

    def crossing(source, target, n):
        return remote(source, target, send_sem.at[n], recv_sem.at[n], peer)

    def staged(start, size, n):
        return crossing(stage.at[pl.ds(start, size)], hosted.at[pl.ds(start, size)], n)

    def across(j):
        return staged(host(j), pair_slots, j)

    across_first = crossing(dens.at[0, pl.ds(0, WIDE)], theirs.at[1, pl.ds(0, WIDE)], 0)
    across_second = staged(0, WIDE, tail + 1)
    across_last = staged(host(1), pair_slots, 1)
    across_half = staged(host(tail), WIDE, tail)
    extra_at = pl.ds(pair_slots - EXTRA, EXTRA)
    across_extra = crossing(dens.at[pairs - 2, extra_at], theirs.at[4, extra_at], tail + 2)
    across_end = crossing(
        dens.at[tail - 1, pl.ds(WIDE, WIDE)], theirs.at[3, pl.ds(WIDE, WIDE)], tail + 3)

    ends = ((pairs, 0, following), (1, last, prev))
    halo = (0, 2)

    def edge(side):
        j, slot, device = ends[side]
        return remote(dens.at[j - 1], mine.at[slot], edge_send.at[side], edge_recv.at[side], device)

    relay_ahead = remote(hosted.at[pl.ds(host(1), pair_slots)], theirs.at[0],
                         relay_send.at[0], relay_recv.at[0], following)
    relay_first = remote(theirs.at[1, pl.ds(0, WIDE)], theirs.at[2, pl.ds(0, WIDE)],
                         relay_send.at[1], relay_recv.at[1], prev)
    relay_second = remote(hosted.at[pl.ds(0, WIDE)], theirs.at[2, pl.ds(WIDE, WIDE)],
                          relay_send.at[2], relay_recv.at[2], prev)

    def hand_over(j):
        at = pl.ds((j - shared) * pair_slots, pair_slots)
        return remote(hosted.at[pl.ds(host(j), pair_slots)], passed.at[at],
                      pass_send.at[j - shared], pass_recv.at[j - shared], fellow)

    reach = (ring // 2, ring - 1 - ring // 2)

    def flag_hop(side, k):
        source = k - 1 if side == 0 else lax.rem(ring - k + 1, ring)
        target = k if side == 0 else ring - k
        return remote(flags.at[source], flags.at[target],
                      flag_send.at[side, k - 1], flag_recv.at[side, k - 1], ends[side][2])

    def greet(semaphore, device):
        pl.semaphore_signal(semaphore, inc=1, device_id=device, device_id_type=MESH)

    core = lax.rem(r, 2)
    hub = (me == 0) & (core == 0)
    barrier = pltpu.get_barrier_semaphore()

    @pl.when(hub | (core == 1))
    def _():
        greet(barrier, peer)

    own_bits = pltpu.make_async_copy(pattern, bits.at[0], bits_sem)
    own_bits.start()
    own_flags = pltpu.make_async_copy(pattern, flags.at[0], flag_sem)
    own_flags.start()
    own(1).start()
    for i in range(GUEST):
        own_guest(i).start()
    own(pairs).start()

    @pl.loop(2, pairs)
    def _(j):
        own(j).start()

    @pl.when((me == 1) | (core == 1))
    def _():
        pl.semaphore_wait(barrier, 1)

    @pl.when((me == 1) & (core == 0))
    def _():
        greet(ready, peer)

    @pl.when(hub)
    def _():
        pl.semaphore_wait(ready, 1)

    across_first.start()

    @pl.when((me == 0) & (core == 1))
    def _():
        greet(barrier, fellow)

    own_bits.wait()

    def need_rows(b):
        def pack(row, _):
            value = bits[b, 0, row]
            for s in range(1, WIDE):
                value = value | (bits[b, s, row] << s)
            word[row] = value
            return 0

        lax.fori_loop(0, rows, pack, 0, unroll=4)
        for row in (0, 1, rows - 2, rows - 1):
            need[b, row] = word[row]

        def keep(row, _):
            used = jnp.int32(0)
            for d in range(-2, 3):
                value = word[row + d]
                moved = value << d if d >= 0 else value >> -d
                used = used | (moved & -((value >> (2 - d)) & 1))
            need[b, row] = word[row] & used
            return 0

        lax.fori_loop(2, rows - 2, keep, 0, unroll=4)

    def active(b, row, s):
        return (need[b, row] >> s) & 1

    def row_of(j, q):
        return 2 * (j - 1) + q // WIDE, q % WIDE

    def count(value):
        total = value & 1
        for s in range(1, WIDE):
            total = total + ((value >> s) & 1)
        return total

    def holes(b, row):
        return WIDE - count(need[b, row])

    def tally(b):
        free = holes(b, rows - 2) + holes(b, rows - 1)
        free = lax.fori_loop(1, 2 * shared - 2, lambda row, n: n + holes(b, row), free)
        common = lax.fori_loop(2 * shared - 2, 2 * tail - 2, lambda row, n: n + holes(b, row), jnp.int32(0))
        end = holes(b, 2 * tail - 2)
        free = free + common + end
        start = 2 * first_guest - 2
        full, part = room // WIDE, room % WIDE
        used = jnp.int32(0)
        for i in range(full):
            if i == 2 * GUEST - 2:
                early_used = used
            used = used + count(need[b, start + i])
        if part:
            used = used + count(need[b, start + full] & ((1 << part) - 1))
        lend = jnp.minimum(common, jnp.maximum(free - end - used, 0))
        return used, free, lend, early_used

    def list_guests(b):
        nearest = jnp.int32(room)
        chain[room] = nearest
        chain[room + 1] = nearest
        for n in reversed(range(room)):
            nearest = jnp.where(active(b, *row_of(first_guest, n)) > 0, n, nearest)
            chain[n] = nearest
        for k in range(room):
            queue[b, k] = jnp.minimum(nearest, room - 1)
            nearest = chain[nearest + 1]
        queue[b, room] = room - 1

    def fill(j, base, slots, taken):
        for q in slots:
            used = active(0, *row_of(j, q))
            visitor = guests[queue[0, taken]]
            stage[base + q] = jnp.where(used > 0, mine[j, q], visitor)
            taken = jnp.minimum(taken + 1 - used, room)
        return taken

    need_rows(0)
    list_guests(0)
    own(1).wait()
    for i in range(GUEST):
        own_guest(i).wait()
    taken = fill(1, -WIDE, range(WIDE, pair_slots), jnp.int32(0))
    own(pairs).wait()
    across_second.start()
    taken = fill(pairs, host(1), range(pair_slots), taken)

    own(2).wait()
    taken = fill(2, host(2), range(pair_slots), taken)
    across_last.start()

    def prepare(j, taken):
        own(j).wait()
        taken = fill(j, host(j), range(pair_slots), taken)
        across(j - 1).start()
        return taken

    taken = lax.fori_loop(3, shared, prepare, taken)

    deeper = hub & (z < depth - 1)
    further = hub & (z == 0) & (r + 2 < rows_across)

    @pl.when(hub)
    def _():
        pl.semaphore_wait(barrier, 1 + jnp.where(deeper, 1, 0) + jnp.where(further, 1, 0))

    @pl.when(hub & (z > 0))
    def _():
        greet(barrier, {"depth": z - 1})

    @pl.when(hub & (z == 0) & (r > 0))
    def _():
        greet(barrier, {"row": r - 2})

    @pl.when(jnp.logical_not(hub & (z == 0) & (r == 0)))
    def _():
        pl.semaphore_wait(go, 1)

    @pl.when(deeper)
    def _():
        greet(go, {"depth": z + 1})

    @pl.when(further)
    def _():
        greet(go, {"row": r + 2})

    @pl.when(hub)
    def _():
        greet(go, peer)
        greet(go, fellow)
        greet(go, {"row": r + 1, "col": 1 - me})

    fellow_pattern.start()
    for i in range(GUEST):
        fellow_guest(i).start()
    own_flags.wait()
    for side in (0, 1):
        flag_hop(side, 1).start()
        edge(side).start()

    fellow_pattern.wait_recv()
    fellow_bits = pltpu.make_async_copy(fellow_flags, bits.at[1], bits_sem)
    fellow_bits.start()
    own_used, own_free, own_lend, own_early = tally(0)
    excess[0, 0] = jnp.maximum(own_used - own_free, 0)
    excess[1, 0] = jnp.maximum(own_early - own_free, 0)
    spare[0] = own_lend
    fellow_bits.wait()
    need_rows(1)
    list_guests(1)
    fellow_used, fellow_free, _, _ = tally(1)
    for i in range(GUEST):
        fellow_guest(i).wait_recv()

    def prepare_shared(j, carry):
        taken, lent = carry
        own(j).wait()
        base = host(j)
        for q in range(pair_slots):
            used = active(0, *row_of(j, q))
            ours = taken < own_used
            visitor = jnp.where(
                ours, guests[queue[0, jnp.minimum(taken, room)]],
                fellows[queue[1, jnp.minimum(fellow_free + lent, room)]])
            stage[base + q] = jnp.where(used > 0, mine[j, q], visitor)
            taken = taken + 1 - used
            lent = lent + jnp.where(ours, 0, 1 - used)
        across(j - 1).start()
        return taken, lent

    taken, _ = lax.fori_loop(shared, tail, prepare_shared, (taken, jnp.int32(0)))
    own(tail).wait()
    fill(tail, host(tail), range(WIDE), jnp.minimum(taken, room))
    across(tail - 1).start()

    @pl.loop(tail + 1, pairs)
    def _(j):
        own(j).wait()

    def scan(j, base, slots, free):
        for q in reversed(slots):
            free = jnp.where(active(0, *row_of(j, q)) > 0, free, base + q)
            chain[base + q] = free
        return free

    def scan_pair(i, free):
        j = tail - 1 - i
        return scan(j, host(j), range(pair_slots), free)

    free = jnp.int32(hosts)
    chain[hosts] = free
    chain[hosts + 1] = free
    free = scan(tail, host(tail), range(WIDE), free)
    free = lax.fori_loop(0, tail - 2, scan_pair, free)
    free = scan(pairs, host(1), range(pair_slots), free)
    free = scan(1, -WIDE, range(WIDE, pair_slots), free)
    across_half.start()
    across_extra.start()
    across_end.start()
    for k in range(room):
        spot[0, k] = jnp.minimum(free, hosts - 1)
        free = chain[free + 1]

    common = passed.shape[0]

    def scan_fellow(i, carry):
        nearest, above = carry
        j = tail - 1 - i
        for q in reversed(range(pair_slots)):
            hole = 1 - active(1, *row_of(j, q))
            above = above + hole
            lends = (hole > 0) & (fellow_free - above >= fellow_used)
            at = (j - shared) * pair_slots + q
            nearest = jnp.where(lends, at, nearest)
            chain[at] = nearest
        return nearest, above

    nearest = jnp.int32(common)
    chain[common] = nearest
    chain[common + 1] = nearest
    nearest, _ = lax.fori_loop(0, tail - shared, scan_fellow, (nearest, holes(1, 2 * tail - 2)))
    for k in range(room):
        spot[1, k] = jnp.minimum(nearest, common - 1)
        nearest = chain[nearest + 1]
    rank = jnp.int32(0)
    for n in range(room):
        place_own[n] = spot[0, jnp.minimum(rank, room - 1)]
        place_fellow[n] = spot[1, jnp.clip(rank - own_free, 0, room - 1)]
        from_fellow[n] = jnp.where(rank >= own_free, 1, 0)
        rank = rank + active(0, *row_of(first_guest, n))

    def absorb(k):
        fetch = pltpu.make_async_copy(flags.at[k], bits.at[2], bits_sem)
        fetch.start()
        fetch.wait()
        need_rows(2)
        used, free, lend, early_used = tally(2)
        excess[0, k] = jnp.maximum(used - free, 0)
        excess[1, k] = jnp.maximum(early_used - free, 0)
        spare[k] = lend

    def expand(which, i, j):
        lane = lax.broadcasted_iota(jnp.int32, flags.shape[1:], 1)
        for p in range(2):
            picked = jnp.where(lane == i + p, flags[which], 0).astype(jnp.float32)
            spread = jnp.broadcast_to(jnp.sum(picked, axis=1, keepdims=True), (WIDE, block))
            for s in range(WIDE):
                masks[j, p:p + 1, (p + s) * block:(p + s + 1) * block] = spread[s:s + 1]
            empty = slice(0, block) if p else slice(WIDE * block, SLOTS * block)
            masks[j, p:p + 1, empty] = jnp.zeros((1, block), jnp.float32)

    def convert(j, other, halves=(0, 1)):
        for p in halves:
            for s in range(WIDE):
                slot = p + s
                lanes = slice(slot * block, (slot + 1) * block)
                factor = masks[j, p:p + 1, lanes]
                for c, value in ((me, mine[j, p * WIDE + s]), (1 - me, other(p * WIDE + s))):
                    a, b = split(value * factor)
                    at = pl.ds(pl.multiple_of(p * block + c * h, h), h)
                    high[j, at, lanes] = a
                    low[j, at, lanes] = b
            empty = slice(0, block) if p else slice(WIDE * block, SLOTS * block)
            nothing = jnp.zeros((block, block), jnp.bfloat16)
            high[j, p * block:(p + 1) * block, empty] = nothing
            low[j, p * block:(p + 1) * block, empty] = nothing

    def arrived(j):
        return lambda q: hosted[host(j) + q]

    def direct(i):
        return lambda q: theirs[i, q]

    def visiting(j):
        def block_at(q):
            n = (j - first_guest) * pair_slots + q
            if n >= room:
                return theirs[4, q]
            return jnp.where(from_fellow[n] > 0, passed[place_fellow[n]], hosted[place_own[n]])

        return block_at

    product, own_rows, compute = products(block, h, me, masks, high, low, early)

    @pl.loop(1, pairs + 1)
    def _(j):
        expand(0, 2 * (j - 1), j)

    for side in (0, 1):
        flag_hop(side, 1).wait_recv()
    for side in (0, 1):
        if reach[side] > 1:
            flag_hop(side, 2).start()
    expand(1, 2 * (pairs - 1), 0)
    expand(ring - 1, 0, last)

    across_first.wait_recv()
    relay_first.start()
    across_second.wait_recv()
    relay_second.start()
    convert(1, lambda q: theirs[1, q] if q < WIDE else hosted[q - WIDE])
    across_last.wait_recv()
    relay_ahead.start()
    convert(pairs, arrived(1))
    absorb(1)
    absorb(ring - 1)
    edge(0).wait_recv()
    relay_ahead.wait_recv()
    convert(0, direct(0))
    edge(1).wait_recv()
    relay_first.wait_recv()
    relay_second.wait_recv()
    convert(last, direct(2))

    turns = tail - 2
    each = -(-(reach[0] - 1) // turns)

    def pass_on(side, k):
        @pl.when(k <= reach[side])
        def _():
            flag_hop(side, k).wait_recv()

        @pl.when(k + 1 <= reach[side])
        def _():
            flag_hop(side, k + 1).start()

        @pl.when(k <= reach[side])
        def _():
            absorb(k if side == 0 else ring - k)

    @pl.loop(2, tail)
    def _(j):
        across(j).wait_recv()

        @pl.when(j >= shared)
        def _():
            hand_over(j).start()

        convert(j, arrived(j))
        compute(j - 1, j - 2)
        for u in range(each):
            for side in (0, 1):
                pass_on(side, (j - 2) * each + u + 2)

    level = jnp.int32(0)
    for k in range(ring):
        there = lax.rem(place - k + ring, ring)
        band = there // depth
        partner = there + (1 - 2 * lax.rem(band, 2)) * depth
        lent = spare[lax.rem(place - partner + ring, ring)]
        level = jnp.maximum(level, jnp.where(excess[0, k] > lent, 1, 0))
        level = jnp.maximum(level, jnp.where(excess[1, k] > lent, 2, 0))
    over[0] = level

    def local_rows(j):
        parts = []
        for p in range(2):
            blocks = [mine[j, p * WIDE + s] for s in range(WIDE)]
            empty = [jnp.zeros((h, block), jnp.float32)]
            row = jnp.concatenate(empty + blocks if p else blocks + empty, axis=1)
            parts.append(row * masks[j, p:p + 1, :])
        return split(jnp.concatenate(parts, axis=0))

    def converted_rows(j):
        return own_rows(high, j), own_rows(low, j)

    begun[0] = product(tail - 1, *converted_rows(tail - 1), BEFORE[0])
    begun[1] = product(tail, *local_rows(tail), (0,))
    ahead[0] = product(pairs - 1, *local_rows(pairs - 1), (2,))
    ahead[1] = product(pairs, *converted_rows(pairs), (1, 2))

    for j in range(shared, tail):
        hand_over(j).wait_recv()
    across_half.wait_recv()
    for j in range(first_guest, pairs - 1):
        convert(j, visiting(j))
    convert(tail, arrived(tail), (0,))
    begun[1] = product(tail, *local_rows(tail), (2,), begun[1])
    across_extra.wait_recv()
    convert(pairs - 1, visiting(pairs - 1))
    for j in range(first_guest + 1, pairs - 1):
        compute(j, j - LATE - 1)
    begun[2] = product(first_guest, *converted_rows(first_guest), BEFORE[2])
    compute(pairs - 1, pairs - LATE - 2, (0, 1), ahead[0])
    compute(pairs, pairs - LATE - 1, (0,), ahead[1])

    fellow_pattern.wait_send()
    for i in range(GUEST):
        fellow_guest(i).wait_send()
    for j in range(shared, tail):
        hand_over(j).wait_send()
    for side in (0, 1):
        edge(side).wait_send()

        @pl.loop(1, reach[side] + 1)
        def _(k):
            flag_hop(side, k).wait_send()

    relay_ahead.wait_send()
    relay_first.wait_send()
    relay_second.wait_send()

    across_end.wait_recv()
    convert(tail, direct(3), (1,))
    across_first.wait_send()
    across_second.wait_send()
    across_last.wait_send()
    across_half.wait_send()
    across_extra.wait_send()
    across_end.wait_send()

    @pl.loop(2, tail)
    def _(j):
        across(j).wait_send()


class Patched:
    def __init__(self, ref, fixed, first):
        self.ref, self.fixed, self.first = ref, fixed, first

    def __getitem__(self, at):
        j = at[0] - self.first
        if 0 <= j < self.fixed.shape[0]:
            return self.fixed[(j,) + tuple(at[1:])]
        return self.ref[at]


def top_up_kernel(dens, got, send_sem, recv_sem):
    count = got.shape[0]
    first = dens.shape[0] - 1 - count
    peer = {"col": 1 - lax.axis_index("col")}
    barrier = pltpu.get_barrier_semaphore()
    pl.semaphore_signal(barrier, inc=1, device_id=peer, device_id_type=MESH)
    pl.semaphore_wait(barrier, 1)

    def across(i):
        return pltpu.make_async_remote_copy(
            dens.at[first + i], got.at[i], send_sem.at[i], recv_sem.at[i],
            device_id=peer, device_id_type=MESH)

    for i in range(count):
        across(i).start()
    for i in range(count):
        across(i).wait()


def finish_again(first_late, masks, high, low, early, begun, got, out,
                 late, fixed_high, fixed_low, early_sem, late_sem):
    h, block = early.shape[3], early.shape[4]
    me = lax.axis_index("col")
    before = first_late - 1
    count = late.shape[0]
    first = pltpu.make_async_copy(early.at[pl.ds(0, before)], out.at[pl.ds(0, before)], early_sem)
    first.start()
    fixed = got.shape[0]
    first_guest = first_late + count - 1 - fixed
    fixed_high[...] = high[pl.ds(first_guest, fixed)]
    fixed_low[...] = low[pl.ds(first_guest, fixed)]
    for i in range(fixed):
        for q in range(2 * WIDE):
            p, s = divmod(q, WIDE)
            lanes = slice((p + s) * block, (p + s + 1) * block)
            a, b = split(got[i, q] * masks[first_guest + i, p:p + 1, lanes])
            at = pl.ds(pl.multiple_of(p * block + (1 - me) * h, h), h)
            fixed_high[i, at, lanes] = a
            fixed_low[i, at, lanes] = b
    _, _, compute = products(block, h, me, masks, Patched(high, fixed_high, first_guest),
                             Patched(low, fixed_low, first_guest), late)

    def result(i):
        return pltpu.make_async_copy(late.at[i], out.at[before + i], late_sem.at[i])

    for i in range(count):
        if fixed < GUEST and i < LATE:
            compute(first_late + i, i, AFTER[i], begun[i])
        else:
            compute(first_late + i, i)
        result(i).start()
    first.wait()

    @pl.loop(0, count)
    def _(i):
        result(i).wait()


DMA = pltpu.SemaphoreType.DMA
IN_VMEM = pl.BlockSpec(memory_space=pltpu.VMEM)


def results(pairs, wide, h, block):
    width = SLOTS * block
    return [
        pltpu.VMEM((pairs + 2, 8, width), jnp.float32),
        pltpu.VMEM((pairs + 2, 2 * block, width), jnp.bfloat16),
        pltpu.VMEM((pairs + 2, 2 * block, width), jnp.bfloat16),
        pltpu.VMEM((pairs - LATE, 2, wide, h, block), jnp.float32),
        pltpu.VMEM((LATE, 2 * h, width), jnp.float32),
    ]


def in_hbm(*arrays):
    return (pltpu.with_memory_space_constraint(x, pltpu.HBM) for x in arrays)


def finished(first_late, held, pairs, wide, h, block):
    return pl.pallas_call(
        functools.partial(finish, first_late),
        out_shape=pltpu.HBM((pairs, 2, wide, h, block), jnp.float32),
        in_specs=[IN_VMEM] * 5,
        out_specs=pl.BlockSpec(memory_space=pltpu.HBM),
        scratch_shapes=[
            pltpu.VMEM((LATE, 2, wide, h, block), jnp.float32),
            DMA((2,)),
            DMA((LATE,)),
        ],
        compiler_params=pltpu.CompilerParams(vmem_limit_bytes=16 << 20),
    )(*held)


def dense(cols, ring, density, pattern):
    rows, wide, h, block = density.shape
    pairs = rows // 2
    paired = density.reshape(pairs, 2, wide, h, block)
    held = pl.pallas_call(
        functools.partial(dense_kernel, cols, ring),
        out_shape=results(pairs, wide, h, block),
        in_specs=[pl.BlockSpec(memory_space=pltpu.HBM)] * 2,
        out_specs=[IN_VMEM] * 5,
        scratch_shapes=[
            pltpu.VMEM((cols, pairs + 2, 2, wide, h, block), jnp.float32),
            pltpu.VMEM((3, wide, rows), jnp.int32),
            DMA((pairs,)),
            DMA,
            DMA((cols - 1, pairs)),
            DMA((cols - 1, pairs)),
            DMA((2,)),
            DMA((2,)),
            DMA((2, cols - 1)),
            DMA((2, cols - 1)),
            DMA((2,)),
            DMA((2,)),
            pltpu.SemaphoreType.REGULAR,
            pltpu.SemaphoreType.REGULAR,
            pltpu.SemaphoreType.REGULAR,
        ],
        compiler_params=pltpu.CompilerParams(
            collective_id=0, has_side_effects=True, vmem_limit_bytes=42 << 20),
    )(*in_hbm(paired, pattern.T))
    out = finished(pairs - LATE + 1, held, pairs, wide, h, block)
    return out.reshape(density.shape)


def sparse(ring, density, pattern):
    rows, wide, h, block = density.shape
    pairs = rows // 2
    paired = density.reshape(pairs, 2 * wide, h, block)
    tail = pairs - GUEST - 1
    hosts = tail * 2 * wide
    entries = GUEST * 2 * wide
    room = entries - EXTRA
    common = SHARED * 2 * wide
    scalars = pltpu.SMEM
    *held, over = pl.pallas_call(
        functools.partial(sparse_kernel, ring, lax.axis_size("row")),
        out_shape=results(pairs, wide, h, block) + [pltpu.SMEM((1,), jnp.int32)],
        in_specs=[pl.BlockSpec(memory_space=pltpu.HBM)] * 2,
        out_specs=[IN_VMEM] * 5 + [pl.BlockSpec(memory_space=pltpu.SMEM)],
        scratch_shapes=[
            pltpu.VMEM((pairs + 2, 2 * wide, h, block), jnp.float32),
            pltpu.VMEM((5, 2 * wide, h, block), jnp.float32),
            pltpu.VMEM((hosts, h, block), jnp.float32),
            pltpu.VMEM((hosts, h, block), jnp.float32),
            pltpu.VMEM((common, h, block), jnp.float32),
            pltpu.VMEM((entries, h, block), jnp.float32),
            pltpu.VMEM((entries, h, block), jnp.float32),
            pltpu.VMEM((ring, wide, rows), jnp.int32),
            pltpu.VMEM((wide, rows), jnp.int32),
            scalars((3, wide, rows), jnp.int32),
            scalars((rows,), jnp.int32),
            scalars((3, rows), jnp.int32),
            scalars((hosts + 2,), jnp.int32),
            scalars((2, room + 1), jnp.int32),
            scalars((2, room), jnp.int32),
            scalars((room,), jnp.int32),
            scalars((room,), jnp.int32),
            scalars((room,), jnp.int32),
            scalars((2, ring), jnp.int32),
            scalars((ring,), jnp.int32),
            pltpu.VMEM((2, 2 * h, SLOTS * block), jnp.float32),
            DMA((pairs,)),
            DMA((GUEST,)),
            DMA,
            DMA,
            DMA((tail + 4,)),
            DMA((tail + 4,)),
            DMA((2,)),
            DMA((2,)),
            DMA((3,)),
            DMA((3,)),
            DMA((2, ring // 2)),
            DMA((2, ring // 2)),
            DMA((GUEST + 1,)),
            DMA((GUEST + 1,)),
            DMA((SHARED,)),
            DMA((SHARED,)),
            pltpu.SemaphoreType.REGULAR,
            pltpu.SemaphoreType.REGULAR,
        ],
        compiler_params=pltpu.CompilerParams(
            collective_id=1, has_side_effects=True, vmem_limit_bytes=40 << 20),
    )(*in_hbm(paired, pattern.T))

    def done(paired, *held):
        return finished(tail - 1, held, pairs, wide, h, block)

    ids = {1: 2, GUEST: 0}

    def again(fixed, paired, *held):
        got = pl.pallas_call(
            top_up_kernel,
            out_shape=pltpu.VMEM((fixed, 2 * wide, h, block), jnp.float32),
            in_specs=[pl.BlockSpec(memory_space=pltpu.HBM)],
            out_specs=IN_VMEM,
            scratch_shapes=[DMA((fixed,)), DMA((fixed,))],
            compiler_params=pltpu.CompilerParams(
                collective_id=ids[fixed], has_side_effects=True, vmem_limit_bytes=8 << 20),
        )(*in_hbm(paired))
        count = pairs - tail + 2
        return pl.pallas_call(
            functools.partial(finish_again, tail - 1),
            out_shape=pltpu.HBM((pairs, 2, wide, h, block), jnp.float32),
            in_specs=[IN_VMEM] * 6,
            out_specs=pl.BlockSpec(memory_space=pltpu.HBM),
            scratch_shapes=[
                pltpu.VMEM((count, 2, wide, h, block), jnp.float32),
                pltpu.VMEM((fixed, 2 * block, SLOTS * block), jnp.bfloat16),
                pltpu.VMEM((fixed, 2 * block, SLOTS * block), jnp.bfloat16),
                DMA,
                DMA((count,)),
            ],
            compiler_params=pltpu.CompilerParams(vmem_limit_bytes=20 << 20),
        )(*held, got)

    branches = [done, functools.partial(again, 1), functools.partial(again, GUEST)]
    return lax.switch(over[0], branches, paired, *held).reshape(density.shape)


def shards(cols, ring, density, pattern):
    if cols == 2 and lax.axis_size("row") % 2 == 0 and density.shape[0] >= 32:
        return sparse(ring, density, pattern)
    return dense(cols, ring, density, pattern)


def solution(mesh):
    cols = mesh.shape["col"]
    ring = mesh.shape["row"] * mesh.shape["depth"]
    in_specs = (P(RING, None, "col", None), P(RING, None))
    out_specs = P(RING, None, "col", None)
    body = functools.partial(shards, cols, ring)
    return jax.shard_map(body, mesh=mesh, in_specs=in_specs, out_specs=out_specs, check_vma=False)
```

```python
import functools

import jax
import jax.numpy as jnp
from jax import lax
from jax.experimental import pallas as pl
from jax.experimental.pallas import tpu as pltpu
from jax.sharding import PartitionSpec as P

MESH = pl.DeviceIdType.MESH
WIDE = 5
SLOTS = 6
RING = ("row", "depth")


def split(value):
    high = value.astype(jnp.bfloat16)
    low = (value - high.astype(jnp.float32)).astype(jnp.bfloat16)
    return high, low


def dot(a, b):
    return jnp.dot(a, b, preferred_element_type=jnp.float32)


def products(block, h, me, masks, high, low, out):
    two = 2 * block

    def product(j, a, b, sources=(0, 1, 2), start=None):
        both = jnp.concatenate([a, b], axis=0)
        m = a.shape[0]
        parts = []
        for n in range(3):
            total = None if start is None else start[:, n * two:(n + 1) * two]
            for k in sources:
                at = n - k + 1
                if at < 0 or at > 2:
                    continue
                lanes = slice(at * two, (at + 1) * two)
                ks = slice(k * two, (k + 1) * two)
                stacked = dot(both[:, ks], high[j + k - 1, :, lanes])
                term = stacked[:m] + stacked[m:] + dot(a[:, ks], low[j + k - 1, :, lanes])
                total = term if total is None else total + term
            parts.append(jnp.zeros((m, two), jnp.float32) if total is None else total)
        return jnp.concatenate(parts, axis=1)

    def own_rows(ref, j):
        return jnp.concatenate(
            [ref[j, pl.ds(pl.multiple_of(p * block + me * h, h), h), :] for p in range(2)], axis=0)

    def compute(j, to, sources=(0, 1, 2), start=None):
        factor = jnp.concatenate(
            [jnp.broadcast_to(masks[j, p:p + 1, :], (h, SLOTS * block)) for p in range(2)], axis=0)
        square = product(j, own_rows(high, j), own_rows(low, j), sources, start) * factor
        cube = product(j, *split(square)) * factor
        value = 3.0 * square - 2.0 * cube
        for p in range(2):
            for s in range(WIDE):
                out[to, p, s] = value[p * h:(p + 1) * h, (p + s) * block:(p + s + 1) * block]

    return product, own_rows, compute


BEFORE = ((0, 1), (0, 2), (1, 2))
AFTER = ((2,), (1,), (0,))
LATE = 3


def finish(first_late, masks, high, low, early, begun, out, late, early_sem, late_sem):
    h, block = early.shape[3], early.shape[4]
    me = lax.axis_index("col")
    before = first_late - 1
    after = early.shape[0] - before
    firsts = [pltpu.make_async_copy(early.at[pl.ds(0, before)], out.at[pl.ds(0, before)], early_sem.at[0])]
    if after:
        firsts.append(pltpu.make_async_copy(
            early.at[pl.ds(before, after)], out.at[pl.ds(before + LATE, after)], early_sem.at[1]))
    for first in firsts:
        first.start()
    _, _, compute = products(block, h, me, masks, high, low, late)

    def result(i):
        return pltpu.make_async_copy(late.at[i], out.at[before + i], late_sem.at[i])

    for i in range(LATE):
        compute(first_late + i, i, AFTER[i], begun[i])
        result(i).start()

    for first in firsts:
        first.wait()

    @pl.loop(0, LATE)
    def _(i):
        result(i).wait()


def dense_kernel(cols, ring, dens, pattern, masks, high, low, early, begun, raw, flags,
           local_sem, flag_sem, send_sem, recv_sem, edge_send, edge_recv,
           relay_send, relay_recv, flag_send, flag_recv, up, down, corner):
    pairs = dens.shape[0]
    h = dens.shape[3]
    block = dens.shape[4]
    last = pairs + 1
    me = lax.axis_index("col")
    depth = lax.axis_size("depth")
    place = lax.axis_index("row") * depth + lax.axis_index("depth")

    def on_ring(shift):
        at = lax.rem(place + shift + ring, ring)
        return {"row": at // depth, "depth": lax.rem(at, depth)}

    prev, following = on_ring(-1), on_ring(1)

    def peer(step):
        return {"col": lax.rem(me + step, cols)}

    def source(step):
        return lax.rem(me + cols - step, cols)

    def own(j):
        return pltpu.make_async_copy(dens.at[j - 1], raw.at[me, j], local_sem.at[j - 1])

    def across(step, j):
        return pltpu.make_async_remote_copy(
            dens.at[j - 1], raw.at[me, j], send_sem.at[step - 1, j - 1],
            recv_sem.at[step - 1, j - 1], device_id=peer(step), device_id_type=MESH)

    ends = ((pairs, 0, following), (1, last, prev))

    def edge(side):
        j, slot, device = ends[side]
        return pltpu.make_async_remote_copy(
            dens.at[j - 1], raw.at[me, slot], edge_send.at[side], edge_recv.at[side],
            device_id=device, device_id_type=MESH)

    def relay(side, step):
        j, slot, device = ends[side]
        return pltpu.make_async_remote_copy(
            raw.at[source(step), j], raw.at[source(step), slot], relay_send.at[side, step - 1],
            relay_recv.at[side, step - 1], device_id=device, device_id_type=MESH)

    def flag_edge(side):
        return pltpu.make_async_remote_copy(
            pattern, flags.at[2 * side], flag_send.at[side], flag_recv.at[side],
            device_id=ends[side][2], device_id_type=MESH)

    steps = range(1, cols)

    z, r = lax.axis_index("depth"), lax.axis_index("row")
    row_count = lax.axis_size("row")

    def greet(semaphore, device):
        pl.semaphore_signal(semaphore, inc=1, device_id=device, device_id_type=MESH)

    def along(step):
        return {"depth": z + step}

    def beside(step):
        return {"row": lax.rem(r + step + row_count, row_count)}

    barrier = pltpu.get_barrier_semaphore()
    for s in steps:
        greet(barrier, peer(s))

    @pl.when(z > 0)
    def _():
        greet(barrier, along(-1))

    @pl.when(z < depth - 1)
    def _():
        greet(barrier, along(1))

    @pl.when(z == 0)
    def _():
        greet(barrier, beside(-1))
        greet(barrier, beside(1))

    own_flags = pltpu.make_async_copy(pattern, flags.at[1], flag_sem)
    own_flags.start()
    near = jnp.where(z == 0, 2, 1) + jnp.where(z < depth - 1, 1, 0)
    pl.semaphore_wait(barrier, cols - 1 + near)

    for j in (1, pairs):
        for s in steps:
            across(s, j).start()

    @pl.loop(2, pairs)
    def _(j):
        for s in steps:
            across(s, j).start()

    @pl.when(z > 0)
    def _():
        pl.semaphore_wait(up, 1)

    @pl.when(z < depth - 1)
    def _():
        greet(up, along(1))

    @pl.when(z < depth - 2)
    def _():
        pl.semaphore_wait(down, 1)

    @pl.when((z > 0) & (z <= depth - 2))
    def _():
        greet(down, along(-1))

    @pl.when(z == 0)
    def _():
        greet(corner, beside(1))
        pl.semaphore_wait(corner, 1)

    for side in (0, 1):
        flag_edge(side).start()
        edge(side).start()

    @pl.loop(1, pairs + 1)
    def _(j):
        own(j).start()

    def expand(which, i, j):
        lane = lax.broadcasted_iota(jnp.int32, flags.shape[1:], 1)
        for p in range(2):
            picked = jnp.where(lane == i + p, flags[which], 0).astype(jnp.float32)
            spread = jnp.broadcast_to(jnp.sum(picked, axis=1, keepdims=True), (WIDE, block))
            for s in range(WIDE):
                masks[j, p:p + 1, (p + s) * block:(p + s + 1) * block] = spread[s:s + 1]
            empty = slice(0, block) if p else slice(WIDE * block, SLOTS * block)
            masks[j, p:p + 1, empty] = jnp.zeros((1, block), jnp.float32)

    def convert(j):
        for p in range(2):
            for s in range(WIDE):
                slot = p + s
                factor = masks[j, p:p + 1, slot * block:(slot + 1) * block]
                for c in range(cols):
                    a, b = split(raw[c, j, p, s] * factor)
                    rows = slice(p * block + c * h, p * block + (c + 1) * h)
                    lanes = slice(slot * block, (slot + 1) * block)
                    high[j, rows, lanes] = a
                    low[j, rows, lanes] = b
            empty = slice(0, block) if p else slice(WIDE * block, SLOTS * block)
            nothing = jnp.zeros((block, block), jnp.bfloat16)
            high[j, p * block:(p + 1) * block, empty] = nothing
            low[j, p * block:(p + 1) * block, empty] = nothing

    product, own_rows, compute = products(block, h, me, masks, high, low, early)

    own_flags.wait()

    @pl.loop(1, pairs + 1)
    def _(j):
        expand(1, 2 * (j - 1), j)

    for side in (0, 1):
        flag_edge(side).wait_recv()
    expand(0, 2 * (pairs - 1), 0)
    expand(2, 0, last)

    @pl.loop(1, pairs + 1)
    def _(j):
        own(j).wait()

    for j, side in ((1, 1), (pairs, 0)):
        for s in steps:
            across(s, j).wait_recv()
            relay(side, s).start()
        convert(j)
    for side in (0, 1):
        edge(side).wait_recv()
        for s in steps:
            relay(side, s).wait_recv()
        convert(ends[side][1])

    @pl.loop(2, pairs - 1)
    def _(j):
        for s in steps:
            across(s, j).wait_recv()
        convert(j)
        compute(j - 1, j - 2)

    def local_rows(j):
        rows = []
        for p in range(2):
            blocks = [raw[me, j, p, s] for s in range(WIDE)]
            empty = [jnp.zeros((h, block), jnp.float32)]
            row = jnp.concatenate(empty + blocks if p else blocks + empty, axis=1)
            rows.append(row * masks[j, p:p + 1, :])
        return split(jnp.concatenate(rows, axis=0))

    for i in range(LATE):
        j = pairs - LATE + 1 + i
        a, b = local_rows(j) if i == 1 else (own_rows(high, j), own_rows(low, j))
        begun[i] = product(j, a, b, BEFORE[i])

    for side in (0, 1):
        flag_edge(side).wait_send()
        edge(side).wait_send()
        for s in steps:
            relay(side, s).wait_send()
    for s in steps:
        across(s, pairs - 1).wait_recv()
    convert(pairs - 1)

    @pl.loop(1, pairs + 1)
    def _(j):
        for s in steps:
            across(s, j).wait_send()


GUEST = 3
SHARED = 6


def sparse_kernel(ring, rows_across, dens, pattern, masks, high, low, early, begun, over,
                  mine, theirs, stage, hosted, passed, guests, fellows, flags, fellow_flags,
                  bits, word, need, chain, queue, spot, place_own, place_fellow, from_fellow, excess, spare, ahead,
                  local_sem, guest_sem, flag_sem, bits_sem, send_sem, recv_sem, edge_send, edge_recv,
                  relay_send, relay_recv, flag_send, flag_recv, fellow_send, fellow_recv,
                  pass_send, pass_recv, ready, go):
    pairs, pair_slots, h, block = dens.shape
    rows = 2 * pairs
    last = pairs + 1
    first_guest = pairs - GUEST
    tail = first_guest - 1
    shared = tail - SHARED
    room = guests.shape[0]
    hosts = hosted.shape[0]
    me = lax.axis_index("col")
    depth = lax.axis_size("depth")
    z, r = lax.axis_index("depth"), lax.axis_index("row")
    place = r * depth + z

    def on_ring(shift):
        at = lax.rem(place + shift + ring, ring)
        return {"row": at // depth, "depth": lax.rem(at, depth)}

    prev, following = on_ring(-1), on_ring(1)
    peer = {"col": 1 - me}
    fellow = {"row": r + 1 - 2 * lax.rem(r, 2)}

    def remote(source, target, send, recv, device):
        return pltpu.make_async_remote_copy(
            source, target, send, recv, device_id=device, device_id_type=MESH)

    def own(j):
        return pltpu.make_async_copy(dens.at[j - 1], mine.at[j], local_sem.at[j - 1])

    def guest_pair(i):
        return pl.ds(i * pair_slots, pair_slots)

    def own_guest(i):
        return pltpu.make_async_copy(
            dens.at[first_guest - 1 + i], guests.at[guest_pair(i)], guest_sem.at[i])

    def fellow_guest(i):
        return remote(dens.at[first_guest - 1 + i], fellows.at[guest_pair(i)],
                      fellow_send.at[i], fellow_recv.at[i], fellow)

    fellow_pattern = remote(pattern, fellow_flags, fellow_send.at[GUEST], fellow_recv.at[GUEST], fellow)

    def host(j):
        return j * pair_slots - WIDE

    def crossing(source, target, n):
        return remote(source, target, send_sem.at[n], recv_sem.at[n], peer)

    def staged(start, size, n):
        return crossing(stage.at[pl.ds(start, size)], hosted.at[pl.ds(start, size)], n)

    def across(j):
        return staged(host(j), pair_slots, j)

    across_first = crossing(dens.at[0, pl.ds(0, WIDE)], theirs.at[1, pl.ds(0, WIDE)], 0)
    across_second = staged(0, WIDE, tail + 1)
    across_last = staged(host(1), pair_slots, 1)
    across_half = staged(host(tail), WIDE, tail)
    across_end = crossing(
        dens.at[tail - 1, pl.ds(WIDE, WIDE)], theirs.at[3, pl.ds(WIDE, WIDE)], tail + 2)

    ends = ((pairs, 0, following), (1, last, prev))
    halo = (0, 2)

    def edge(side):
        j, slot, device = ends[side]
        return remote(dens.at[j - 1], mine.at[slot], edge_send.at[side], edge_recv.at[side], device)

    relay_ahead = remote(hosted.at[pl.ds(host(1), pair_slots)], theirs.at[0],
                         relay_send.at[0], relay_recv.at[0], following)
    relay_first = remote(theirs.at[1, pl.ds(0, WIDE)], theirs.at[2, pl.ds(0, WIDE)],
                         relay_send.at[1], relay_recv.at[1], prev)
    relay_second = remote(hosted.at[pl.ds(0, WIDE)], theirs.at[2, pl.ds(WIDE, WIDE)],
                          relay_send.at[2], relay_recv.at[2], prev)

    def hand_over(j):
        at = pl.ds((j - shared) * pair_slots, pair_slots)
        return remote(hosted.at[pl.ds(host(j), pair_slots)], passed.at[at],
                      pass_send.at[j - shared], pass_recv.at[j - shared], fellow)

    reach = (ring // 2, ring - 1 - ring // 2)

    def flag_hop(side, k):
        source = k - 1 if side == 0 else lax.rem(ring - k + 1, ring)
        target = k if side == 0 else ring - k
        return remote(flags.at[source], flags.at[target],
                      flag_send.at[side, k - 1], flag_recv.at[side, k - 1], ends[side][2])

    def greet(semaphore, device):
        pl.semaphore_signal(semaphore, inc=1, device_id=device, device_id_type=MESH)

    core = lax.rem(r, 2)
    hub = (me == 0) & (core == 0)
    barrier = pltpu.get_barrier_semaphore()

    @pl.when(hub | (core == 1))
    def _():
        greet(barrier, peer)

    own_bits = pltpu.make_async_copy(pattern, bits.at[0], bits_sem)
    own_bits.start()
    own_flags = pltpu.make_async_copy(pattern, flags.at[0], flag_sem)
    own_flags.start()
    own(1).start()
    for i in range(GUEST):
        own_guest(i).start()
    own(pairs).start()

    @pl.loop(2, pairs)
    def _(j):
        own(j).start()

    @pl.when((me == 1) | (core == 1))
    def _():
        pl.semaphore_wait(barrier, 1)

    @pl.when((me == 1) & (core == 0))
    def _():
        greet(ready, peer)

    @pl.when(hub)
    def _():
        pl.semaphore_wait(ready, 1)

    across_first.start()

    @pl.when((me == 0) & (core == 1))
    def _():
        greet(barrier, fellow)

    own_bits.wait()

    def need_rows(b):
        def pack(row, _):
            value = bits[b, 0, row]
            for s in range(1, WIDE):
                value = value | (bits[b, s, row] << s)
            word[row] = value
            return 0

        lax.fori_loop(0, rows, pack, 0, unroll=4)
        for row in (0, 1, rows - 2, rows - 1):
            need[b, row] = word[row]

        def keep(row, _):
            used = jnp.int32(0)
            for d in range(-2, 3):
                value = word[row + d]
                moved = value << d if d >= 0 else value >> -d
                used = used | (moved & -((value >> (2 - d)) & 1))
            need[b, row] = word[row] & used
            return 0

        lax.fori_loop(2, rows - 2, keep, 0, unroll=4)

    def active(b, row, s):
        return (need[b, row] >> s) & 1

    def row_of(j, q):
        return 2 * (j - 1) + q // WIDE, q % WIDE

    def count(value):
        total = value & 1
        for s in range(1, WIDE):
            total = total + ((value >> s) & 1)
        return total

    def holes(b, row):
        return WIDE - count(need[b, row])

    def tally(b):
        free = holes(b, rows - 2) + holes(b, rows - 1)
        free = lax.fori_loop(1, 2 * shared - 2, lambda row, n: n + holes(b, row), free)
        common = lax.fori_loop(2 * shared - 2, 2 * tail - 2, lambda row, n: n + holes(b, row), jnp.int32(0))
        end = holes(b, 2 * tail - 2)
        free = free + common + end
        start = 2 * first_guest - 2
        used = jnp.int32(0)
        for i in range(2 * GUEST):
            if i == 2 * GUEST - 2:
                early_used = used
            used = used + count(need[b, start + i])
        lend = jnp.minimum(common, jnp.maximum(free - end - used, 0))
        return used, free, lend, early_used

    def list_guests(b):
        nearest = jnp.int32(room)
        chain[room] = nearest
        chain[room + 1] = nearest
        for n in reversed(range(room)):
            nearest = jnp.where(active(b, *row_of(first_guest, n)) > 0, n, nearest)
            chain[n] = nearest
        for k in range(room):
            queue[b, k] = jnp.minimum(nearest, room - 1)
            nearest = chain[nearest + 1]
        queue[b, room] = room - 1

    def fill(j, base, slots, taken):
        for q in slots:
            used = active(0, *row_of(j, q))
            visitor = guests[queue[0, taken]]
            stage[base + q] = jnp.where(used > 0, mine[j, q], visitor)
            taken = jnp.minimum(taken + 1 - used, room)
        return taken

    need_rows(0)
    list_guests(0)
    own(1).wait()
    for i in range(GUEST):
        own_guest(i).wait()
    taken = fill(1, -WIDE, range(WIDE, pair_slots), jnp.int32(0))
    own(pairs).wait()
    across_second.start()
    taken = fill(pairs, host(1), range(pair_slots), taken)

    own(2).wait()
    taken = fill(2, host(2), range(pair_slots), taken)
    across_last.start()

    def prepare(j, taken):
        own(j).wait()
        taken = fill(j, host(j), range(pair_slots), taken)
        across(j - 1).start()
        return taken

    taken = lax.fori_loop(3, shared, prepare, taken)

    deeper = hub & (z < depth - 1)
    further = hub & (z == 0) & (r + 2 < rows_across)

    @pl.when(hub)
    def _():
        pl.semaphore_wait(barrier, 1 + jnp.where(deeper, 1, 0) + jnp.where(further, 1, 0))

    @pl.when(hub & (z > 0))
    def _():
        greet(barrier, {"depth": z - 1})

    @pl.when(hub & (z == 0) & (r > 0))
    def _():
        greet(barrier, {"row": r - 2})

    @pl.when(jnp.logical_not(hub & (z == 0) & (r == 0)))
    def _():
        pl.semaphore_wait(go, 1)

    @pl.when(deeper)
    def _():
        greet(go, {"depth": z + 1})

    @pl.when(further)
    def _():
        greet(go, {"row": r + 2})

    @pl.when(hub)
    def _():
        greet(go, peer)
        greet(go, fellow)
        greet(go, {"row": r + 1, "col": 1 - me})

    fellow_pattern.start()
    for i in range(GUEST):
        fellow_guest(i).start()
    own_flags.wait()
    for side in (0, 1):
        flag_hop(side, 1).start()
        edge(side).start()

    fellow_pattern.wait_recv()
    fellow_bits = pltpu.make_async_copy(fellow_flags, bits.at[1], bits_sem)
    fellow_bits.start()
    own_used, own_free, own_lend, own_early = tally(0)
    excess[0, 0] = jnp.maximum(own_used - own_free, 0)
    excess[1, 0] = jnp.maximum(own_early - own_free, 0)
    spare[0] = own_lend
    fellow_bits.wait()
    need_rows(1)
    list_guests(1)
    fellow_used, fellow_free, _, _ = tally(1)
    for i in range(GUEST):
        fellow_guest(i).wait_recv()

    def prepare_shared(j, carry):
        taken, lent = carry
        own(j).wait()
        base = host(j)
        for q in range(pair_slots):
            used = active(0, *row_of(j, q))
            ours = taken < own_used
            visitor = jnp.where(
                ours, guests[queue[0, jnp.minimum(taken, room)]],
                fellows[queue[1, jnp.minimum(fellow_free + lent, room)]])
            stage[base + q] = jnp.where(used > 0, mine[j, q], visitor)
            taken = taken + 1 - used
            lent = lent + jnp.where(ours, 0, 1 - used)
        across(j - 1).start()
        return taken, lent

    taken, _ = lax.fori_loop(shared, tail, prepare_shared, (taken, jnp.int32(0)))
    own(tail).wait()
    fill(tail, host(tail), range(WIDE), jnp.minimum(taken, room))
    across(tail - 1).start()

    @pl.loop(tail + 1, pairs)
    def _(j):
        own(j).wait()

    def scan(j, base, slots, free):
        for q in reversed(slots):
            free = jnp.where(active(0, *row_of(j, q)) > 0, free, base + q)
            chain[base + q] = free
        return free

    def scan_pair(i, free):
        j = tail - 1 - i
        return scan(j, host(j), range(pair_slots), free)

    free = jnp.int32(hosts)
    chain[hosts] = free
    chain[hosts + 1] = free
    free = scan(tail, host(tail), range(WIDE), free)
    free = lax.fori_loop(0, tail - 2, scan_pair, free)
    free = scan(pairs, host(1), range(pair_slots), free)
    free = scan(1, -WIDE, range(WIDE, pair_slots), free)
    across_half.start()
    across_end.start()
    for k in range(room):
        spot[0, k] = jnp.minimum(free, hosts - 1)
        free = chain[free + 1]

    common = passed.shape[0]

    def scan_fellow(i, carry):
        nearest, above = carry
        j = tail - 1 - i
        for q in reversed(range(pair_slots)):
            hole = 1 - active(1, *row_of(j, q))
            above = above + hole
            lends = (hole > 0) & (fellow_free - above >= fellow_used)
            at = (j - shared) * pair_slots + q
            nearest = jnp.where(lends, at, nearest)
            chain[at] = nearest
        return nearest, above

    nearest = jnp.int32(common)
    chain[common] = nearest
    chain[common + 1] = nearest
    nearest, _ = lax.fori_loop(0, tail - shared, scan_fellow, (nearest, holes(1, 2 * tail - 2)))
    for k in range(room):
        spot[1, k] = jnp.minimum(nearest, common - 1)
        nearest = chain[nearest + 1]
    rank = jnp.int32(0)
    for n in range(room):
        place_own[n] = spot[0, jnp.minimum(rank, room - 1)]
        place_fellow[n] = spot[1, jnp.clip(rank - own_free, 0, room - 1)]
        from_fellow[n] = jnp.where(rank >= own_free, 1, 0)
        rank = rank + active(0, *row_of(first_guest, n))

    def absorb(k):
        fetch = pltpu.make_async_copy(flags.at[k], bits.at[2], bits_sem)
        fetch.start()
        fetch.wait()
        need_rows(2)
        used, free, lend, early_used = tally(2)
        excess[0, k] = jnp.maximum(used - free, 0)
        excess[1, k] = jnp.maximum(early_used - free, 0)
        spare[k] = lend

    def expand(which, i, j):
        lane = lax.broadcasted_iota(jnp.int32, flags.shape[1:], 1)
        for p in range(2):
            picked = jnp.where(lane == i + p, flags[which], 0).astype(jnp.float32)
            spread = jnp.broadcast_to(jnp.sum(picked, axis=1, keepdims=True), (WIDE, block))
            for s in range(WIDE):
                masks[j, p:p + 1, (p + s) * block:(p + s + 1) * block] = spread[s:s + 1]
            empty = slice(0, block) if p else slice(WIDE * block, SLOTS * block)
            masks[j, p:p + 1, empty] = jnp.zeros((1, block), jnp.float32)

    def convert(j, other, halves=(0, 1), ours=True):
        for p in halves:
            for s in range(WIDE):
                slot = p + s
                lanes = slice(slot * block, (slot + 1) * block)
                factor = masks[j, p:p + 1, lanes]
                pieces = [(me, mine[j, p * WIDE + s])] if ours else []
                if other is not None:
                    pieces.append((1 - me, other(p * WIDE + s)))
                for c, value in pieces:
                    a, b = split(value * factor)
                    at = pl.ds(pl.multiple_of(p * block + c * h, h), h)
                    high[j, at, lanes] = a
                    low[j, at, lanes] = b
            if not ours:
                continue
            empty = slice(0, block) if p else slice(WIDE * block, SLOTS * block)
            nothing = jnp.zeros((block, block), jnp.bfloat16)
            high[j, p * block:(p + 1) * block, empty] = nothing
            low[j, p * block:(p + 1) * block, empty] = nothing

    def arrived(j):
        return lambda q: hosted[host(j) + q]

    def direct(i):
        return lambda q: theirs[i, q]

    def visiting(j):
        def block_at(q):
            n = (j - first_guest) * pair_slots + q
            return jnp.where(from_fellow[n] > 0, passed[place_fellow[n]], hosted[place_own[n]])

        return block_at

    product, own_rows, compute = products(block, h, me, masks, high, low, early)

    @pl.loop(1, pairs + 1)
    def _(j):
        expand(0, 2 * (j - 1), j)

    for side in (0, 1):
        flag_hop(side, 1).wait_recv()
    for side in (0, 1):
        if reach[side] > 1:
            flag_hop(side, 2).start()
    expand(1, 2 * (pairs - 1), 0)
    expand(ring - 1, 0, last)

    across_first.wait_recv()
    relay_first.start()
    across_second.wait_recv()
    relay_second.start()
    convert(1, lambda q: theirs[1, q] if q < WIDE else hosted[q - WIDE])
    across_last.wait_recv()
    relay_ahead.start()
    convert(pairs, arrived(1))
    absorb(1)
    absorb(ring - 1)
    edge(0).wait_recv()
    relay_ahead.wait_recv()
    convert(0, direct(0))
    edge(1).wait_recv()
    relay_first.wait_recv()
    relay_second.wait_recv()
    convert(last, direct(2))

    def local_rows(j):
        parts = []
        for p in range(2):
            blocks = [mine[j, p * WIDE + s] for s in range(WIDE)]
            empty = [jnp.zeros((h, block), jnp.float32)]
            row = jnp.concatenate(empty + blocks if p else blocks + empty, axis=1)
            parts.append(row * masks[j, p:p + 1, :])
        return split(jnp.concatenate(parts, axis=0))

    def converted_rows(j):
        return own_rows(high, j), own_rows(low, j)

    for j in range(tail, pairs):
        convert(j, None)
    ahead[0] = product(pairs - 1, *local_rows(pairs - 1), (2,))
    ahead[1] = product(pairs, *converted_rows(pairs), (1, 2))

    turns = tail - 2
    each = -(-(reach[0] - 1) // turns)

    def pass_on(side, k):
        @pl.when(k <= reach[side])
        def _():
            flag_hop(side, k).wait_recv()

        @pl.when(k + 1 <= reach[side])
        def _():
            flag_hop(side, k + 1).start()

        @pl.when(k <= reach[side])
        def _():
            absorb(k if side == 0 else ring - k)

    @pl.loop(2, tail)
    def _(j):
        across(j).wait_recv()

        @pl.when(j >= shared)
        def _():
            hand_over(j).start()

        convert(j, arrived(j))
        compute(j - 1, j - 2)
        for u in range(each):
            for side in (0, 1):
                pass_on(side, (j - 2) * each + u + 2)

    level = jnp.int32(0)
    for k in range(ring):
        there = lax.rem(place - k + ring, ring)
        band = there // depth
        partner = there + (1 - 2 * lax.rem(band, 2)) * depth
        lent = spare[lax.rem(place - partner + ring, ring)]
        level = jnp.maximum(level, jnp.where(excess[0, k] > lent, 1, 0))
        level = jnp.maximum(level, jnp.where(excess[1, k] > lent, 2, 0))
    over[0] = level

    begun[0] = product(tail - 1, *converted_rows(tail - 1), BEFORE[0])
    begun[1] = product(tail, *local_rows(tail), (0,))

    for j in range(shared, tail):
        hand_over(j).wait_recv()
    across_half.wait_recv()
    for j in range(first_guest, pairs - 1):
        convert(j, visiting(j), ours=False)
    convert(tail, arrived(tail), (0,), False)
    begun[1] = product(tail, *local_rows(tail), (2,), begun[1])
    convert(pairs - 1, visiting(pairs - 1), ours=False)
    for j in range(first_guest + 1, pairs - 1):
        compute(j, j - LATE - 1)
    begun[2] = product(first_guest, *converted_rows(first_guest), BEFORE[2])
    compute(pairs - 1, pairs - LATE - 2, (0, 1), ahead[0])
    compute(pairs, pairs - LATE - 1, (0,), ahead[1])

    fellow_pattern.wait_send()
    for i in range(GUEST):
        fellow_guest(i).wait_send()
    for j in range(shared, tail):
        hand_over(j).wait_send()
    for side in (0, 1):
        edge(side).wait_send()

        @pl.loop(1, reach[side] + 1)
        def _(k):
            flag_hop(side, k).wait_send()

    relay_ahead.wait_send()
    relay_first.wait_send()
    relay_second.wait_send()

    across_end.wait_recv()
    convert(tail, direct(3), (1,), False)
    across_first.wait_send()
    across_second.wait_send()
    across_last.wait_send()
    across_half.wait_send()
    across_end.wait_send()

    @pl.loop(2, tail)
    def _(j):
        across(j).wait_send()


class Patched:
    def __init__(self, ref, fixed, first):
        self.ref, self.fixed, self.first = ref, fixed, first

    def __getitem__(self, at):
        j = at[0] - self.first
        if 0 <= j < self.fixed.shape[0]:
            return self.fixed[(j,) + tuple(at[1:])]
        return self.ref[at]


def top_up_kernel(dens, got, send_sem, recv_sem):
    count = got.shape[0]
    first = dens.shape[0] - 1 - count
    peer = {"col": 1 - lax.axis_index("col")}
    barrier = pltpu.get_barrier_semaphore()
    pl.semaphore_signal(barrier, inc=1, device_id=peer, device_id_type=MESH)
    pl.semaphore_wait(barrier, 1)

    def across(i):
        return pltpu.make_async_remote_copy(
            dens.at[first + i], got.at[i], send_sem.at[i], recv_sem.at[i],
            device_id=peer, device_id_type=MESH)

    for i in range(count):
        across(i).start()
    for i in range(count):
        across(i).wait()


def finish_again(first_late, masks, high, low, early, begun, got, out,
                 late, fixed_high, fixed_low, early_sem, late_sem):
    h, block = early.shape[3], early.shape[4]
    me = lax.axis_index("col")
    before = first_late - 1
    count = late.shape[0]
    first = pltpu.make_async_copy(early.at[pl.ds(0, before)], out.at[pl.ds(0, before)], early_sem)
    first.start()
    fixed = got.shape[0]
    first_guest = first_late + count - 1 - fixed
    fixed_high[...] = high[pl.ds(first_guest, fixed)]
    fixed_low[...] = low[pl.ds(first_guest, fixed)]
    for i in range(fixed):
        for q in range(2 * WIDE):
            p, s = divmod(q, WIDE)
            lanes = slice((p + s) * block, (p + s + 1) * block)
            a, b = split(got[i, q] * masks[first_guest + i, p:p + 1, lanes])
            at = pl.ds(pl.multiple_of(p * block + (1 - me) * h, h), h)
            fixed_high[i, at, lanes] = a
            fixed_low[i, at, lanes] = b
    _, _, compute = products(block, h, me, masks, Patched(high, fixed_high, first_guest),
                             Patched(low, fixed_low, first_guest), late)

    def result(i):
        return pltpu.make_async_copy(late.at[i], out.at[before + i], late_sem.at[i])

    for i in range(count):
        if fixed < GUEST and i < LATE:
            compute(first_late + i, i, AFTER[i], begun[i])
        else:
            compute(first_late + i, i)
        result(i).start()
    first.wait()

    @pl.loop(0, count)
    def _(i):
        result(i).wait()


DMA = pltpu.SemaphoreType.DMA
IN_VMEM = pl.BlockSpec(memory_space=pltpu.VMEM)


def results(pairs, wide, h, block):
    width = SLOTS * block
    return [
        pltpu.VMEM((pairs + 2, 8, width), jnp.float32),
        pltpu.VMEM((pairs + 2, 2 * block, width), jnp.bfloat16),
        pltpu.VMEM((pairs + 2, 2 * block, width), jnp.bfloat16),
        pltpu.VMEM((pairs - LATE, 2, wide, h, block), jnp.float32),
        pltpu.VMEM((LATE, 2 * h, width), jnp.float32),
    ]


def in_hbm(*arrays):
    return (pltpu.with_memory_space_constraint(x, pltpu.HBM) for x in arrays)


def finished(first_late, held, pairs, wide, h, block):
    return pl.pallas_call(
        functools.partial(finish, first_late),
        out_shape=pltpu.HBM((pairs, 2, wide, h, block), jnp.float32),
        in_specs=[IN_VMEM] * 5,
        out_specs=pl.BlockSpec(memory_space=pltpu.HBM),
        scratch_shapes=[
            pltpu.VMEM((LATE, 2, wide, h, block), jnp.float32),
            DMA((2,)),
            DMA((LATE,)),
        ],
        compiler_params=pltpu.CompilerParams(vmem_limit_bytes=16 << 20),
    )(*held)


def dense(cols, ring, density, pattern):
    rows, wide, h, block = density.shape
    pairs = rows // 2
    paired = density.reshape(pairs, 2, wide, h, block)
    held = pl.pallas_call(
        functools.partial(dense_kernel, cols, ring),
        out_shape=results(pairs, wide, h, block),
        in_specs=[pl.BlockSpec(memory_space=pltpu.HBM)] * 2,
        out_specs=[IN_VMEM] * 5,
        scratch_shapes=[
            pltpu.VMEM((cols, pairs + 2, 2, wide, h, block), jnp.float32),
            pltpu.VMEM((3, wide, rows), jnp.int32),
            DMA((pairs,)),
            DMA,
            DMA((cols - 1, pairs)),
            DMA((cols - 1, pairs)),
            DMA((2,)),
            DMA((2,)),
            DMA((2, cols - 1)),
            DMA((2, cols - 1)),
            DMA((2,)),
            DMA((2,)),
            pltpu.SemaphoreType.REGULAR,
            pltpu.SemaphoreType.REGULAR,
            pltpu.SemaphoreType.REGULAR,
        ],
        compiler_params=pltpu.CompilerParams(
            collective_id=0, has_side_effects=True, vmem_limit_bytes=42 << 20),
    )(*in_hbm(paired, pattern.T))
    out = finished(pairs - LATE + 1, held, pairs, wide, h, block)
    return out.reshape(density.shape)


def sparse(ring, density, pattern):
    rows, wide, h, block = density.shape
    pairs = rows // 2
    paired = density.reshape(pairs, 2 * wide, h, block)
    tail = pairs - GUEST - 1
    hosts = tail * 2 * wide
    room = GUEST * 2 * wide
    common = SHARED * 2 * wide
    scalars = pltpu.SMEM
    *held, over = pl.pallas_call(
        functools.partial(sparse_kernel, ring, lax.axis_size("row")),
        out_shape=results(pairs, wide, h, block) + [pltpu.SMEM((1,), jnp.int32)],
        in_specs=[pl.BlockSpec(memory_space=pltpu.HBM)] * 2,
        out_specs=[IN_VMEM] * 5 + [pl.BlockSpec(memory_space=pltpu.SMEM)],
        scratch_shapes=[
            pltpu.VMEM((pairs + 2, 2 * wide, h, block), jnp.float32),
            pltpu.VMEM((4, 2 * wide, h, block), jnp.float32),
            pltpu.VMEM((hosts, h, block), jnp.float32),
            pltpu.VMEM((hosts, h, block), jnp.float32),
            pltpu.VMEM((common, h, block), jnp.float32),
            pltpu.VMEM((room, h, block), jnp.float32),
            pltpu.VMEM((room, h, block), jnp.float32),
            pltpu.VMEM((ring, wide, rows), jnp.int32),
            pltpu.VMEM((wide, rows), jnp.int32),
            scalars((3, wide, rows), jnp.int32),
            scalars((rows,), jnp.int32),
            scalars((3, rows), jnp.int32),
            scalars((hosts + 2,), jnp.int32),
            scalars((2, room + 1), jnp.int32),
            scalars((2, room), jnp.int32),
            scalars((room,), jnp.int32),
            scalars((room,), jnp.int32),
            scalars((room,), jnp.int32),
            scalars((2, ring), jnp.int32),
            scalars((ring,), jnp.int32),
            pltpu.VMEM((2, 2 * h, SLOTS * block), jnp.float32),
            DMA((pairs,)),
            DMA((GUEST,)),
            DMA,
            DMA,
            DMA((tail + 3,)),
            DMA((tail + 3,)),
            DMA((2,)),
            DMA((2,)),
            DMA((3,)),
            DMA((3,)),
            DMA((2, ring // 2)),
            DMA((2, ring // 2)),
            DMA((GUEST + 1,)),
            DMA((GUEST + 1,)),
            DMA((SHARED,)),
            DMA((SHARED,)),
            pltpu.SemaphoreType.REGULAR,
            pltpu.SemaphoreType.REGULAR,
        ],
        compiler_params=pltpu.CompilerParams(
            collective_id=1, has_side_effects=True, vmem_limit_bytes=40 << 20),
    )(*in_hbm(paired, pattern.T))

    def done(paired, *held):
        return finished(tail - 1, held, pairs, wide, h, block)

    ids = {1: 2, GUEST: 0}

    def again(fixed, paired, *held):
        got = pl.pallas_call(
            top_up_kernel,
            out_shape=pltpu.VMEM((fixed, 2 * wide, h, block), jnp.float32),
            in_specs=[pl.BlockSpec(memory_space=pltpu.HBM)],
            out_specs=IN_VMEM,
            scratch_shapes=[DMA((fixed,)), DMA((fixed,))],
            compiler_params=pltpu.CompilerParams(
                collective_id=ids[fixed], has_side_effects=True, vmem_limit_bytes=8 << 20),
        )(*in_hbm(paired))
        count = pairs - tail + 2
        return pl.pallas_call(
            functools.partial(finish_again, tail - 1),
            out_shape=pltpu.HBM((pairs, 2, wide, h, block), jnp.float32),
            in_specs=[IN_VMEM] * 6,
            out_specs=pl.BlockSpec(memory_space=pltpu.HBM),
            scratch_shapes=[
                pltpu.VMEM((count, 2, wide, h, block), jnp.float32),
                pltpu.VMEM((fixed, 2 * block, SLOTS * block), jnp.bfloat16),
                pltpu.VMEM((fixed, 2 * block, SLOTS * block), jnp.bfloat16),
                DMA,
                DMA((count,)),
            ],
            compiler_params=pltpu.CompilerParams(vmem_limit_bytes=20 << 20),
        )(*held, got)

    branches = [done, functools.partial(again, 1), functools.partial(again, GUEST)]
    return lax.switch(over[0], branches, paired, *held).reshape(density.shape)


def shards(cols, ring, density, pattern):
    if cols == 2 and lax.axis_size("row") % 2 == 0 and density.shape[0] >= 32:
        return sparse(ring, density, pattern)
    return dense(cols, ring, density, pattern)


def solution(mesh):
    cols = mesh.shape["col"]
    ring = mesh.shape["row"] * mesh.shape["depth"]
    in_specs = (P(RING, None, "col", None), P(RING, None))
    out_specs = P(RING, None, "col", None)
    body = functools.partial(shards, cols, ring)
    return jax.shard_map(body, mesh=mesh, in_specs=in_specs, out_specs=out_specs, check_vma=False)
```
